32 devices in a mesh: groups: 2 (over x), tok: 16 (over z, y, core).
Axes of the slice: x: 2, y: 2, z: 4, core: 2. Of those that a mesh axis runs over, the one named last changes fastest.
Arguments:
- single: bfloat16 [512, 8, 768], P(('groups', 'tok')), parts along dimension 0, may hold values from -6 to 6
- pair: bfloat16 [512, 256, 128], P(('groups', 'tok')), parts along dimension 0, may hold values from -400 to 400, as said below
- chain: int32 [512], P(('groups', 'tok')), parts along dimension 0, may hold values from 0 to 7, never falling along the last dimension, each value on 1 to 64 neighbouring positions
- residue: int32 [512], P(('groups', 'tok')), parts along dimension 0, may hold values from 0 to 510, as said below
- valid: int32 [512], P(('groups', 'tok')), parts along dimension 0, may hold values 0 or 1
- w_query: bfloat16 [768, 768], replicated, may hold values from -0.21875 to 0.21875
- w_key: bfloat16 [768, 768], replicated, may hold values from -0.21875 to 0.21875
- w_value: bfloat16 [768, 768], replicated, may hold values from -0.21875 to 0.21875
- w_gate: bfloat16 [768, 768], replicated, may hold values from -0.21875 to 0.21875
- w_out: bfloat16 [768, 768], replicated, may hold values from -0.21875 to 0.21875
- w_pair: bfloat16 [128, 16], replicated, may hold values from -1.1953125 to 1.1953125
- rel_table: float32 [66, 16], replicated, may hold values from -6 to 6
Outputs:
- updated: bfloat16 [512, 8, 768], P(('groups', 'tok')), parts along dimension 0
The draws below stay inside these ranges and needn't reach their ends.
There are 2 independent parts, one for each index of `groups`. The reference program is written for one: setup_inputs(seed, part) draws one part's arguments, and reference() takes and returns one part's arrays. A program takes and returns all parts, laid end to end along the dimension named above; an argument that names none is the same for every part. Nothing has to cross between parts.
Inputs may be any that keep to these rules, and one draw needn't show every extreme that they name: `pair`: pair entries are of order one, except possibly in a few query rows where two entries have many times the usual size. `residue`: starts at 0 and rises from each token to the next, by 1 or 2 except into the last token, which holds the largest value.
All inputs are finite; a program needn't handle non-finite values. No bound on the sum of `valid` on one device may be relied on, other than what follows from the above.
Results may differ from the reference program's by a relative error of at most 0.0045.
Values may be sent and summed in bfloat16 or wider, within the bound.
No kernel may reach another device: no remote copies, remote signals or barrier semaphores. Data moves between devices by JAX's collectives and lax.ppermute only.
A program may use at most 128 MiB of HBM per device.

```python
import math
import jax
import jax.numpy as jnp
import numpy as np
from jax import lax

D = 768
HEADS = 16
PAIR_C = 128
SAMPLES = 8
CHAINS = 8
RELBINS = 66
TOKENS = 256


def draw_pair(key, part):
    key_base = jax.random.fold_in(key, 0)
    base = jax.random.normal(key_base, (TOKENS, TOKENS, PAIR_C), jnp.float32)
    return jnp.clip(base, -400.0, 400.0).astype(jnp.bfloat16)


def draw_residue(key, part):
    steps_up = jax.random.randint(key, (TOKENS,), 1, 3)
    rising = (jnp.cumsum(steps_up) - steps_up[0]).astype(jnp.int32)
    positions = jnp.arange(TOKENS, dtype=jnp.int32)
    return jnp.where(positions == TOKENS - 1, 2 * TOKENS - 2, rising).astype(jnp.int32)


def with_ends(values, stream_key, low, top_value):
    longest = values.shape.index(max(values.shape))
    spots = []
    for shift in (0, 1):
        where = [jax.random.randint(jax.random.fold_in(stream_key, axis), (), 0, length) for axis, length in enumerate(values.shape)]
        where[longest] = (where[longest] + shift) % values.shape[longest]
        spots.append(tuple(where))
    return values.at[spots[0]].set(low).at[spots[1]].set(top_value)


def levels(stream_key, shape, cuts, low, largest):
    level = 1.0
    for dim, blocks in cuts:
        steps = jax.random.uniform(jax.random.fold_in(jax.random.fold_in(stream_key, 6), dim), (blocks,), jnp.float32, low / len(cuts), largest / len(cuts))
        level = level * jnp.repeat(jnp.exp(steps), shape[dim] // blocks).reshape((-1,) + (1,) * (len(shape) - 1 - dim))
    return level


def profile(amount, total, limit, slope):
    weights = [(1 << 20) // math.isqrt(rank ** slope) + 1 for rank in range(2, amount + 1)]
    surplus, given = total - limit - (amount - 1), [1] * (amount - 1)
    while surplus > 0:
        movable = [i for i in range(amount - 1) if given[i] < limit]
        whole, left = sum([weights[i] for i in movable]), surplus
        for i in movable:
            more = min(limit - given[i], max(1, left * weights[i] // whole), surplus)
            given[i] = given[i] + more
            surplus = surplus - more
    return np.array([limit] + given)


def ragged(stream_key, amount, total, bound, lean):
    if amount == 2:
        one = jax.random.randint(stream_key, (), max(1, total - bound), min(bound, total - 1) + 1)
        return jnp.stack([one, total - one])
    sizes = jnp.asarray(profile(amount, total, bound, lean), jnp.int32)
    pairs = (amount - 1) // 2
    donor, receiver = sizes[1:1 + 2 * pairs:2], sizes[2:2 + 2 * pairs:2]
    margin = jnp.minimum(donor - 1, bound - receiver)
    moved = jax.random.randint(jax.random.fold_in(stream_key, 1), (pairs,), 0, 1 << 20) % (margin + 1)
    sizes = sizes.at[1:1 + 2 * pairs:2].set(donor - moved).at[2:2 + 2 * pairs:2].set(receiver + moved)
    return sizes[jax.random.permutation(jax.random.fold_in(stream_key, 2), amount)]


def noise(own_key, shape, scale, reach, shards=(), kind=jnp.bfloat16):
    drawn = scale * jax.random.normal(own_key, shape, jnp.float32)
    if shards:
        drawn = drawn * levels(own_key, shape, shards, -0.22, 0.18)
    return jnp.clip(drawn, -reach, reach).astype(kind)


def setup_inputs(seed: int = 0, part: int = 0) -> dict:
    key_of = jax.random.split(jax.random.key(seed), 13)
    part_splits = jax.random.split(jax.random.fold_in(key_of[12], part), 13)
    single = noise(part_splits[0], (TOKENS, SAMPLES, D), 1.0, 6.0, ((0, 16),))
    pair = draw_pair(jax.random.fold_in(jax.random.fold_in(key_of[12], part), 71), part)
    chain = jnp.searchsorted(jnp.cumsum(ragged(part_splits[2], CHAINS, TOKENS, TOKENS // 4, 0)), jnp.arange(TOKENS), side="right").astype(jnp.int32)
    residue = draw_residue(jax.random.fold_in(jax.random.fold_in(key_of[12], part), 71), part)
    valid = with_ends((jax.random.randint(part_splits[4], (TOKENS,), 0, 4) < 3).astype(jnp.int32), jax.random.fold_in(part_splits[4], 1), 0, 1)
    w_query = noise(key_of[5], (D, D), D ** -0.5, 0.21875)
    w_key = noise(key_of[6], (D, D), D ** -0.5, 0.21875)
    w_value = noise(key_of[7], (D, D), D ** -0.5, 0.21875)
    w_gate = noise(key_of[8], (D, D), D ** -0.5, 0.21875)
    w_out = noise(key_of[9], (D, D), D ** -0.5, 0.21875)
    w_pair = noise(key_of[10], (PAIR_C, HEADS), 0.2, 1.1953125)
    rel_table = noise(key_of[11], (RELBINS, HEADS), 1.0, 6.0, (), jnp.float32)
    return {"single": single, "pair": pair, "chain": chain, "residue": residue, "valid": valid, "w_query": w_query, "w_key": w_key, "w_value": w_value, "w_gate": w_gate, "w_out": w_out, "w_pair": w_pair, "rel_table": rel_table}


NORM_EPS = 1e-05
MASK_PENALTY = 10000.0

def layer_normed(values_in):
    mean_val = lax.optimization_barrier(jnp.mean(values_in, axis=-1, keepdims=True))
    centred = values_in - mean_val
    spread = lax.optimization_barrier(jnp.mean(centred * centred, axis=-1, keepdims=True))
    return centred * lax.rsqrt(spread + NORM_EPS)

def reference(single, pair, chain, residue, valid, w_query, w_key, w_value, w_gate, w_out, w_pair, rel_table):
    token_count, sample_count, width = single.shape
    head_count = w_pair.shape[1]
    head_size = width // head_count
    channels = pair.shape[2]
    rel_bins = rel_table.shape[0]
    rel_reach = (rel_bins - 2) // 2
    normed = layer_normed(single.astype(jnp.float32)).astype(jnp.bfloat16)
    flat_rows = normed.reshape(token_count * sample_count, width)

    def project(weight):
        return jnp.dot(flat_rows, weight, preferred_element_type=jnp.float32)
    query_proj = lax.optimization_barrier(project(w_query).astype(jnp.bfloat16)).reshape(token_count, sample_count, head_count, head_size)
    key_proj = lax.optimization_barrier(project(w_key).astype(jnp.bfloat16)).reshape(token_count, sample_count, head_count, head_size)
    value_proj = lax.optimization_barrier(project(w_value).astype(jnp.bfloat16)).reshape(token_count, sample_count, head_count, head_size)
    gate_proj = jax.nn.sigmoid(project(w_gate)).reshape(token_count, sample_count, head_count, head_size)
    key_float = key_proj.astype(jnp.float32)
    value_float = value_proj.astype(jnp.float32)
    block_rows = math.gcd(token_count, 64)
    scale_factor = 1.0 / math.sqrt(head_size)
    bucket_ids = jnp.arange(rel_bins, dtype=jnp.int32)
    mask_bias = (valid.astype(jnp.float32) - 1.0) * MASK_PENALTY

    def one_block(block_index):
        start_row = (block_index * block_rows).astype(jnp.int32)
        pair_rows = lax.dynamic_slice_in_dim(pair, start_row, block_rows, 0)
        pair_bias = jnp.dot(pair_rows.reshape(block_rows * token_count, channels), w_pair, preferred_element_type=jnp.float32).reshape(block_rows, token_count, head_count)
        chain_rows = lax.dynamic_slice_in_dim(chain, start_row, block_rows, 0)
        residue_rows = lax.dynamic_slice_in_dim(residue, start_row, block_rows, 0)
        same_chain = chain_rows[:, None] == chain[None, :]
        offset = jnp.clip(residue_rows[:, None] - residue[None, :], -rel_reach, rel_reach) + rel_reach
        bucket = jnp.where(same_chain, offset, rel_bins - 1)
        one_hot = (bucket[:, :, None] == bucket_ids).astype(jnp.float32)
        rel_bias = jnp.einsum('qkb,bh->qkh', one_hot, rel_table, precision=lax.Precision.HIGHEST)
        total_bias = jnp.transpose(pair_bias + rel_bias + mask_bias[None, :, None], (2, 0, 1))
        query_rows = lax.dynamic_slice_in_dim(query_proj, start_row, block_rows, 0).astype(jnp.float32)
        scores = jnp.einsum('qshd,kshd->shqk', query_rows, key_float) * scale_factor + total_bias[None]
        top_score = lax.optimization_barrier(jnp.max(scores, axis=-1, keepdims=True))
        probs = jnp.exp(scores - top_score)
        mass = lax.optimization_barrier(jnp.sum(probs, axis=-1))
        probs_low = lax.optimization_barrier(probs.astype(jnp.bfloat16)).astype(jnp.float32)
        weighted = jnp.einsum('shqk,kshd->shqd', probs_low, value_float)
        attended = jnp.transpose(weighted / mass[..., None], (2, 0, 1, 3))
        gate_rows = lax.dynamic_slice_in_dim(gate_proj, start_row, block_rows, 0)
        gated = (gate_rows * attended).reshape(block_rows * sample_count, width).astype(jnp.bfloat16)
        out_rows = jnp.dot(gated, w_out, preferred_element_type=jnp.float32).reshape(block_rows, sample_count, width)
        single_rows = lax.dynamic_slice_in_dim(single, start_row, block_rows, 0)
        return (single_rows.astype(jnp.float32) + out_rows).astype(jnp.bfloat16)
    blocks = lax.map(one_block, jnp.arange(token_count // block_rows, dtype=jnp.int32))
    return blocks.reshape(token_count, sample_count, width)
```

```python
import functools
import math

import jax
import jax.numpy as jnp
from jax import lax
from jax.experimental import pallas as pl
from jax.experimental.pallas import tpu as pltpu
from jax.sharding import PartitionSpec as P

NORM_EPS = 1e-05
MASK_PENALTY = 10000.0
F32 = jnp.float32
BF16 = jnp.bfloat16
CORES = 2
TILE = 256


def normed_rows(block):
    tokens, samples, width = block.shape
    values = block.astype(F32).reshape(tokens * samples, width)
    centred = values - jnp.mean(values, axis=-1, keepdims=True)
    spread = jnp.mean(centred * centred, axis=-1, keepdims=True)
    return (centred * lax.rsqrt(spread + NORM_EPS)).astype(BF16)


def sample_major(tokens, samples):
    rows = tokens * samples
    to = lax.broadcasted_iota(jnp.int32, (rows, rows), 0)
    frm = lax.broadcasted_iota(jnp.int32, (rows, rows), 1)
    want = (to % tokens) * samples + to // tokens
    return (want == frm).astype(F32).astype(BF16)


def token_major(tokens, samples):
    rows = tokens * samples
    to = lax.broadcasted_iota(jnp.int32, (rows, rows), 0)
    frm = lax.broadcasted_iota(jnp.int32, (rows, rows), 1)
    want = (to % samples) * tokens + to // samples
    return (want == frm).astype(F32).astype(BF16)


def matmul(a, b):
    return jnp.dot(a, b, preferred_element_type=F32)


def query_body(single_ref, wq_ref, wg_ref, q_ref, gate_ref):
    tokens, samples, _ = single_ref.shape
    rows = normed_rows(single_ref[...])
    rows = matmul(sample_major(tokens, samples), rows).astype(BF16)
    q_ref[...] = matmul(rows, wq_ref[...]).astype(BF16)
    gate_ref[...] = jax.nn.sigmoid(matmul(rows, wg_ref[...]))


def keys_values(blocks, wk, wv):
    tokens, samples, width = blocks[0].shape
    perm = sample_major(tokens, samples)
    parts = [
        matmul(perm, normed_rows(b)).astype(BF16).reshape(samples, tokens, width) for b in blocks
    ]
    rows = jnp.concatenate(parts, axis=1) if len(parts) > 1 else parts[0]
    shape = rows.shape
    rows = rows.reshape(shape[0] * shape[1], width)
    return (
        matmul(rows, wk).astype(BF16).reshape(shape),
        matmul(rows, wv).astype(BF16).reshape(shape),
    )


def kv_body(*refs):
    wk_ref, wv_ref, k_ref, v_ref = refs[-4:]
    keys, values = keys_values([r[...] for r in refs[:-4]], wk_ref[...], wv_ref[...])
    k_ref[...] = keys
    v_ref[...] = values


def bias_body(blk_ref, chain_ref, res_ref, pair_ref, wp_ref, tab_ref, meta_ref, out_ref):
    heads, queries, total = out_ref.shape
    channels = pair_ref.shape[2]
    bins = tab_ref.shape[0]
    reach = (bins - 2) // 2
    tokens = total // blk_ref.shape[0]
    weights = jnp.transpose(wp_ref[...].astype(F32)).astype(BF16)
    table = jnp.transpose(tab_ref[...])
    high = table.astype(BF16)
    rest = table - high.astype(F32)
    mid = rest.astype(BF16)
    low = (rest - mid.astype(F32)).astype(BF16)
    chain_keys = meta_ref[0:1, :]
    res_keys = meta_ref[1:2, :]
    mask = (meta_ref[2:3, :] - 1.0) * MASK_PENALTY
    bin_ids = lax.broadcasted_iota(jnp.int32, (bins, total), 0).astype(F32)
    for i in range(queries):
        rows = jnp.concatenate(
            [
                pair_ref[i, pl.ds(pl.multiple_of(blk_ref[b] * tokens, tokens), tokens), :]
                for b in range(blk_ref.shape[0])
            ],
            axis=0,
        )
        acc = lax.dot_general(weights, rows, (((1,), (1,)), ((), ())), preferred_element_type=F32)
        chain_q = chain_ref[i].astype(F32)
        res_q = res_ref[i].astype(F32)
        offset = jnp.clip(res_q - res_keys, -reach, reach) + reach
        bucket = jnp.where(chain_keys == chain_q, offset, float(bins - 1))
        hot = (bin_ids == bucket).astype(F32).astype(BF16)
        rel = (matmul(low, hot) + matmul(mid, hot)) + matmul(high, hot)
        out_ref[:, i, :] = acc + rel + mask


def attend_body(n_kv, heads, scale, *refs):
    kv_refs = refs[: 2 * n_kv]
    last = refs[2 * n_kv : 2 * n_kv + 4]
    q_ref, gate_ref, bias_ref, single_ref, wk_ref, wv_ref, wo_ref, out_ref = refs[2 * n_kv + 4 :]
    tokens, samples, width = single_ref.shape
    hs = width // heads
    blocks = [
        jnp.concatenate([last[0][...], last[1][...]], axis=0),
        jnp.concatenate([last[2][...], last[3][...]], axis=0),
    ]
    k_last, v_last = keys_values(blocks, wk_ref[...], wv_ref[...])
    total = bias_ref.shape[2]
    bias = bias_ref[...].reshape(heads * tokens, total)
    lane_head = lax.broadcasted_iota(jnp.int32, (tokens, width), 1) // hs
    spans = []
    for t in range(width // TILE):
        spans.append(((t * TILE) // hs, ((t + 1) * TILE - 1) // hs))
    gated = []
    for s in range(samples):
        keys = jnp.concatenate([r[s] for r in kv_refs[:n_kv]] + [k_last[s]], axis=0)
        values = jnp.concatenate([r[s] for r in kv_refs[n_kv:]] + [v_last[s]], axis=0)
        q = q_ref[pl.ds(s * tokens, tokens), :].astype(F32)
        per_head = [None] * heads
        for t, (h0, h1) in enumerate(spans):
            cut = slice(t * TILE, (t + 1) * TILE)
            qt = jnp.concatenate(
                [
                    jnp.where(lane_head[:, cut] == h, q[:, cut], 0.0).astype(BF16)
                    for h in range(h0, h1 + 1)
                ],
                axis=0,
            )
            st = lax.dot_general(
                qt, keys[:, cut], (((1,), (1,)), ((), ())), preferred_element_type=F32
            )
            for h in range(h0, h1 + 1):
                part = st[(h - h0) * tokens : (h - h0 + 1) * tokens]
                per_head[h] = part if per_head[h] is None else per_head[h] + part
        scores = jnp.concatenate(per_head, axis=0) * scale + bias
        top = jnp.max(scores, axis=-1, keepdims=True)
        probs = jnp.exp(scores - top)
        inv = 1.0 / jnp.sum(probs, axis=-1, keepdims=True)
        probs = probs.astype(BF16)
        attended = []
        for t, (h0, h1) in enumerate(spans):
            cut = slice(t * TILE, (t + 1) * TILE)
            ot = matmul(probs[h0 * tokens : (h1 + 1) * tokens], values[:, cut])
            ot = ot * inv[h0 * tokens : (h1 + 1) * tokens]
            got = ot[:tokens]
            for h in range(h0 + 1, h1 + 1):
                got = jnp.where(
                    lane_head[:, cut] == h, ot[(h - h0) * tokens : (h - h0 + 1) * tokens], got
                )
            attended.append(got)
        attended = jnp.concatenate(attended, axis=1)
        gated.append((gate_ref[pl.ds(s * tokens, tokens), :] * attended).astype(BF16))
    gated = jnp.concatenate(gated, axis=0)
    gated = matmul(token_major(tokens, samples), gated).astype(BF16)
    out = matmul(gated, wo_ref[...]).reshape(tokens, samples, width)
    out_ref[...] = (single_ref[...].astype(F32) + out).astype(BF16)


def call(body, out_shape, args, in_specs=None, flops=0, moved=0, name=None, limit=40 << 20):
    return pl.pallas_call(
        body,
        out_shape=out_shape,
        in_specs=in_specs or [pl.BlockSpec(memory_space=pltpu.VMEM)] * len(args),
        out_specs=jax.tree.map(lambda _: pl.BlockSpec(memory_space=pltpu.VMEM), out_shape),
        compiler_params=pltpu.CompilerParams(vmem_limit_bytes=limit),
        cost_estimate=pl.CostEstimate(flops=flops, bytes_accessed=moved, transcendentals=0),
        name=name,
    )(*args)


def shards(
    single, pair, chain, residue, valid, w_query, w_key, w_value, w_gate, w_out, w_pair, rel_table
):
    tokens, samples, width = single.shape
    heads = w_pair.shape[1]
    total = pair.shape[1]
    devices = lax.axis_size("tok")
    chips = devices // CORES
    half = chips // 2
    me = lax.axis_index("tok")
    core = me % CORES
    chip = me // CORES
    order = list(range(0, chips, 2)) + list(range(1, chips, 2))[::-1]
    place = jnp.where(chip % 2 == 0, chip // 2, chips - 1 - chip // 2)

    def ring(value, step):
        pairs = [
            (order[i] * CORES + c, order[(i + step) % chips] * CORES + c)
            for i in range(chips)
            for c in range(CORES)
        ]
        return lax.ppermute(value, "tok", pairs)

    def flip(value, bit):
        return lax.ppermute(value, "tok", [(d, d ^ bit) for d in range(devices)])

    steps = [(0, 0), (0, 1)]
    for k in range(1, half):
        steps += [(-k, 0), (k, 0), (-k, 1), (k, 1)]
    steps += [(half, 0), (half, 1)]
    rel_place = jnp.array([r for r, _ in steps], jnp.int32)
    rel_core = jnp.array([c for _, c in steps], jnp.int32)
    at = (place + rel_place + chips) % chips
    at_chip = jnp.where(at < half, 2 * at, 2 * (chips - 1 - at) + 1)
    blocks = at_chip * CORES + (core + rel_core) % CORES

    cw = ring(single, 1)
    ccw = ring(single, -1)
    partner = flip(single, 1)

    meta = jnp.stack([chain, residue, valid], axis=0).astype(F32).reshape(1, 3 * tokens)
    mine = lax.broadcasted_iota(jnp.int32, (devices, 3 * tokens), 0) == me
    meta = jnp.where(mine, meta, 0.0)
    bit = 1
    while bit < devices:
        meta = meta + flip(meta, bit)
        bit *= 2
    meta = jnp.take(meta, blocks, axis=0).reshape(devices, 3, tokens)
    meta = jnp.transpose(meta, (1, 0, 2)).reshape(3, total)

    rows = tokens * samples
    query, gate = call(
        query_body,
        (jax.ShapeDtypeStruct((rows, width), BF16), jax.ShapeDtypeStruct((rows, width), F32)),
        (single, w_query, w_gate),
        flops=4 * rows * width * width,
        moved=4 * width * width + 8 * rows * width,
        name="query",
    )
    smem = pl.BlockSpec(memory_space=pltpu.SMEM)
    vmem = pl.BlockSpec(memory_space=pltpu.VMEM)

    def kv(parts):
        n = len(parts)
        shape = jax.ShapeDtypeStruct((samples, n * tokens, width), BF16)
        return call(
            kv_body,
            (shape, shape),
            (*parts, w_key, w_value),
            flops=4 * n * rows * width * width,
            moved=4 * width * width + 6 * n * rows * width,
            name="kv",
        )

    kvs = [kv([single, partner])]
    for k in range(1, half):
        if k + 1 < half:
            cw_next, ccw_next = ring(cw, 1), ring(ccw, -1)
        else:
            cw_next = ring(cw[: tokens // 2], 1)
            ccw_next = ring(ccw[tokens // 2 :], -1)
        cw_other, ccw_other = flip(cw, 1), flip(ccw, 1)
        kvs.append(kv([cw, ccw, cw_other, ccw_other]))
        cw, ccw = cw_next, ccw_next
    bias = call(
        bias_body,
        jax.ShapeDtypeStruct((heads, tokens, total), F32),
        (blocks, chain, residue, pair, w_pair, rel_table, meta),
        in_specs=[smem, smem, smem, vmem, vmem, vmem, vmem],
        flops=2 * tokens * total * heads * 512,
        moved=pair.size * 2 + heads * tokens * total * 4,
        name="bias",
    )
    cw_other, ccw_other = flip(cw, 1), flip(ccw, 1)
    args = [k for k, _ in kvs] + [v for _, v in kvs]
    args += [cw, ccw, cw_other, ccw_other, query, gate, bias, single, w_key, w_value, w_out]
    return call(
        functools.partial(attend_body, len(kvs), heads, 1.0 / math.sqrt(width // heads)),
        jax.ShapeDtypeStruct(single.shape, BF16),
        args,
        flops=4 * rows * total * width,
        moved=4 * samples * total * width,
        name="attend",
        limit=60 << 20,
    )


def solution(mesh):
    placed = (
        P(("groups", "tok"), None, None),
        P(("groups", "tok"), None, None),
        P(("groups", "tok")),
        P(("groups", "tok")),
        P(("groups", "tok")),
        P(),
        P(),
        P(),
        P(),
        P(),
        P(),
        P(),
    )
    return jax.shard_map(
        shards,
        mesh=mesh,
        in_specs=placed,
        out_specs=P(("groups", "tok"), None, None),
        check_vma=False,
    )
```

```python
import functools
import math

import jax
import jax.numpy as jnp
from jax import lax
from jax.experimental import pallas as pl
from jax.experimental.pallas import tpu as pltpu
from jax.sharding import PartitionSpec as P


NORM_EPS = 1e-05
MASK_PENALTY = 10000.0
F32 = jnp.float32
BF16 = jnp.bfloat16
CORES = 2
TILE = 256
VMEM = pl.BlockSpec(memory_space=pltpu.VMEM)
SMEM = pl.BlockSpec(memory_space=pltpu.SMEM)
VMEM = pl.BlockSpec(memory_space=pltpu.VMEM)
SMEM = pl.BlockSpec(memory_space=pltpu.SMEM)
VMEM = pl.BlockSpec(memory_space=pltpu.VMEM)
SMEM = pl.BlockSpec(memory_space=pltpu.SMEM)


def normed_rows(block):
    tokens, samples, width = block.shape
    values = block.astype(F32).reshape(tokens * samples, width)
    centred = values - jnp.mean(values, axis=-1, keepdims=True)
    spread = jnp.mean(centred * centred, axis=-1, keepdims=True)
    return (centred * lax.rsqrt(spread + NORM_EPS)).astype(BF16)


def sample_major(tokens, samples):
    rows = tokens * samples
    to = lax.broadcasted_iota(jnp.int32, (rows, rows), 0)
    frm = lax.broadcasted_iota(jnp.int32, (rows, rows), 1)
    want = (to % tokens) * samples + to // tokens
    return (want == frm).astype(F32).astype(BF16)


def token_major(tokens, samples):
    rows = tokens * samples
    to = lax.broadcasted_iota(jnp.int32, (rows, rows), 0)
    frm = lax.broadcasted_iota(jnp.int32, (rows, rows), 1)
    want = (to % samples) * tokens + to // samples
    return (want == frm).astype(F32).astype(BF16)


def matmul(a, b):
    return jnp.dot(a, b, preferred_element_type=F32)


META_ROWS = 8
RADIX = 128


def prep_body(single_ref, chain_ref, residue_ref, valid_ref, out_ref):
    tokens, samples, width = single_ref.shape
    rows = tokens * samples
    normed = normed_rows(single_ref[...])
    out_ref[pl.ds(0, rows), :] = matmul(sample_major(tokens, samples), normed).astype(BF16)
    residue = residue_ref[...]
    row = lax.broadcasted_iota(jnp.int32, (META_ROWS, tokens), 0)
    meta = jnp.where(row == 0, chain_ref[...], 0)
    meta = jnp.where(row == 1, residue // RADIX, meta)
    meta = jnp.where(row == 2, residue % RADIX, meta)
    meta = jnp.where(row == 3, valid_ref[...], meta)
    token = lax.broadcasted_iota(jnp.int32, (tokens, width), 0)
    lane = lax.broadcasted_iota(jnp.int32, (tokens, width), 1)
    spread = (lane % tokens == token).astype(F32).astype(BF16)
    tiled = matmul(meta.astype(F32).astype(BF16), spread)
    out_ref[pl.ds(rows, META_ROWS), :] = tiled.astype(BF16)


META_ROWS = 8
RADIX = 128


def prep_body(single_ref, chain_ref, residue_ref, valid_ref, out_ref):
    tokens, samples, width = single_ref.shape
    rows = tokens * samples
    normed = normed_rows(single_ref[...])
    out_ref[pl.ds(0, rows), :] = matmul(sample_major(tokens, samples), normed).astype(BF16)
    residue = residue_ref[...]
    row = lax.broadcasted_iota(jnp.int32, (META_ROWS, tokens), 0)
    meta = jnp.where(row == 0, chain_ref[...], 0)
    meta = jnp.where(row == 1, residue // RADIX, meta)
    meta = jnp.where(row == 2, residue % RADIX, meta)
    meta = jnp.where(row == 3, valid_ref[...], meta)
    token = lax.broadcasted_iota(jnp.int32, (tokens, width), 0)
    lane = lax.broadcasted_iota(jnp.int32, (tokens, width), 1)
    spread = (lane % tokens == token).astype(F32).astype(BF16)
    tiled = matmul(meta.astype(F32).astype(BF16), spread)
    out_ref[pl.ds(rows, META_ROWS), :] = tiled.astype(BF16)


META_ROWS = 8
RADIX = 128


def prep_body(single_ref, chain_ref, residue_ref, valid_ref, out_ref):
    tokens, samples, width = single_ref.shape
    rows = tokens * samples
    normed = normed_rows(single_ref[...])
    out_ref[pl.ds(0, rows), :] = matmul(sample_major(tokens, samples), normed).astype(BF16)
    residue = residue_ref[...]
    row = lax.broadcasted_iota(jnp.int32, (META_ROWS, tokens), 0)
    meta = jnp.where(row == 0, chain_ref[...], 0)
    meta = jnp.where(row == 1, residue // RADIX, meta)
    meta = jnp.where(row == 2, residue % RADIX, meta)
    meta = jnp.where(row == 3, valid_ref[...], meta)
    token = lax.broadcasted_iota(jnp.int32, (tokens, width), 0)
    lane = lax.broadcasted_iota(jnp.int32, (tokens, width), 1)
    spread = (lane % tokens == token).astype(F32).astype(BF16)
    tiled = matmul(meta.astype(F32).astype(BF16), spread)
    out_ref[pl.ds(rows, META_ROWS), :] = tiled.astype(BF16)


def query_body(pay_ref, wq_ref, wg_ref, q_ref, gate_ref):
    rows = pay_ref[pl.ds(0, q_ref.shape[0]), :]
    q_ref[...] = matmul(rows, wq_ref[...]).astype(BF16)
    gate_ref[...] = jax.nn.sigmoid(matmul(rows, wg_ref[...]))


def kv_body(*refs):
    wk_ref, wv_ref, out_ref = refs[-3:]
    blocks = refs[:-3]
    n = len(blocks)
    rows = blocks[0].shape[0] - META_ROWS
    parts = [b[pl.ds(0, rows), :] for b in blocks]
    data = jnp.concatenate(parts, axis=0) if n > 1 else parts[0]
    out_ref[pl.ds(0, n * rows), :] = matmul(data, wk_ref[...]).astype(BF16)
    out_ref[pl.ds(n * rows, n * rows), :] = matmul(data, wv_ref[...]).astype(BF16)
    for i, b in enumerate(blocks):
        out_ref[pl.ds(2 * n * rows + i * META_ROWS, META_ROWS), :] = b[pl.ds(rows, META_ROWS), :]


def ring_chip(place, chips):
    place = lax.rem(place + 2 * chips, chips)
    return jnp.where(place < chips // 2, 2 * place, 2 * (chips - 1 - place) + 1)


def bias_body(steps, chips, rows, me_ref, chain_ref, res_ref, pair_ref, wp_ref, tab_ref, *refs):
    out_ref = refs[-1]
    metas = refs[:-1]
    _, queries, total = out_ref.shape
    bins = tab_ref.shape[0]
    reach = (bins - 2) // 2
    tokens = total // len(steps)
    me = me_ref[0]
    chip = me // CORES
    core = lax.rem(me, CORES)
    place = jnp.where(lax.rem(chip, 2) == 0, chip // 2, chips - 1 - chip // 2)
    starts = []
    for r, c in steps:
        block = ring_chip(place + r, chips) * CORES + lax.rem(core + c, CORES)
        starts.append(pl.multiple_of(block * tokens, tokens))
    slot = lax.broadcasted_iota(jnp.int32, (META_ROWS, total), 1) // tokens
    keys = jnp.zeros((META_ROWS, total), F32)
    at = 0
    for m in metas:
        n = max(1, m.shape[0] // (2 * rows + META_ROWS))
        for u in range(n):
            row = m[pl.ds(m.shape[0] - (n - u) * META_ROWS, META_ROWS), :].astype(F32)
            row = jnp.concatenate([row] * (-(-total // row.shape[1])), axis=1)[:, :total]
            keys = jnp.where(slot == at, row, keys)
            at += 1
    chain_keys = keys[0:1, :]
    res_keys = keys[1:2, :] * RADIX + keys[2:3, :]
    mask = (keys[3:4, :] - 1.0) * MASK_PENALTY
    weights = jnp.transpose(wp_ref[...].astype(F32)).astype(BF16)
    table = jnp.transpose(tab_ref[...])
    high = table.astype(BF16)
    rest = table - high.astype(F32)
    mid = rest.astype(BF16)
    low = (rest - mid.astype(F32)).astype(BF16)
    bin_ids = lax.broadcasted_iota(jnp.int32, (bins, total), 0).astype(F32)
    for i in range(queries):
        data = jnp.concatenate([pair_ref[i, pl.ds(b, tokens), :] for b in starts], axis=0)
        acc = lax.dot_general(weights, data, (((1,), (1,)), ((), ())), preferred_element_type=F32)
        offset = jnp.clip(res_ref[i].astype(F32) - res_keys, -reach, reach) + reach
        bucket = jnp.where(chain_keys == chain_ref[i].astype(F32), offset, float(bins - 1))
        hot = (bin_ids == bucket).astype(F32).astype(BF16)
        rel = (matmul(low, hot) + matmul(mid, hot)) + matmul(high, hot)
        out_ref[:, i, :] = acc + rel + mask


def attend_rows(first, count, heads, scale, kv_refs, mine, other, q_ref, gate_ref, bias_ref, wk, wv):
    rows, width = gate_ref.shape
    half = mine.shape[0]
    tokens = half // count
    hs = width // heads
    data = jnp.concatenate([mine, other], axis=0)
    k_last = matmul(data, wk).astype(BF16)
    v_last = matmul(data, wv).astype(BF16)
    total = bias_ref.shape[2]
    bias = bias_ref[...].reshape(heads * tokens, total)
    lane_head = lax.broadcasted_iota(jnp.int32, (tokens, width), 1) // hs
    spans = []
    for t in range(width // TILE):
        spans.append(((t * TILE) // hs, ((t + 1) * TILE - 1) // hs))
    gated = []
    for s in range(count):
        keys, values = [], []
        for r in kv_refs:
            n = r.shape[0] // (2 * rows + META_ROWS)
            for u in range(n):
                keys.append(r[pl.ds(u * rows + (first + s) * tokens, tokens), :])
                values.append(r[pl.ds((n + u) * rows + (first + s) * tokens, tokens), :])
        for u in range(2):
            keys.append(k_last[u * half + s * tokens : u * half + (s + 1) * tokens])
            values.append(v_last[u * half + s * tokens : u * half + (s + 1) * tokens])
        keys = jnp.concatenate(keys, axis=0)
        values = jnp.concatenate(values, axis=0)
        q = q_ref[pl.ds((first + s) * tokens, tokens), :].astype(F32)
        per_head = [None] * heads
        for t, (h0, h1) in enumerate(spans):
            cut = slice(t * TILE, (t + 1) * TILE)
            masked = [
                jnp.where(lane_head[:, cut] == h, q[:, cut], 0.0).astype(BF16)
                for h in range(h0, h1 + 1)
            ]
            qt = jnp.concatenate(masked, axis=0)
            st = lax.dot_general(
                qt, keys[:, cut], (((1,), (1,)), ((), ())), preferred_element_type=F32
            )
            for h in range(h0, h1 + 1):
                part = st[(h - h0) * tokens : (h - h0 + 1) * tokens]
                per_head[h] = part if per_head[h] is None else per_head[h] + part
        scores = jnp.concatenate(per_head, axis=0) * scale + bias
        top = jnp.max(scores, axis=-1, keepdims=True)
        probs = jnp.exp(scores - top)
        inv = 1.0 / jnp.sum(probs, axis=-1, keepdims=True)
        probs = probs.astype(BF16)
        attended = []
        for t, (h0, h1) in enumerate(spans):
            cut = slice(t * TILE, (t + 1) * TILE)
            ot = matmul(probs[h0 * tokens : (h1 + 1) * tokens], values[:, cut])
            ot = ot * inv[h0 * tokens : (h1 + 1) * tokens]
            got = ot[:tokens]
            for h in range(h0 + 1, h1 + 1):
                here = ot[(h - h0) * tokens : (h - h0 + 1) * tokens]
                got = jnp.where(lane_head[:, cut] == h, here, got)
            attended.append(got)
        attended = jnp.concatenate(attended, axis=1)
        gated.append((gate_ref[pl.ds((first + s) * tokens, tokens), :] * attended).astype(BF16))
    return jnp.concatenate(gated, axis=0)


def attend_body(count, heads, scale, *refs):
    mine, other, q_ref, gate_ref, bias_ref, wk, wv, out_ref = refs[-8:]
    out_ref[...] = attend_rows(
        0, count, heads, scale, refs[:-8], mine[...], other[...], q_ref, gate_ref, bias_ref,
        wk[...], wv[...],
    )


def finish_body(count, heads, scale, *refs):
    mine, other, q_ref, gate_ref, bias_ref, wk, wv, done, single_ref, wo_ref, out_ref = refs[-11:]
    tokens, samples, width = single_ref.shape
    gated = attend_rows(
        samples - count, count, heads, scale, refs[:-11], mine[...], other[...], q_ref, gate_ref,
        bias_ref, wk[...], wv[...],
    )
    gated = jnp.concatenate([done[...], gated], axis=0)
    gated = matmul(token_major(tokens, samples), gated).astype(BF16)
    out = matmul(gated, wo_ref[...]).reshape(tokens, samples, width)
    out_ref[...] = (single_ref[...].astype(F32) + out).astype(BF16)


def call(body, out_shape, args, in_specs=None, flops=0, moved=0, limit=16 << 20):
    return pl.pallas_call(
        body,
        out_shape=out_shape,
        in_specs=in_specs or [VMEM] * len(args),
        out_specs=jax.tree.map(lambda _: VMEM, out_shape),
        compiler_params=pltpu.CompilerParams(vmem_limit_bytes=limit),
        cost_estimate=pl.CostEstimate(flops=flops, bytes_accessed=moved, transcendentals=0),
    )(*args)


def shards(
    single, pair, chain, residue, valid, w_query, w_key, w_value, w_gate, w_out, w_pair, rel_table
):
    tokens, samples, width = single.shape
    heads = w_pair.shape[1]
    total = pair.shape[1]
    rows = tokens * samples
    devices = lax.axis_size("tok")
    chips = devices // CORES
    half = chips // 2
    order = list(range(0, chips, 2)) + list(range(1, chips, 2))[::-1]
    me = lax.axis_index("tok").astype(jnp.int32).reshape(1)

    def ring(value, step):
        pairs = [
            (order[i] * CORES + c, order[(i + step) % chips] * CORES + c)
            for i in range(chips)
            for c in range(CORES)
        ]
        return lax.ppermute(value, "tok", pairs)

    def flip(value):
        return lax.ppermute(value, "tok", [(d, d ^ 1) for d in range(devices)])

    steps = [(0, 0), (0, 1)]
    for k in range(1, half):
        steps += [(-k, 0), (k, 0), (-k, 1), (k, 1)]
    steps += [(half, 0), (half, 1)]

    payload = call(
        prep_body,
        jax.ShapeDtypeStruct((rows + META_ROWS, width), BF16),
        (single, *(v.reshape(1, tokens) for v in (chain, residue, valid))),
        flops=rows * width * 16,
        moved=4 * rows * width,
    )
    cw = ring(payload, 1)
    ccw = ring(payload, -1)

    query, gate = call(
        query_body,
        (jax.ShapeDtypeStruct((rows, width), BF16), jax.ShapeDtypeStruct((rows, width), F32)),
        (payload, w_query, w_gate),
        flops=4 * rows * width * width,
        moved=4 * width * width + 8 * rows * width,
    )

    def kv(parts):
        n = len(parts)
        return call(
            kv_body,
            jax.ShapeDtypeStruct((n * (2 * rows + META_ROWS), width), BF16),
            (*parts, w_key, w_value),
            flops=4 * n * rows * width * width,
            moved=4 * width * width + 6 * n * rows * width,
        )

    far = ring(payload[rows:], half)
    far = [far, flip(far)]
    kvs = [kv([payload])]
    kvs.append(flip(kvs[-1]))
    for k in range(1, half):
        if k + 1 < half:
            cw_next = ring(cw, 1)
            ccw_next = ring(ccw, -1)
        else:
            cw_next = ring(cw[: rows // 2], 1)
            ccw_next = ring(ccw[rows // 2 : rows], -1)
        kvs.append(kv([cw, ccw]))
        kvs.append(flip(kvs[-1]))
        cw, ccw = cw_next, ccw_next
    bias = call(
        functools.partial(bias_body, steps, chips, rows),
        jax.ShapeDtypeStruct((heads, tokens, total), F32),
        (me, chain, residue, pair, w_pair, rel_table, *kvs, *far),
        in_specs=[SMEM, SMEM, SMEM, *[VMEM] * (5 + len(kvs))],
        flops=2 * tokens * total * heads * 512,
        moved=pair.size * 2 + heads * tokens * total * 4,
    )
    scale = 1.0 / math.sqrt(width // heads)
    count = samples // 2
    limit = min(60 << 20, (16 << 20) + 4 * samples * total * width)
    common = dict(flops=2 * rows * total * width, moved=2 * samples * total * width, limit=limit)
    gated = call(
        functools.partial(attend_body, count, heads, scale),
        jax.ShapeDtypeStruct((rows // 2, width), BF16),
        (*kvs, cw, flip(cw), query, gate, bias, w_key, w_value),
        **common,
    )
    return call(
        functools.partial(finish_body, count, heads, scale),
        jax.ShapeDtypeStruct(single.shape, BF16),
        (*kvs, ccw, flip(ccw), query, gate, bias, w_key, w_value, gated, single, w_out),
        **common,
    )


def solution(mesh):
    placed = (
        P(("groups", "tok"), None, None),
        P(("groups", "tok"), None, None),
        P(("groups", "tok")),
        P(("groups", "tok")),
        P(("groups", "tok")),
        P(),
        P(),
        P(),
        P(),
        P(),
        P(),
        P(),
    )

    return jax.shard_map(
        shards,
        mesh=mesh,
        in_specs=placed,
        out_specs=P(("groups", "tok"), None, None),
        check_vma=False,
    )
```

```python
import functools
import math

import jax
import jax.numpy as jnp
from jax import lax
from jax.experimental import pallas as pl
from jax.experimental.pallas import tpu as pltpu
from jax.sharding import PartitionSpec as P


NORM_EPS = 1e-05
MASK_PENALTY = 10000.0
F32 = jnp.float32
BF16 = jnp.bfloat16
CORES = 2
TILE = 256
VMEM = pl.BlockSpec(memory_space=pltpu.VMEM)
HBM = pl.BlockSpec(memory_space=pltpu.HBM)
ANY = pl.BlockSpec(memory_space=pl.ANY)
SMEM = pl.BlockSpec(memory_space=pltpu.SMEM)
VMEM = pl.BlockSpec(memory_space=pltpu.VMEM)
HBM = pl.BlockSpec(memory_space=pltpu.HBM)
ANY = pl.BlockSpec(memory_space=pl.ANY)
HBM = pl.BlockSpec(memory_space=pltpu.HBM)
ANY = pl.BlockSpec(memory_space=pl.ANY)
SMEM = pl.BlockSpec(memory_space=pltpu.SMEM)
VMEM = pl.BlockSpec(memory_space=pltpu.VMEM)
HBM = pl.BlockSpec(memory_space=pltpu.HBM)
ANY = pl.BlockSpec(memory_space=pl.ANY)
HBM = pl.BlockSpec(memory_space=pltpu.HBM)
ANY = pl.BlockSpec(memory_space=pl.ANY)
SMEM = pl.BlockSpec(memory_space=pltpu.SMEM)
VMEM = pl.BlockSpec(memory_space=pltpu.VMEM)
HBM = pl.BlockSpec(memory_space=pltpu.HBM)
ANY = pl.BlockSpec(memory_space=pl.ANY)
HBM = pl.BlockSpec(memory_space=pltpu.HBM)
ANY = pl.BlockSpec(memory_space=pl.ANY)
SMEM = pl.BlockSpec(memory_space=pltpu.SMEM)
VMEM = pl.BlockSpec(memory_space=pltpu.VMEM)
HBM = pl.BlockSpec(memory_space=pltpu.HBM)
ANY = pl.BlockSpec(memory_space=pl.ANY)
HBM = pl.BlockSpec(memory_space=pltpu.HBM)
ANY = pl.BlockSpec(memory_space=pl.ANY)
SMEM = pl.BlockSpec(memory_space=pltpu.SMEM)


def normed_rows(block):
    tokens, samples, width = block.shape
    values = block.astype(F32).reshape(tokens * samples, width)
    centred = values - jnp.mean(values, axis=-1, keepdims=True)
    spread = jnp.mean(centred * centred, axis=-1, keepdims=True)
    return (centred * lax.rsqrt(spread + NORM_EPS)).astype(BF16)


def sample_major(tokens, samples):
    rows = tokens * samples
    to = lax.broadcasted_iota(jnp.int32, (rows, rows), 0)
    frm = lax.broadcasted_iota(jnp.int32, (rows, rows), 1)
    want = (to % tokens) * samples + to // tokens
    return (want == frm).astype(F32).astype(BF16)


def token_major(tokens, samples):
    rows = tokens * samples
    to = lax.broadcasted_iota(jnp.int32, (rows, rows), 0)
    frm = lax.broadcasted_iota(jnp.int32, (rows, rows), 1)
    want = (to % samples) * tokens + to // samples
    return (want == frm).astype(F32).astype(BF16)


def matmul(a, b):
    return jnp.dot(a, b, preferred_element_type=F32)


META_ROWS = 8
RADIX = 128


def prep_body(single_ref, chain_ref, residue_ref, valid_ref, out_ref):
    tokens, samples, width = single_ref.shape
    rows = tokens * samples
    normed = normed_rows(single_ref[...])
    out_ref[pl.ds(0, rows), :] = matmul(sample_major(tokens, samples), normed).astype(BF16)
    residue = residue_ref[...]
    row = lax.broadcasted_iota(jnp.int32, (META_ROWS, tokens), 0)
    meta = jnp.where(row == 0, chain_ref[...], 0)
    meta = jnp.where(row == 1, residue // RADIX, meta)
    meta = jnp.where(row == 2, residue % RADIX, meta)
    meta = jnp.where(row == 3, valid_ref[...], meta)
    token = lax.broadcasted_iota(jnp.int32, (tokens, width), 0)
    lane = lax.broadcasted_iota(jnp.int32, (tokens, width), 1)
    spread = (lane % tokens == token).astype(F32).astype(BF16)
    tiled = matmul(meta.astype(F32).astype(BF16), spread)
    out_ref[pl.ds(rows, META_ROWS), :] = tiled.astype(BF16)


META_ROWS = 8
RADIX = 128


def prep_body(single_ref, chain_ref, residue_ref, valid_ref, out_ref):
    tokens, samples, width = single_ref.shape
    rows = tokens * samples
    normed = normed_rows(single_ref[...])
    out_ref[pl.ds(0, rows), :] = matmul(sample_major(tokens, samples), normed).astype(BF16)
    residue = residue_ref[...]
    row = lax.broadcasted_iota(jnp.int32, (META_ROWS, tokens), 0)
    meta = jnp.where(row == 0, chain_ref[...], 0)
    meta = jnp.where(row == 1, residue // RADIX, meta)
    meta = jnp.where(row == 2, residue % RADIX, meta)
    meta = jnp.where(row == 3, valid_ref[...], meta)
    token = lax.broadcasted_iota(jnp.int32, (tokens, width), 0)
    lane = lax.broadcasted_iota(jnp.int32, (tokens, width), 1)
    spread = (lane % tokens == token).astype(F32).astype(BF16)
    tiled = matmul(meta.astype(F32).astype(BF16), spread)
    out_ref[pl.ds(rows, META_ROWS), :] = tiled.astype(BF16)


META_ROWS = 8
RADIX = 128


def prep_body(single_ref, chain_ref, residue_ref, valid_ref, out_ref):
    tokens, samples, width = single_ref.shape
    rows = tokens * samples
    normed = normed_rows(single_ref[...])
    out_ref[pl.ds(0, rows), :] = matmul(sample_major(tokens, samples), normed).astype(BF16)
    residue = residue_ref[...]
    row = lax.broadcasted_iota(jnp.int32, (META_ROWS, tokens), 0)
    meta = jnp.where(row == 0, chain_ref[...], 0)
    meta = jnp.where(row == 1, residue // RADIX, meta)
    meta = jnp.where(row == 2, residue % RADIX, meta)
    meta = jnp.where(row == 3, valid_ref[...], meta)
    token = lax.broadcasted_iota(jnp.int32, (tokens, width), 0)
    lane = lax.broadcasted_iota(jnp.int32, (tokens, width), 1)
    spread = (lane % tokens == token).astype(F32).astype(BF16)
    tiled = matmul(meta.astype(F32).astype(BF16), spread)
    out_ref[pl.ds(rows, META_ROWS), :] = tiled.astype(BF16)


META_ROWS = 8
RADIX = 128


def prep_body(single_hbm, chain_hbm, residue_hbm, valid_hbm, out_ref, single_ref, ints_ref, sems):
    copies = [pltpu.make_async_copy(single_hbm, single_ref, sems.at[0])]
    for i, ref in enumerate((chain_hbm, residue_hbm, valid_hbm)):
        copies.append(pltpu.make_async_copy(ref, ints_ref.at[i], sems.at[i + 1]))
    for copy in copies:
        copy.start()
    tokens, samples, width = single_ref.shape
    rows = tokens * samples
    token = lax.broadcasted_iota(jnp.int32, (tokens, width), 0)
    lane = lax.broadcasted_iota(jnp.int32, (tokens, width), 1)
    spread = (lane % tokens == token).astype(F32).astype(BF16)
    perm = sample_major(tokens, samples)
    for copy in copies:
        copy.wait()
    normed = normed_rows(single_ref[...])
    out_ref[pl.ds(0, rows), :] = matmul(perm, normed).astype(BF16)
    residue = ints_ref[1]
    row = lax.broadcasted_iota(jnp.int32, (META_ROWS, tokens), 0)
    meta = jnp.where(row == 0, ints_ref[0], 0)
    meta = jnp.where(row == 1, residue // RADIX, meta)
    meta = jnp.where(row == 2, residue % RADIX, meta)
    meta = jnp.where(row == 3, ints_ref[2], meta)
    tiled = matmul(meta.astype(F32).astype(BF16), spread)
    out_ref[pl.ds(rows, META_ROWS), :] = tiled.astype(BF16)


META_ROWS = 8
RADIX = 128


def prep_body(single_hbm, chain_hbm, residue_hbm, valid_hbm, out_ref, meta_ref, single_ref, ints_ref, sems):
    copies = [pltpu.make_async_copy(single_hbm, single_ref, sems.at[0])]
    for i, ref in enumerate((chain_hbm, residue_hbm, valid_hbm)):
        copies.append(pltpu.make_async_copy(ref, ints_ref.at[i], sems.at[i + 1]))
    for copy in copies:
        copy.start()
    tokens, samples, width = single_ref.shape
    rows = tokens * samples
    token = lax.broadcasted_iota(jnp.int32, (tokens, width), 0)
    lane = lax.broadcasted_iota(jnp.int32, (tokens, width), 1)
    spread = (lane % tokens == token).astype(F32).astype(BF16)
    perm = sample_major(tokens, samples)
    for copy in copies:
        copy.wait()
    normed = normed_rows(single_ref[...])
    out_ref[pl.ds(0, rows), :] = matmul(perm, normed).astype(BF16)
    residue = ints_ref[1]
    row = lax.broadcasted_iota(jnp.int32, (META_ROWS, tokens), 0)
    meta = jnp.where(row == 0, ints_ref[0], 0)
    meta = jnp.where(row == 1, residue // RADIX, meta)
    meta = jnp.where(row == 2, residue % RADIX, meta)
    meta = jnp.where(row == 3, ints_ref[2], meta)
    tiled = matmul(meta.astype(F32).astype(BF16), spread)
    out_ref[pl.ds(rows, META_ROWS), :] = tiled.astype(BF16)
    meta_ref[...] = tiled.astype(BF16)


def query_body(pay_ref, wq_ref, wg_ref, q_ref, gate_ref):
    rows = pay_ref[pl.ds(0, q_ref.shape[0]), :]
    q_ref[...] = matmul(rows, wq_ref[...]).astype(BF16)
    gate_ref[...] = jax.nn.sigmoid(matmul(rows, wg_ref[...]))


def kv_body(*refs):
    wk_ref, wv_ref, out_ref = refs[-3:]
    blocks = refs[:-3]
    n = len(blocks)
    rows = blocks[0].shape[0] - META_ROWS
    parts = [b[pl.ds(0, rows), :] for b in blocks]
    data = jnp.concatenate(parts, axis=0) if n > 1 else parts[0]
    out_ref[pl.ds(0, n * rows), :] = matmul(data, wk_ref[...]).astype(BF16)
    out_ref[pl.ds(n * rows, n * rows), :] = matmul(data, wv_ref[...]).astype(BF16)
    for i, b in enumerate(blocks):
        out_ref[pl.ds(2 * n * rows + i * META_ROWS, META_ROWS), :] = b[pl.ds(rows, META_ROWS), :]


def ring_chip(place, chips):
    place = lax.rem(place + 2 * chips, chips)
    return jnp.where(place < chips // 2, 2 * place, 2 * (chips - 1 - place) + 1)


def pair_body(steps, chips, early, me_ref, pair_ref, wp_ref, *out_refs):
    queries, total, _ = pair_ref.shape
    tokens = total // len(steps)
    me = me_ref[0]
    chip = me // CORES
    core = lax.rem(me, CORES)
    place = jnp.where(lax.rem(chip, 2) == 0, chip // 2, chips - 1 - chip // 2)
    starts = []
    for r, c in steps:
        block = ring_chip(place + r, chips) * CORES + lax.rem(core + c, CORES)
        starts.append(pl.multiple_of(block * tokens, tokens))
    weights = wp_ref[...]
    for i in range(queries):
        for out_ref, part in zip(out_refs, (starts[:early], starts[early:])):
            data = jnp.concatenate([pair_ref[i, pl.ds(b, tokens), :] for b in part], axis=0)
            out_ref[:, i, :] = lax.dot_general(
                weights, data, (((1,), (1,)), ((), ())), preferred_element_type=F32
            )


def rel_body(counts, chain_ref, res_ref, tab_ref, bias_ref, *refs):
    n = len(counts)
    metas, out_ref, meta_ref, sems = refs[:n], refs[n], refs[n + 1], refs[n + 2]
    heads, queries, total = out_ref.shape
    copies, at = [], 0
    for i, (m, count) in enumerate(zip(metas, counts)):
        size = count * META_ROWS
        source = m.at[pl.ds(m.shape[0] - size, size), :]
        target = meta_ref.at[pl.ds(at * META_ROWS, size), :]
        copies.append(pltpu.make_async_copy(source, target, sems.at[i]))
        at += count
    for copy in copies:
        copy.start()
    bins = tab_ref.shape[1]
    reach = (bins - 2) // 2
    tokens = total // at
    table = tab_ref[...]
    high = table.astype(BF16)
    rest = table - high.astype(F32)
    mid = rest.astype(BF16)
    low = (rest - mid.astype(F32)).astype(BF16)
    parts = jnp.concatenate([low, mid, high], axis=0)
    bin_ids = lax.broadcasted_iota(jnp.int32, (bins, total), 0).astype(F32)
    slot = lax.broadcasted_iota(jnp.int32, (META_ROWS, total), 1) // tokens
    keys = jnp.zeros((META_ROWS, total), F32)
    for copy in copies:
        copy.wait()
    for u in range(at):
        row = meta_ref[pl.ds(u * META_ROWS, META_ROWS), :].astype(F32)
        row = jnp.concatenate([row] * (-(-total // row.shape[1])), axis=1)[:, :total]
        keys = jnp.where(slot == u, row, keys)
    chain_keys = keys[0:1, :]
    res_keys = keys[1:2, :] * RADIX + keys[2:3, :]
    mask = (keys[3:4, :] - 1.0) * MASK_PENALTY
    for i in range(queries):
        offset = jnp.clip(res_ref[i].astype(F32) - res_keys, -reach, reach) + reach
        bucket = jnp.where(chain_keys == chain_ref[i].astype(F32), offset, float(bins - 1))
        hot = (bin_ids == bucket).astype(F32).astype(BF16)
        rel = matmul(parts, hot)
        rel = (rel[:heads] + rel[heads : 2 * heads]) + rel[2 * heads :]
        out_ref[:, i, :] = bias_ref[:, i, :] + rel + mask


def head_spans(width, hs):
    return [((t * TILE) // hs, ((t + 1) * TILE - 1) // hs) for t in range(width // TILE)]


def score_rows(q, keys, bias, heads, scale):
    tokens, width = q.shape
    hs = width // heads
    lane_head = lax.broadcasted_iota(jnp.int32, (tokens, width), 1) // hs
    per_head = [None] * heads
    for t, (h0, h1) in enumerate(head_spans(width, hs)):
        cut = slice(t * TILE, (t + 1) * TILE)
        masked = [
            jnp.where(lane_head[:, cut] == h, q[:, cut], 0.0).astype(BF16)
            for h in range(h0, h1 + 1)
        ]
        st = lax.dot_general(
            jnp.concatenate(masked, axis=0),
            keys[:, cut],
            (((1,), (1,)), ((), ())),
            preferred_element_type=F32,
        )
        for h in range(h0, h1 + 1):
            part = st[(h - h0) * tokens : (h - h0 + 1) * tokens]
            per_head[h] = part if per_head[h] is None else per_head[h] + part
    return jnp.concatenate(per_head, axis=0) * scale + bias


def gather_keys(kv_refs, rows, at, tokens):
    keys, values = [], []
    for r in kv_refs:
        n = r.shape[0] // (2 * rows + META_ROWS)
        for u in range(n):
            keys.append(r[pl.ds(u * rows + at, tokens), :])
            values.append(r[pl.ds((n + u) * rows + at, tokens), :])
    return keys, values


def early_body(samples, heads, scale, *refs):
    q_ref, bias_ref, sum_ref, top_ref, mass_ref = refs[-5:]
    rows, width = q_ref.shape
    tokens = rows // samples
    spans = head_spans(width, width // heads)
    height = sum(h1 - h0 + 1 for h0, h1 in spans) * tokens
    bias = bias_ref[...].reshape(heads * tokens, bias_ref.shape[2])
    for s in range(samples):
        keys, values = gather_keys(refs[:-5], rows, s * tokens, tokens)
        keys, values = jnp.concatenate(keys, axis=0), jnp.concatenate(values, axis=0)
        q = q_ref[pl.ds(s * tokens, tokens), :].astype(F32)
        scores = score_rows(q, keys, bias, heads, scale)
        top = jnp.max(scores, axis=-1, keepdims=True)
        probs = jnp.exp(scores - top)
        mass = jnp.sum(probs, axis=-1, keepdims=True)
        here = pl.ds(s * heads * tokens, heads * tokens)
        top_ref[here, :] = jnp.broadcast_to(top, (heads * tokens, top_ref.shape[1]))
        mass_ref[here, :] = jnp.broadcast_to(mass, (heads * tokens, mass_ref.shape[1]))
        probs = probs.astype(BF16)
        at = s * height
        for t, (h0, h1) in enumerate(spans):
            part = probs[h0 * tokens : (h1 + 1) * tokens]
            got = matmul(part, values[:, t * TILE : (t + 1) * TILE])
            sum_ref[pl.ds(at, got.shape[0]), :] = got
            at += got.shape[0]


def attend_rows(first, count, heads, scale, kv_refs, mine, other, shared):
    q_ref, gate_ref, bias_ref, sum_ref, top_ref, mass_ref, wk_ref, wv_ref = shared
    rows, width = gate_ref.shape
    half = mine.shape[0]
    tokens = half // count
    hs = width // heads
    data = jnp.concatenate([mine, other], axis=0)
    k_last = matmul(data, wk_ref[...]).astype(BF16)
    v_last = matmul(data, wv_ref[...]).astype(BF16)
    bias = bias_ref[...].reshape(heads * tokens, bias_ref.shape[2])
    lane_head = lax.broadcasted_iota(jnp.int32, (tokens, width), 1) // hs
    spans = head_spans(width, hs)
    height = sum(h1 - h0 + 1 for h0, h1 in spans) * tokens
    gated = []
    for s in range(count):
        keys, values = gather_keys(kv_refs, rows, (first + s) * tokens, tokens)
        for u in range(2):
            keys.append(k_last[u * half + s * tokens : u * half + (s + 1) * tokens])
            values.append(v_last[u * half + s * tokens : u * half + (s + 1) * tokens])
        keys, values = jnp.concatenate(keys, axis=0), jnp.concatenate(values, axis=0)
        q = q_ref[pl.ds((first + s) * tokens, tokens), :].astype(F32)
        scores = score_rows(q, keys, bias, heads, scale)
        here = pl.ds((first + s) * heads * tokens, heads * tokens)
        top_before = top_ref[here, :][:, :1]
        top = jnp.maximum(jnp.max(scores, axis=-1, keepdims=True), top_before)
        shrink = jnp.exp(top_before - top)
        probs = jnp.exp(scores - top)
        mass = jnp.sum(probs, axis=-1, keepdims=True) + mass_ref[here, :][:, :1] * shrink
        inv = 1.0 / mass
        probs = probs.astype(BF16)
        shrink = shrink * inv
        attended = []
        at = (first + s) * height
        for t, (h0, h1) in enumerate(spans):
            cut = slice(t * TILE, (t + 1) * TILE)
            span = slice(h0 * tokens, (h1 + 1) * tokens)
            ot = matmul(probs[span], values[:, cut]) * inv[span]
            ot = ot + sum_ref[pl.ds(at, ot.shape[0]), :] * shrink[span]
            at += ot.shape[0]
            got = ot[:tokens]
            for h in range(h0 + 1, h1 + 1):
                part = ot[(h - h0) * tokens : (h - h0 + 1) * tokens]
                got = jnp.where(lane_head[:, cut] == h, part, got)
            attended.append(got)
        attended = jnp.concatenate(attended, axis=1)
        gated.append((gate_ref[pl.ds((first + s) * tokens, tokens), :] * attended).astype(BF16))
    return jnp.concatenate(gated, axis=0)


def attend_body(count, heads, scale, *refs):
    out_ref = refs[-1]
    shared = refs[-9:-1]
    mine, other = refs[-11], refs[-10]
    out_ref[...] = attend_rows(0, count, heads, scale, refs[:-11], mine[...], other[...], shared)


def finish_body(count, samples, heads, scale, *refs):
    done, single_ref, wo_ref, out_ref = refs[-4:]
    shared = refs[-12:-4]
    mine, other = refs[-14], refs[-13]
    tokens, samples, width = single_ref.shape
    gated = attend_rows(
        samples - count, count, heads, scale, refs[:-14], mine[...], other[...], shared
    )
    gated = jnp.concatenate([done[...], gated], axis=0)
    gated = matmul(token_major(tokens, samples), gated).astype(BF16)
    out = matmul(gated, wo_ref[...]).reshape(tokens, samples, width)
    out_ref[...] = (single_ref[...].astype(F32) + out).astype(BF16)


def call(body, out_shape, args, in_specs=None, flops=0, moved=0, limit=8 << 20, scratch=()):
    return pl.pallas_call(
        body,
        out_shape=out_shape,
        in_specs=in_specs or [VMEM] * len(args),
        out_specs=jax.tree.map(lambda _: VMEM, out_shape),
        scratch_shapes=scratch,
        compiler_params=pltpu.CompilerParams(vmem_limit_bytes=limit),
        cost_estimate=pl.CostEstimate(flops=flops, bytes_accessed=moved, transcendentals=0),
    )(*args)


def shards(
    single, pair, chain, residue, valid, w_query, w_key, w_value, w_gate, w_out, w_pair, rel_table
):
    tokens, samples, width = single.shape
    heads = w_pair.shape[1]
    total = pair.shape[1]
    rows = tokens * samples
    devices = lax.axis_size("tok")
    chips = devices // CORES
    half = chips // 2
    order = list(range(0, chips, 2)) + list(range(1, chips, 2))[::-1]
    me = lax.axis_index("tok").astype(jnp.int32).reshape(1)

    def ring(value, step):
        pairs = [
            (order[i] * CORES + c, order[(i + step) % chips] * CORES + c)
            for i in range(chips)
            for c in range(CORES)
        ]
        return lax.ppermute(value, "tok", pairs)

    def flip(value):
        return lax.ppermute(value, "tok", [(d, d ^ 1) for d in range(devices)])

    steps = [(0, 0), (0, 1)]
    for k in range(1, half):
        steps += [(-k, 0), (k, 0), (-k, 1), (k, 1)]
    steps += [(half, 0), (half, 1)]

    payload, meta = call(
        prep_body,
        (
            jax.ShapeDtypeStruct((rows + META_ROWS, width), BF16),
            jax.ShapeDtypeStruct((META_ROWS, width), BF16),
        ),
        (single, *(v.reshape(1, tokens) for v in (chain, residue, valid))),
        in_specs=[HBM] * 4,
        scratch=[
            pltpu.VMEM(single.shape, BF16),
            pltpu.VMEM((3, 1, tokens), jnp.int32),
            pltpu.SemaphoreType.DMA((4,)),
        ],
        flops=rows * width * 16,
        moved=4 * rows * width,
    )
    cw = ring(payload, 1)
    ccw = ring(payload, -1)

    query, gate = call(
        query_body,
        (jax.ShapeDtypeStruct((rows, width), BF16), jax.ShapeDtypeStruct((rows, width), F32)),
        (payload, w_query, w_gate),
        flops=4 * rows * width * width,
        moved=4 * width * width + 8 * rows * width,
    )

    def kv(parts):
        n = len(parts)
        return call(
            kv_body,
            jax.ShapeDtypeStruct((n * (2 * rows + META_ROWS), width), BF16),
            (*parts, w_key, w_value),
            flops=4 * n * rows * width * width,
            moved=4 * width * width + 6 * n * rows * width,
        )

    def piece(value, at):
        def body(in_ref, out_ref):
            out_ref[...] = in_ref[pl.ds(at, rows // 2), :]

        shape = jax.ShapeDtypeStruct((rows // 2, width), BF16)
        return call(body, shape, (value,), moved=2 * rows * width)

    far = ring(meta, half)
    far = [far, flip(far)]
    kvs = [kv([payload])]
    kvs.append(flip(kvs[-1]))
    for k in range(1, half):
        if k + 1 < half:
            cw_next = ring(cw, 1)
            ccw_next = ring(ccw, -1)
        else:
            cw_next = ring(piece(cw, 0), 1)
            ccw_next = ring(piece(ccw, rows // 2), -1)
        kvs.append(kv([cw, ccw]))
        kvs.append(flip(kvs[-1]))
        cw, ccw = cw_next, ccw_next
    early = len(steps) - 3 * CORES
    split = 2 * (half - 1)
    pair_shapes = tuple(
        jax.ShapeDtypeStruct((heads, tokens, n * tokens), F32) for n in (early, len(steps) - early)
    )
    pair_bias = call(
        functools.partial(pair_body, steps, chips, early),
        pair_shapes,
        (me, pair, w_pair.T),
        in_specs=[SMEM, VMEM, VMEM],
        flops=2 * pair.size * heads,
        moved=pair.size * 2 + heads * tokens * total * 4,
        limit=(4 << 20) + 2 * pair.size + 8 * heads * tokens * total,
    )

    def relative(at, metas):
        counts = [max(1, m.shape[0] // (2 * rows + META_ROWS)) for m in metas]
        return call(
            functools.partial(rel_body, counts),
            pair_shapes[at],
            (chain, residue, rel_table.T, pair_bias[at], *metas),
            in_specs=[SMEM, SMEM, VMEM, VMEM] + [ANY] * len(metas),
            flops=pair_shapes[at].size * 256,
            moved=8 * pair_shapes[at].size,
            scratch=[
                pltpu.VMEM((sum(counts) * META_ROWS, width), BF16),
                pltpu.SemaphoreType.DMA((len(metas),)),
            ],
        )

    scale = 1.0 / math.sqrt(width // heads)
    spans = head_spans(width, width // heads)
    height = sum(h1 - h0 + 1 for h0, h1 in spans) * tokens * samples
    state = jax.ShapeDtypeStruct((samples * heads * tokens, 128), F32)
    bias = relative(0, kvs[:split])
    limit = (10 << 20) + 4 * samples * total * width
    before = call(
        functools.partial(early_body, samples, heads, scale),
        (jax.ShapeDtypeStruct((height, TILE), F32), state, state),
        (*kvs[:split], query, bias),
        flops=4 * rows * early * tokens * width,
        moved=4 * samples * early * tokens * width,
        limit=limit,
    )
    bias = relative(1, [*kvs[split:], *far])
    count = samples // 2
    common = dict(flops=2 * rows * total * width, moved=samples * total * width, limit=limit)
    shared = (query, gate, bias, *before, w_key, w_value)
    gated = call(
        functools.partial(attend_body, count, heads, scale),
        jax.ShapeDtypeStruct((rows // 2, width), BF16),
        (*kvs[split:], cw, flip(cw), *shared),
        **common,
    )
    return call(
        functools.partial(finish_body, count, samples, heads, scale),
        jax.ShapeDtypeStruct(single.shape, BF16),
        (*kvs[split:], ccw, flip(ccw), *shared, gated, single, w_out),
        **common,
    )


def solution(mesh):
    placed = (
        P(("groups", "tok"), None, None),
        P(("groups", "tok"), None, None),
        P(("groups", "tok")),
        P(("groups", "tok")),
        P(("groups", "tok")),
        P(),
        P(),
        P(),
        P(),
        P(),
        P(),
        P(),
    )

    step = jax.shard_map(
        shards,
        mesh=mesh,
        in_specs=placed,
        out_specs=P(("groups", "tok"), None, None),
        check_vma=False,
    )
    return step
    return step
    return step
```

```python
import functools
import math

import jax
import jax.numpy as jnp
from jax import lax
from jax.experimental import pallas as pl
from jax.experimental.pallas import tpu as pltpu
from jax.sharding import PartitionSpec as P


NORM_EPS = 1e-05
MASK_PENALTY = 10000.0
F32 = jnp.float32
BF16 = jnp.bfloat16
CORES = 2
TILE = 256
LANES = 128
FULL = 60 << 20
VMEM = pl.BlockSpec(memory_space=pltpu.VMEM)
ANY = pl.BlockSpec(memory_space=pl.ANY)
SMEM = pl.BlockSpec(memory_space=pltpu.SMEM)
VMEM = pl.BlockSpec(memory_space=pltpu.VMEM)
ANY = pl.BlockSpec(memory_space=pl.ANY)
ANY = pl.BlockSpec(memory_space=pl.ANY)
SMEM = pl.BlockSpec(memory_space=pltpu.SMEM)
VMEM = pl.BlockSpec(memory_space=pltpu.VMEM)
ANY = pl.BlockSpec(memory_space=pl.ANY)
ANY = pl.BlockSpec(memory_space=pl.ANY)
ANY = pl.BlockSpec(memory_space=pl.ANY)
SMEM = pl.BlockSpec(memory_space=pltpu.SMEM)
VMEM = pl.BlockSpec(memory_space=pltpu.VMEM)
ANY = pl.BlockSpec(memory_space=pl.ANY)
ANY = pl.BlockSpec(memory_space=pl.ANY)
ANY = pl.BlockSpec(memory_space=pl.ANY)
SMEM = pl.BlockSpec(memory_space=pltpu.SMEM)
VMEM = pl.BlockSpec(memory_space=pltpu.VMEM)
ANY = pl.BlockSpec(memory_space=pl.ANY)
ANY = pl.BlockSpec(memory_space=pl.ANY)
ANY = pl.BlockSpec(memory_space=pl.ANY)
SMEM = pl.BlockSpec(memory_space=pltpu.SMEM)
VMEM = pl.BlockSpec(memory_space=pltpu.VMEM)
ANY = pl.BlockSpec(memory_space=pl.ANY)
ANY = pl.BlockSpec(memory_space=pl.ANY)
ANY = pl.BlockSpec(memory_space=pl.ANY)
SMEM = pl.BlockSpec(memory_space=pltpu.SMEM)


def normed_rows(block):
    tokens, samples, width = block.shape
    values = block.astype(F32).reshape(tokens * samples, width)
    centred = values - jnp.mean(values, axis=-1, keepdims=True)
    spread = jnp.mean(centred * centred, axis=-1, keepdims=True)
    return (centred * lax.rsqrt(spread + NORM_EPS)).astype(BF16)


def sample_major(tokens, samples):
    rows = tokens * samples
    to = lax.broadcasted_iota(jnp.int32, (rows, rows), 0)
    frm = lax.broadcasted_iota(jnp.int32, (rows, rows), 1)
    want = (to % tokens) * samples + to // tokens
    return (want == frm).astype(F32).astype(BF16)


def token_major(tokens, samples):
    rows = tokens * samples
    to = lax.broadcasted_iota(jnp.int32, (rows, rows), 0)
    frm = lax.broadcasted_iota(jnp.int32, (rows, rows), 1)
    want = (to % samples) * tokens + to // samples
    return (want == frm).astype(F32).astype(BF16)


def matmul(a, b):
    return jnp.dot(a, b, preferred_element_type=F32)


META_ROWS = 8
RADIX = 128


def prep_body(single_ref, chain_ref, residue_ref, valid_ref, out_ref):
    tokens, samples, width = single_ref.shape
    rows = tokens * samples
    normed = normed_rows(single_ref[...])
    out_ref[pl.ds(0, rows), :] = matmul(sample_major(tokens, samples), normed).astype(BF16)
    residue = residue_ref[...]
    row = lax.broadcasted_iota(jnp.int32, (META_ROWS, tokens), 0)
    meta = jnp.where(row == 0, chain_ref[...], 0)
    meta = jnp.where(row == 1, residue // RADIX, meta)
    meta = jnp.where(row == 2, residue % RADIX, meta)
    meta = jnp.where(row == 3, valid_ref[...], meta)
    token = lax.broadcasted_iota(jnp.int32, (tokens, width), 0)
    lane = lax.broadcasted_iota(jnp.int32, (tokens, width), 1)
    spread = (lane % tokens == token).astype(F32).astype(BF16)
    tiled = matmul(meta.astype(F32).astype(BF16), spread)
    out_ref[pl.ds(rows, META_ROWS), :] = tiled.astype(BF16)


META_ROWS = 8
RADIX = 128


def prep_body(single_ref, chain_ref, residue_ref, valid_ref, out_ref):
    tokens, samples, width = single_ref.shape
    rows = tokens * samples
    normed = normed_rows(single_ref[...])
    out_ref[pl.ds(0, rows), :] = matmul(sample_major(tokens, samples), normed).astype(BF16)
    residue = residue_ref[...]
    row = lax.broadcasted_iota(jnp.int32, (META_ROWS, tokens), 0)
    meta = jnp.where(row == 0, chain_ref[...], 0)
    meta = jnp.where(row == 1, residue // RADIX, meta)
    meta = jnp.where(row == 2, residue % RADIX, meta)
    meta = jnp.where(row == 3, valid_ref[...], meta)
    token = lax.broadcasted_iota(jnp.int32, (tokens, width), 0)
    lane = lax.broadcasted_iota(jnp.int32, (tokens, width), 1)
    spread = (lane % tokens == token).astype(F32).astype(BF16)
    tiled = matmul(meta.astype(F32).astype(BF16), spread)
    out_ref[pl.ds(rows, META_ROWS), :] = tiled.astype(BF16)


META_ROWS = 8
RADIX = 128


def prep_body(single_ref, chain_ref, residue_ref, valid_ref, out_ref):
    tokens, samples, width = single_ref.shape
    rows = tokens * samples
    normed = normed_rows(single_ref[...])
    out_ref[pl.ds(0, rows), :] = matmul(sample_major(tokens, samples), normed).astype(BF16)
    residue = residue_ref[...]
    row = lax.broadcasted_iota(jnp.int32, (META_ROWS, tokens), 0)
    meta = jnp.where(row == 0, chain_ref[...], 0)
    meta = jnp.where(row == 1, residue // RADIX, meta)
    meta = jnp.where(row == 2, residue % RADIX, meta)
    meta = jnp.where(row == 3, valid_ref[...], meta)
    token = lax.broadcasted_iota(jnp.int32, (tokens, width), 0)
    lane = lax.broadcasted_iota(jnp.int32, (tokens, width), 1)
    spread = (lane % tokens == token).astype(F32).astype(BF16)
    tiled = matmul(meta.astype(F32).astype(BF16), spread)
    out_ref[pl.ds(rows, META_ROWS), :] = tiled.astype(BF16)


META_ROWS = 8
RADIX = 128


def prep_body(single_hbm, chain_hbm, residue_hbm, valid_hbm, out_ref, single_ref, ints_ref, sems):
    copies = [pltpu.make_async_copy(single_hbm, single_ref, sems.at[0])]
    for i, ref in enumerate((chain_hbm, residue_hbm, valid_hbm)):
        copies.append(pltpu.make_async_copy(ref, ints_ref.at[i], sems.at[i + 1]))
    for copy in copies:
        copy.start()
    tokens, samples, width = single_ref.shape
    rows = tokens * samples
    token = lax.broadcasted_iota(jnp.int32, (tokens, width), 0)
    lane = lax.broadcasted_iota(jnp.int32, (tokens, width), 1)
    spread = (lane % tokens == token).astype(F32).astype(BF16)
    perm = sample_major(tokens, samples)
    for copy in copies:
        copy.wait()
    normed = normed_rows(single_ref[...])
    out_ref[pl.ds(0, rows), :] = matmul(perm, normed).astype(BF16)
    residue = ints_ref[1]
    row = lax.broadcasted_iota(jnp.int32, (META_ROWS, tokens), 0)
    meta = jnp.where(row == 0, ints_ref[0], 0)
    meta = jnp.where(row == 1, residue // RADIX, meta)
    meta = jnp.where(row == 2, residue % RADIX, meta)
    meta = jnp.where(row == 3, ints_ref[2], meta)
    tiled = matmul(meta.astype(F32).astype(BF16), spread)
    out_ref[pl.ds(rows, META_ROWS), :] = tiled.astype(BF16)


META_ROWS = 8
RADIX = 128


def prep_body(single_hbm, chain_hbm, residue_hbm, valid_hbm, out_ref, meta_ref, single_ref, ints_ref, sems):
    copies = [pltpu.make_async_copy(single_hbm, single_ref, sems.at[0])]
    for i, ref in enumerate((chain_hbm, residue_hbm, valid_hbm)):
        copies.append(pltpu.make_async_copy(ref, ints_ref.at[i], sems.at[i + 1]))
    for copy in copies:
        copy.start()
    tokens, samples, width = single_ref.shape
    rows = tokens * samples
    token = lax.broadcasted_iota(jnp.int32, (tokens, width), 0)
    lane = lax.broadcasted_iota(jnp.int32, (tokens, width), 1)
    spread = (lane % tokens == token).astype(F32).astype(BF16)
    perm = sample_major(tokens, samples)
    for copy in copies:
        copy.wait()
    normed = normed_rows(single_ref[...])
    out_ref[pl.ds(0, rows), :] = matmul(perm, normed).astype(BF16)
    residue = ints_ref[1]
    row = lax.broadcasted_iota(jnp.int32, (META_ROWS, tokens), 0)
    meta = jnp.where(row == 0, ints_ref[0], 0)
    meta = jnp.where(row == 1, residue // RADIX, meta)
    meta = jnp.where(row == 2, residue % RADIX, meta)
    meta = jnp.where(row == 3, ints_ref[2], meta)
    tiled = matmul(meta.astype(F32).astype(BF16), spread)
    out_ref[pl.ds(rows, META_ROWS), :] = tiled.astype(BF16)
    meta_ref[...] = tiled.astype(BF16)


META_ROWS = 8
RADIX = 128


def prep_body(single_hbm, chain_hbm, residue_hbm, valid_hbm, out_ref, single_ref, ints_ref, sems):
    copies = [pltpu.make_async_copy(single_hbm, single_ref, sems.at[0])]
    for i, ref in enumerate((chain_hbm, residue_hbm, valid_hbm)):
        copies.append(pltpu.make_async_copy(ref, ints_ref.at[i], sems.at[i + 1]))
    for copy in copies:
        copy.start()
    tokens, samples, width = single_ref.shape
    rows = tokens * samples
    token = lax.broadcasted_iota(jnp.int32, (tokens, width), 0)
    lane = lax.broadcasted_iota(jnp.int32, (tokens, width), 1)
    spread = (lane % tokens == token).astype(F32).astype(BF16)
    perm = sample_major(tokens, samples)
    for copy in copies:
        copy.wait()
    normed = normed_rows(single_ref[...])
    out_ref[pl.ds(0, rows), :] = matmul(perm, normed).astype(BF16)
    residue = ints_ref[1]
    row = lax.broadcasted_iota(jnp.int32, (META_ROWS, tokens), 0)
    meta = jnp.where(row == 0, ints_ref[0], 0)
    meta = jnp.where(row == 1, residue // RADIX, meta)
    meta = jnp.where(row == 2, residue % RADIX, meta)
    meta = jnp.where(row == 3, ints_ref[2], meta)
    tiled = matmul(meta.astype(F32).astype(BF16), spread)
    out_ref[pl.ds(rows, META_ROWS), :] = tiled.astype(BF16)


def own_body(
    steps, chips, early, me_ref, pay_hbm, wq_hbm, wk_hbm, wv_hbm, wg_hbm, pair_hbm, wp_hbm,
    q_ref, gate_ref, kv_ref, first_ref, second_ref,
    pay_ref, wq_ref, wk_ref, wv_ref, wg_ref, pair_ref, wp_ref, sems,
):
    copies = {}
    moves = [
        (pay_hbm, pay_ref), (wq_hbm, wq_ref), (wp_hbm, wp_ref), (pair_hbm, pair_ref),
        (wk_hbm, wk_ref), (wv_hbm, wv_ref), (wg_hbm, wg_ref),
    ]
    for i, (source, target) in enumerate(moves):
        copies[i] = pltpu.make_async_copy(source, target, sems.at[i])
        copies[i].start()
    rows = q_ref.shape[0]
    copies[0].wait()
    data = pay_ref[pl.ds(0, rows), :]
    copies[1].wait()
    q_ref[...] = matmul(data, wq_ref[...]).astype(BF16)
    copies[2].wait()
    copies[3].wait()
    pair_rows(steps, chips, early, me_ref[0], pair_ref, wp_ref[...], (first_ref, second_ref))
    copies[4].wait()
    kv_ref[pl.ds(0, rows), :] = matmul(data, wk_ref[...]).astype(BF16)
    copies[5].wait()
    kv_ref[pl.ds(rows, rows), :] = matmul(data, wv_ref[...]).astype(BF16)
    kv_ref[pl.ds(2 * rows, META_ROWS), :] = pay_ref[pl.ds(rows, META_ROWS), :]
    copies[6].wait()
    gate_ref[...] = jax.nn.sigmoid(matmul(data, wg_ref[...]))


def kv_body(*refs):
    wk_ref, wv_ref, out_ref = refs[-3:]
    blocks = refs[:-3]
    n = len(blocks)
    rows = blocks[0].shape[0] - META_ROWS
    parts = [b[pl.ds(0, rows), :] for b in blocks]
    data = jnp.concatenate(parts, axis=0) if n > 1 else parts[0]
    out_ref[pl.ds(0, n * rows), :] = matmul(data, wk_ref[...]).astype(BF16)
    out_ref[pl.ds(n * rows, n * rows), :] = matmul(data, wv_ref[...]).astype(BF16)
    for i, b in enumerate(blocks):
        out_ref[pl.ds(2 * n * rows + i * META_ROWS, META_ROWS), :] = b[pl.ds(rows, META_ROWS), :]


def ring_chip(place, chips):
    place = lax.rem(place + 2 * chips, chips)
    return jnp.where(place < chips // 2, 2 * place, 2 * (chips - 1 - place) + 1)


def pair_rows(steps, chips, early, me, pair_ref, weights, out_refs):
    queries, total, _ = pair_ref.shape
    tokens = total // len(steps)
    chip = me // CORES
    core = lax.rem(me, CORES)
    place = jnp.where(lax.rem(chip, 2) == 0, chip // 2, chips - 1 - chip // 2)
    starts = []
    for r, c in steps:
        block = ring_chip(place + r, chips) * CORES + lax.rem(core + c, CORES)
        starts.append(pl.multiple_of(block * tokens, tokens))
    for i in range(queries):
        for out_ref, part in zip(out_refs, (starts[:early], starts[early:])):
            data = jnp.concatenate([pair_ref[i, pl.ds(b, tokens), :] for b in part], axis=0)
            out_ref[:, i, :] = lax.dot_general(
                weights, data, (((1,), (1,)), ((), ())), preferred_element_type=F32
            )


def kv_count(ref, rows):
    return ref.shape[0] // (2 * rows + META_ROWS)


def kv_metas(kv_refs, rows):
    found = []
    for r in kv_refs:
        n = kv_count(r, rows)
        found += [r[pl.ds(2 * n * rows + u * META_ROWS, META_ROWS), :] for u in range(n)]
    return found


def full_bias(own, metas, tokens, pair_ref, tab_ref, pad_ref):
    heads, _, total = pair_ref.shape
    bins = tab_ref.shape[1]
    reach = (bins - 2) // 2
    wide = -(-total // LANES) * LANES
    slot = lax.broadcasted_iota(jnp.int32, (META_ROWS, wide), 1) // tokens
    keys = jnp.zeros((META_ROWS, wide), F32)
    for u, row in enumerate(metas):
        row = row.astype(F32)
        row = jnp.concatenate([row] * (-(-wide // row.shape[1])), axis=1)[:, :wide]
        keys = jnp.where(slot == u, row, keys)
    here = own.astype(F32)[:, :LANES]
    lane = lax.broadcasted_iota(jnp.int32, (tokens, LANES), 1)
    row = lax.broadcasted_iota(jnp.int32, (tokens, LANES), 0)

    def column(values):
        values = jnp.where(lane == row, jnp.broadcast_to(values, (tokens, LANES)), 0.0)
        return jnp.sum(values, axis=-1, keepdims=True)

    chain_q = column(here[0:1, :])
    res_q = column(here[1:2, :] * RADIX + here[2:3, :])
    res_keys = keys[1:2, :] * RADIX + keys[2:3, :]
    offset = jnp.clip(res_q - res_keys, -reach, reach) + reach
    bucket = jnp.where(chain_q == keys[0:1, :], offset, float(bins - 1)).astype(jnp.int32)
    mask = (keys[3:4, :total] - 1.0) * MASK_PENALTY
    pad_ref[...] = jnp.zeros_like(pad_ref)
    pad_ref[:, pl.ds(0, bins)] = tab_ref[...]
    out = []
    for h in range(heads):
        table = jnp.broadcast_to(pad_ref[h : h + 1, :], (tokens, LANES))
        rel = [
            jnp.take_along_axis(
                table, bucket[:, at : at + LANES], axis=1, mode="promise_in_bounds"
            )
            for at in range(0, wide, LANES)
        ]
        rel = jnp.concatenate(rel, axis=1)[:, :total] if len(rel) > 1 else rel[0][:, :total]
        out.append(pair_ref[h] + rel + mask)
    return jnp.concatenate(out, axis=0)


def head_spans(width, hs):
    return [((t * TILE) // hs, ((t + 1) * TILE - 1) // hs) for t in range(width // TILE)]


def score_rows(q, keys, bias, heads, scale):
    tokens, width = q.shape
    hs = width // heads
    lane_head = lax.broadcasted_iota(jnp.int32, (tokens, width), 1) // hs
    per_head = [None] * heads
    for t, (h0, h1) in enumerate(head_spans(width, hs)):
        cut = slice(t * TILE, (t + 1) * TILE)
        masked = [
            jnp.where(lane_head[:, cut] == h, q[:, cut], 0.0).astype(BF16)
            for h in range(h0, h1 + 1)
        ]
        st = lax.dot_general(
            jnp.concatenate(masked, axis=0),
            keys[:, cut],
            (((1,), (1,)), ((), ())),
            preferred_element_type=F32,
        )
        for h in range(h0, h1 + 1):
            part = st[(h - h0) * tokens : (h - h0 + 1) * tokens]
            per_head[h] = part if per_head[h] is None else per_head[h] + part
    return jnp.concatenate(per_head, axis=0) * scale + bias


def gather_keys(kv_refs, rows, at, tokens):
    keys, values = [], []
    for r in kv_refs:
        n = r.shape[0] // (2 * rows + META_ROWS)
        for u in range(n):
            keys.append(r[pl.ds(u * rows + at, tokens), :])
            values.append(r[pl.ds((n + u) * rows + at, tokens), :])
    return keys, values


def early_body(samples, heads, scale, *refs):
    q_ref, pair_ref, tab_ref, sum_ref, top_ref, mass_ref, pad_ref = refs[-7:]
    kv_refs = refs[:-7]
    rows, width = q_ref.shape
    tokens = rows // samples
    spans = head_spans(width, width // heads)
    height = sum(h1 - h0 + 1 for h0, h1 in spans) * tokens
    metas = kv_metas(kv_refs, rows)
    bias = full_bias(metas[0], metas, tokens, pair_ref, tab_ref, pad_ref)
    for s in range(samples):
        keys, values = gather_keys(kv_refs, rows, s * tokens, tokens)
        keys, values = jnp.concatenate(keys, axis=0), jnp.concatenate(values, axis=0)
        q = q_ref[pl.ds(s * tokens, tokens), :].astype(F32)
        scores = score_rows(q, keys, bias, heads, scale)
        top = jnp.max(scores, axis=-1, keepdims=True)
        probs = jnp.exp(scores - top)
        mass = jnp.sum(probs, axis=-1, keepdims=True)
        here = pl.ds(s * heads * tokens, heads * tokens)
        top_ref[here, :] = jnp.broadcast_to(top, (heads * tokens, top_ref.shape[1]))
        mass_ref[here, :] = jnp.broadcast_to(mass, (heads * tokens, mass_ref.shape[1]))
        probs = probs.astype(BF16)
        at = s * height
        for t, (h0, h1) in enumerate(spans):
            part = probs[h0 * tokens : (h1 + 1) * tokens]
            got = matmul(part, values[:, t * TILE : (t + 1) * TILE])
            sum_ref[pl.ds(at, got.shape[0]), :] = got
            at += got.shape[0]


def attend_rows(first, count, heads, scale, kv_refs, mine, other, bias, shared):
    q_ref, gate_ref, sum_ref, top_ref, mass_ref, wk_ref, wv_ref = shared
    rows, width = gate_ref.shape
    half = mine.shape[0]
    tokens = half // count
    hs = width // heads
    data = jnp.concatenate([mine, other], axis=0)
    k_last = matmul(data, wk_ref[...]).astype(BF16)
    v_last = matmul(data, wv_ref[...]).astype(BF16)
    lane_head = lax.broadcasted_iota(jnp.int32, (tokens, width), 1) // hs
    spans = head_spans(width, hs)
    height = sum(h1 - h0 + 1 for h0, h1 in spans) * tokens
    gated = []
    for s in range(count):
        keys, values = gather_keys(kv_refs, rows, (first + s) * tokens, tokens)
        for u in range(2):
            keys.append(k_last[u * half + s * tokens : u * half + (s + 1) * tokens])
            values.append(v_last[u * half + s * tokens : u * half + (s + 1) * tokens])
        keys, values = jnp.concatenate(keys, axis=0), jnp.concatenate(values, axis=0)
        q = q_ref[pl.ds((first + s) * tokens, tokens), :].astype(F32)
        scores = score_rows(q, keys, bias, heads, scale)
        here = pl.ds((first + s) * heads * tokens, heads * tokens)
        top_before = top_ref[here, :][:, :1]
        top = jnp.maximum(jnp.max(scores, axis=-1, keepdims=True), top_before)
        shrink = jnp.exp(top_before - top)
        probs = jnp.exp(scores - top)
        mass = jnp.sum(probs, axis=-1, keepdims=True) + mass_ref[here, :][:, :1] * shrink
        inv = 1.0 / mass
        probs = probs.astype(BF16)
        shrink = shrink * inv
        attended = []
        at = (first + s) * height
        for t, (h0, h1) in enumerate(spans):
            cut = slice(t * TILE, (t + 1) * TILE)
            span = slice(h0 * tokens, (h1 + 1) * tokens)
            ot = matmul(probs[span], values[:, cut]) * inv[span]
            ot = ot + sum_ref[pl.ds(at, ot.shape[0]), :] * shrink[span]
            at += ot.shape[0]
            got = ot[:tokens]
            for h in range(h0 + 1, h1 + 1):
                part = ot[(h - h0) * tokens : (h - h0 + 1) * tokens]
                got = jnp.where(lane_head[:, cut] == h, part, got)
            attended.append(got)
        attended = jnp.concatenate(attended, axis=1)
        gated.append((gate_ref[pl.ds((first + s) * tokens, tokens), :] * attended).astype(BF16))
    return jnp.concatenate(gated, axis=0)


def attend_body(count, samples, heads, scale, *refs):
    pair_ref, tab_ref, pay_ref, out_ref, bias_ref, pad_ref = refs[-6:]
    shared = refs[-13:-6]
    kv_refs, mine, other = refs[:-15], refs[-15], refs[-14]
    rows = shared[0].shape[0]
    tokens = rows // samples
    half = count * tokens
    metas = kv_metas(kv_refs, rows)
    metas += [m[pl.ds(half, META_ROWS), :] for m in (mine, other)]
    own = pay_ref[pl.ds(rows, META_ROWS), :]
    bias = full_bias(own, metas, tokens, pair_ref, tab_ref, pad_ref)
    bias_ref[...] = bias
    mine, other = mine[pl.ds(0, half), :], other[pl.ds(0, half), :]
    out_ref[...] = attend_rows(0, count, heads, scale, kv_refs, mine, other, bias, shared)


def finish_body(count, samples, heads, scale, *refs):
    bias_ref, done, single_ref, wo_ref, out_ref = refs[-5:]
    shared = refs[-12:-5]
    kv_refs, mine, other = refs[:-14], refs[-14], refs[-13]
    tokens, samples, width = single_ref.shape
    gated = attend_rows(
        samples - count, count, heads, scale, kv_refs, mine[...], other[...],
        bias_ref[...], shared,
    )
    gated = jnp.concatenate([done[...], gated], axis=0)
    gated = matmul(token_major(tokens, samples), gated).astype(BF16)
    out = matmul(gated, wo_ref[...]).reshape(tokens, samples, width)
    out_ref[...] = (single_ref[...].astype(F32) + out).astype(BF16)


def call(body, out_shape, args, in_specs=None, flops=0, moved=0, limit=8 << 20, scratch=()):
    return pl.pallas_call(
        body,
        out_shape=out_shape,
        in_specs=in_specs or [VMEM] * len(args),
        out_specs=jax.tree.map(lambda _: VMEM, out_shape),
        scratch_shapes=scratch,
        compiler_params=pltpu.CompilerParams(vmem_limit_bytes=limit),
        cost_estimate=pl.CostEstimate(flops=flops, bytes_accessed=moved, transcendentals=0),
    )(*args)


def shards(
    single, pair, chain, residue, valid, w_query, w_key, w_value, w_gate, w_out, w_pair, rel_table
):
    tokens, samples, width = single.shape
    heads = w_pair.shape[1]
    total = pair.shape[1]
    rows = tokens * samples
    devices = lax.axis_size("tok")
    chips = devices // CORES
    half = chips // 2
    order = list(range(0, chips, 2)) + list(range(1, chips, 2))[::-1]
    me = lax.axis_index("tok").astype(jnp.int32).reshape(1)

    def ring(value, step):
        pairs = [
            (order[i] * CORES + c, order[(i + step) % chips] * CORES + c)
            for i in range(chips)
            for c in range(CORES)
        ]
        return lax.ppermute(value, "tok", pairs)

    def flip(value):
        return lax.ppermute(value, "tok", [(d, d ^ 1) for d in range(devices)])

    steps = [(0, 0), (0, 1)]
    for k in range(1, half):
        steps += [(-k, 0), (k, 0), (-k, 1), (k, 1)]
    steps += [(half, 0), (half, 1)]

    payload = call(
        prep_body,
        jax.ShapeDtypeStruct((rows + META_ROWS, width), BF16),
        (single, *(v.reshape(1, tokens) for v in (chain, residue, valid))),
        in_specs=[ANY] * 4,
        scratch=[
            pltpu.VMEM(single.shape, BF16),
            pltpu.VMEM((3, 1, tokens), jnp.int32),
            pltpu.SemaphoreType.DMA((4,)),
        ],
        flops=rows * width * 16,
        moved=4 * rows * width,
        limit=FULL,
    )
    cw = ring(payload, 1)
    ccw = ring(payload, -1)

    def kv(parts):
        n = len(parts)
        return call(
            kv_body,
            jax.ShapeDtypeStruct((n * (2 * rows + META_ROWS), width), BF16),
            (*parts, w_key, w_value),
            flops=4 * n * rows * width * width,
            moved=4 * width * width + 6 * n * rows * width,
        )

    def piece(value, at, meta):
        count = rows // 2 + (META_ROWS if meta else 0)

        def body(in_ref, out_ref):
            out_ref[pl.ds(0, rows // 2), :] = in_ref[pl.ds(at, rows // 2), :]
            if meta:
                out_ref[pl.ds(rows // 2, META_ROWS), :] = in_ref[pl.ds(rows, META_ROWS), :]

        shape = jax.ShapeDtypeStruct((count, width), BF16)
        return call(body, shape, (value,), moved=2 * rows * width)

    early = len(steps) - 3 * CORES
    split = 2 * (half - 1)
    pair_shapes = tuple(
        jax.ShapeDtypeStruct((heads, tokens, n * tokens), F32) for n in (early, len(steps) - early)
    )
    weight = pltpu.VMEM((width, width), BF16)
    query, gate, kv_own, pair_first, pair_second = call(
        functools.partial(own_body, steps, chips, early),
        (
            jax.ShapeDtypeStruct((rows, width), BF16),
            jax.ShapeDtypeStruct((rows, width), F32),
            jax.ShapeDtypeStruct((2 * rows + META_ROWS, width), BF16),
            *pair_shapes,
        ),
        (me, payload, w_query, w_key, w_value, w_gate, pair, w_pair.T),
        in_specs=[SMEM] + [ANY] * 7,
        flops=8 * rows * width * width + 2 * pair.size * heads,
        moved=8 * width * width + 12 * rows * width + 2 * pair.size,
        limit=FULL,
        scratch=[
            pltpu.VMEM(payload.shape, BF16),
            weight,
            weight,
            weight,
            weight,
            pltpu.VMEM(pair.shape, BF16),
            pltpu.VMEM(w_pair.shape[::-1], BF16),
            pltpu.SemaphoreType.DMA((7,)),
        ],
    )

    kvs = [kv_own]
    kvs.append(flip(kvs[-1]))
    for k in range(1, half):
        if k + 1 < half:
            cw_next = ring(cw, 1)
            ccw_next = ring(ccw, -1)
        else:
            cw_next = ring(piece(cw, 0, True), 1)
            ccw_next = ring(piece(ccw, rows // 2, False), -1)
        kvs.append(kv([cw, ccw]))
        kvs.append(flip(kvs[-1]))
        cw, ccw = cw_next, ccw_next
    scale = 1.0 / math.sqrt(width // heads)
    spans = head_spans(width, width // heads)
    height = sum(h1 - h0 + 1 for h0, h1 in spans) * tokens * samples
    state = jax.ShapeDtypeStruct((samples * heads * tokens, 128), F32)
    table = rel_table.T
    pad = [pltpu.VMEM((heads, LANES), F32)]
    limit = (10 << 20) + 4 * samples * total * width
    before = call(
        functools.partial(early_body, samples, heads, scale),
        (jax.ShapeDtypeStruct((height, TILE), F32), state, state),
        (*kvs[:split], query, pair_first, table),
        flops=4 * rows * early * tokens * width,
        moved=4 * samples * early * tokens * width,
        limit=limit,
        scratch=pad,
    )
    count = samples // 2
    common = dict(flops=2 * rows * total * width, moved=samples * total * width, limit=limit)
    shared = (query, gate, *before, w_key, w_value)
    last = (len(steps) - early) * tokens
    gated, bias = call(
        functools.partial(attend_body, count, samples, heads, scale),
        (
            jax.ShapeDtypeStruct((rows // 2, width), BF16),
            jax.ShapeDtypeStruct((heads * tokens, last), F32),
        ),
        (*kvs[split:], cw, flip(cw), *shared, pair_second, table, payload),
        scratch=pad,
        **common,
    )
    return call(
        functools.partial(finish_body, count, samples, heads, scale),
        jax.ShapeDtypeStruct(single.shape, BF16),
        (*kvs[split:], ccw, flip(ccw), *shared, bias, gated, single, w_out),
        **common,
    )


def solution(mesh):
    placed = (
        P(("groups", "tok"), None, None),
        P(("groups", "tok"), None, None),
        P(("groups", "tok")),
        P(("groups", "tok")),
        P(("groups", "tok")),
        P(),
        P(),
        P(),
        P(),
        P(),
        P(),
        P(),
    )

    step = jax.shard_map(
        shards,
        mesh=mesh,
        in_specs=placed,
        out_specs=P(("groups", "tok"), None, None),
        check_vma=False,
    )
    return step
    return step
    return step
    return step
```

```python
import functools
import math

import jax
import jax.numpy as jnp
from jax import lax
from jax.experimental import pallas as pl
from jax.experimental.pallas import tpu as pltpu
from jax.sharding import PartitionSpec as P


NORM_EPS = 1e-05
MASK_PENALTY = 10000.0
F32 = jnp.float32
BF16 = jnp.bfloat16
CORES = 2
TILE = 256
LANES = 128
FULL = 60 << 20
VMEM = pl.BlockSpec(memory_space=pltpu.VMEM)
ANY = pl.BlockSpec(memory_space=pl.ANY)
SMEM = pl.BlockSpec(memory_space=pltpu.SMEM)
VMEM = pl.BlockSpec(memory_space=pltpu.VMEM)
ANY = pl.BlockSpec(memory_space=pl.ANY)
ANY = pl.BlockSpec(memory_space=pl.ANY)
SMEM = pl.BlockSpec(memory_space=pltpu.SMEM)
VMEM = pl.BlockSpec(memory_space=pltpu.VMEM)
ANY = pl.BlockSpec(memory_space=pl.ANY)
ANY = pl.BlockSpec(memory_space=pl.ANY)
ANY = pl.BlockSpec(memory_space=pl.ANY)
SMEM = pl.BlockSpec(memory_space=pltpu.SMEM)
VMEM = pl.BlockSpec(memory_space=pltpu.VMEM)
ANY = pl.BlockSpec(memory_space=pl.ANY)
ANY = pl.BlockSpec(memory_space=pl.ANY)
ANY = pl.BlockSpec(memory_space=pl.ANY)
SMEM = pl.BlockSpec(memory_space=pltpu.SMEM)
VMEM = pl.BlockSpec(memory_space=pltpu.VMEM)
ANY = pl.BlockSpec(memory_space=pl.ANY)
ANY = pl.BlockSpec(memory_space=pl.ANY)
ANY = pl.BlockSpec(memory_space=pl.ANY)
SMEM = pl.BlockSpec(memory_space=pltpu.SMEM)
VMEM = pl.BlockSpec(memory_space=pltpu.VMEM)
ANY = pl.BlockSpec(memory_space=pl.ANY)
ANY = pl.BlockSpec(memory_space=pl.ANY)
ANY = pl.BlockSpec(memory_space=pl.ANY)
SMEM = pl.BlockSpec(memory_space=pltpu.SMEM)


def normed_rows(block):
    tokens, samples, width = block.shape
    values = block.astype(F32).reshape(tokens * samples, width)
    centred = values - jnp.mean(values, axis=-1, keepdims=True)
    spread = jnp.mean(centred * centred, axis=-1, keepdims=True)
    return (centred * lax.rsqrt(spread + NORM_EPS)).astype(BF16)


def sample_major(tokens, samples):
    rows = tokens * samples
    to = lax.broadcasted_iota(jnp.int32, (rows, rows), 0)
    frm = lax.broadcasted_iota(jnp.int32, (rows, rows), 1)
    want = (to % tokens) * samples + to // tokens
    return (want == frm).astype(F32).astype(BF16)


def token_major(tokens, samples):
    rows = tokens * samples
    to = lax.broadcasted_iota(jnp.int32, (rows, rows), 0)
    frm = lax.broadcasted_iota(jnp.int32, (rows, rows), 1)
    want = (to % samples) * tokens + to // samples
    return (want == frm).astype(F32).astype(BF16)


def matmul(a, b):
    return jnp.dot(a, b, preferred_element_type=F32)


META_ROWS = 8
RADIX = 128


def prep_body(single_ref, chain_ref, residue_ref, valid_ref, out_ref):
    tokens, samples, width = single_ref.shape
    rows = tokens * samples
    normed = normed_rows(single_ref[...])
    out_ref[pl.ds(0, rows), :] = matmul(sample_major(tokens, samples), normed).astype(BF16)
    residue = residue_ref[...]
    row = lax.broadcasted_iota(jnp.int32, (META_ROWS, tokens), 0)
    meta = jnp.where(row == 0, chain_ref[...], 0)
    meta = jnp.where(row == 1, residue // RADIX, meta)
    meta = jnp.where(row == 2, residue % RADIX, meta)
    meta = jnp.where(row == 3, valid_ref[...], meta)
    token = lax.broadcasted_iota(jnp.int32, (tokens, width), 0)
    lane = lax.broadcasted_iota(jnp.int32, (tokens, width), 1)
    spread = (lane % tokens == token).astype(F32).astype(BF16)
    tiled = matmul(meta.astype(F32).astype(BF16), spread)
    out_ref[pl.ds(rows, META_ROWS), :] = tiled.astype(BF16)


META_ROWS = 8
RADIX = 128


def prep_body(single_ref, chain_ref, residue_ref, valid_ref, out_ref):
    tokens, samples, width = single_ref.shape
    rows = tokens * samples
    normed = normed_rows(single_ref[...])
    out_ref[pl.ds(0, rows), :] = matmul(sample_major(tokens, samples), normed).astype(BF16)
    residue = residue_ref[...]
    row = lax.broadcasted_iota(jnp.int32, (META_ROWS, tokens), 0)
    meta = jnp.where(row == 0, chain_ref[...], 0)
    meta = jnp.where(row == 1, residue // RADIX, meta)
    meta = jnp.where(row == 2, residue % RADIX, meta)
    meta = jnp.where(row == 3, valid_ref[...], meta)
    token = lax.broadcasted_iota(jnp.int32, (tokens, width), 0)
    lane = lax.broadcasted_iota(jnp.int32, (tokens, width), 1)
    spread = (lane % tokens == token).astype(F32).astype(BF16)
    tiled = matmul(meta.astype(F32).astype(BF16), spread)
    out_ref[pl.ds(rows, META_ROWS), :] = tiled.astype(BF16)


META_ROWS = 8
RADIX = 128


def prep_body(single_ref, chain_ref, residue_ref, valid_ref, out_ref):
    tokens, samples, width = single_ref.shape
    rows = tokens * samples
    normed = normed_rows(single_ref[...])
    out_ref[pl.ds(0, rows), :] = matmul(sample_major(tokens, samples), normed).astype(BF16)
    residue = residue_ref[...]
    row = lax.broadcasted_iota(jnp.int32, (META_ROWS, tokens), 0)
    meta = jnp.where(row == 0, chain_ref[...], 0)
    meta = jnp.where(row == 1, residue // RADIX, meta)
    meta = jnp.where(row == 2, residue % RADIX, meta)
    meta = jnp.where(row == 3, valid_ref[...], meta)
    token = lax.broadcasted_iota(jnp.int32, (tokens, width), 0)
    lane = lax.broadcasted_iota(jnp.int32, (tokens, width), 1)
    spread = (lane % tokens == token).astype(F32).astype(BF16)
    tiled = matmul(meta.astype(F32).astype(BF16), spread)
    out_ref[pl.ds(rows, META_ROWS), :] = tiled.astype(BF16)


META_ROWS = 8
RADIX = 128


def prep_body(single_hbm, chain_hbm, residue_hbm, valid_hbm, out_ref, single_ref, ints_ref, sems):
    copies = [pltpu.make_async_copy(single_hbm, single_ref, sems.at[0])]
    for i, ref in enumerate((chain_hbm, residue_hbm, valid_hbm)):
        copies.append(pltpu.make_async_copy(ref, ints_ref.at[i], sems.at[i + 1]))
    for copy in copies:
        copy.start()
    tokens, samples, width = single_ref.shape
    rows = tokens * samples
    token = lax.broadcasted_iota(jnp.int32, (tokens, width), 0)
    lane = lax.broadcasted_iota(jnp.int32, (tokens, width), 1)
    spread = (lane % tokens == token).astype(F32).astype(BF16)
    perm = sample_major(tokens, samples)
    for copy in copies:
        copy.wait()
    normed = normed_rows(single_ref[...])
    out_ref[pl.ds(0, rows), :] = matmul(perm, normed).astype(BF16)
    residue = ints_ref[1]
    row = lax.broadcasted_iota(jnp.int32, (META_ROWS, tokens), 0)
    meta = jnp.where(row == 0, ints_ref[0], 0)
    meta = jnp.where(row == 1, residue // RADIX, meta)
    meta = jnp.where(row == 2, residue % RADIX, meta)
    meta = jnp.where(row == 3, ints_ref[2], meta)
    tiled = matmul(meta.astype(F32).astype(BF16), spread)
    out_ref[pl.ds(rows, META_ROWS), :] = tiled.astype(BF16)


META_ROWS = 8
RADIX = 128


def prep_body(single_hbm, chain_hbm, residue_hbm, valid_hbm, out_ref, meta_ref, single_ref, ints_ref, sems):
    copies = [pltpu.make_async_copy(single_hbm, single_ref, sems.at[0])]
    for i, ref in enumerate((chain_hbm, residue_hbm, valid_hbm)):
        copies.append(pltpu.make_async_copy(ref, ints_ref.at[i], sems.at[i + 1]))
    for copy in copies:
        copy.start()
    tokens, samples, width = single_ref.shape
    rows = tokens * samples
    token = lax.broadcasted_iota(jnp.int32, (tokens, width), 0)
    lane = lax.broadcasted_iota(jnp.int32, (tokens, width), 1)
    spread = (lane % tokens == token).astype(F32).astype(BF16)
    perm = sample_major(tokens, samples)
    for copy in copies:
        copy.wait()
    normed = normed_rows(single_ref[...])
    out_ref[pl.ds(0, rows), :] = matmul(perm, normed).astype(BF16)
    residue = ints_ref[1]
    row = lax.broadcasted_iota(jnp.int32, (META_ROWS, tokens), 0)
    meta = jnp.where(row == 0, ints_ref[0], 0)
    meta = jnp.where(row == 1, residue // RADIX, meta)
    meta = jnp.where(row == 2, residue % RADIX, meta)
    meta = jnp.where(row == 3, ints_ref[2], meta)
    tiled = matmul(meta.astype(F32).astype(BF16), spread)
    out_ref[pl.ds(rows, META_ROWS), :] = tiled.astype(BF16)
    meta_ref[...] = tiled.astype(BF16)


META_ROWS = 8
RADIX = 128


def prep_body(single_hbm, chain_hbm, residue_hbm, valid_hbm, out_ref, single_ref, ints_ref, sems):
    copies = [pltpu.make_async_copy(single_hbm, single_ref, sems.at[0])]
    for i, ref in enumerate((chain_hbm, residue_hbm, valid_hbm)):
        copies.append(pltpu.make_async_copy(ref, ints_ref.at[i], sems.at[i + 1]))
    for copy in copies:
        copy.start()
    tokens, samples, width = single_ref.shape
    rows = tokens * samples
    token = lax.broadcasted_iota(jnp.int32, (tokens, width), 0)
    lane = lax.broadcasted_iota(jnp.int32, (tokens, width), 1)
    spread = (lane % tokens == token).astype(F32).astype(BF16)
    perm = sample_major(tokens, samples)
    for copy in copies:
        copy.wait()
    normed = normed_rows(single_ref[...])
    out_ref[pl.ds(0, rows), :] = matmul(perm, normed).astype(BF16)
    residue = ints_ref[1]
    row = lax.broadcasted_iota(jnp.int32, (META_ROWS, tokens), 0)
    meta = jnp.where(row == 0, ints_ref[0], 0)
    meta = jnp.where(row == 1, residue // RADIX, meta)
    meta = jnp.where(row == 2, residue % RADIX, meta)
    meta = jnp.where(row == 3, ints_ref[2], meta)
    tiled = matmul(meta.astype(F32).astype(BF16), spread)
    out_ref[pl.ds(rows, META_ROWS), :] = tiled.astype(BF16)


def own_body(
    steps, chips, me_ref, pay_hbm, wq_hbm, wk_hbm, wv_hbm, wg_hbm, pair_hbm, wp_hbm,
    q_ref, gate_ref, kv_ref, first_ref, second_ref,
    pay_ref, wq_ref, wk_ref, wv_ref, wg_ref, pair_ref, wp_ref, sems,
):
    copies = {}
    moves = [
        (pay_hbm, pay_ref), (wq_hbm, wq_ref), (wp_hbm, wp_ref), (pair_hbm, pair_ref),
        (wk_hbm, wk_ref), (wv_hbm, wv_ref), (wg_hbm, wg_ref),
    ]
    for i, (source, target) in enumerate(moves):
        copies[i] = pltpu.make_async_copy(source, target, sems.at[i])
        copies[i].start()
    rows = q_ref.shape[0]
    copies[0].wait()
    data = pay_ref[pl.ds(0, rows), :]
    copies[1].wait()
    q_ref[...] = matmul(data, wq_ref[...]).astype(BF16)
    copies[2].wait()
    copies[3].wait()
    pair_rows(steps, chips, me_ref[0], pair_ref, wp_ref[...], (first_ref, second_ref))
    copies[4].wait()
    kv_ref[pl.ds(0, rows), :] = matmul(data, wk_ref[...]).astype(BF16)
    copies[5].wait()
    kv_ref[pl.ds(rows, rows), :] = matmul(data, wv_ref[...]).astype(BF16)
    kv_ref[pl.ds(2 * rows, META_ROWS), :] = pay_ref[pl.ds(rows, META_ROWS), :]
    copies[6].wait()
    gate_ref[...] = jax.nn.sigmoid(matmul(data, wg_ref[...]))


def kv_body(*refs):
    wk_ref, wv_ref, out_ref = refs[-3:]
    blocks = refs[:-3]
    n = len(blocks)
    rows = blocks[0].shape[0] - META_ROWS
    parts = [b[pl.ds(0, rows), :] for b in blocks]
    data = jnp.concatenate(parts, axis=0) if n > 1 else parts[0]
    out_ref[pl.ds(0, n * rows), :] = matmul(data, wk_ref[...]).astype(BF16)
    out_ref[pl.ds(n * rows, n * rows), :] = matmul(data, wv_ref[...]).astype(BF16)
    for i, b in enumerate(blocks):
        out_ref[pl.ds(2 * n * rows + i * META_ROWS, META_ROWS), :] = b[pl.ds(rows, META_ROWS), :]


def ring_chip(place, chips):
    place = lax.rem(place + 2 * chips, chips)
    return jnp.where(place < chips // 2, 2 * place, 2 * (chips - 1 - place) + 1)


def pair_rows(steps, chips, me, pair_ref, weights, out_refs):
    queries, total, channels = pair_ref.shape
    heads = weights.shape[0]
    tokens = total // len(steps)
    chip = me // CORES
    core = lax.rem(me, CORES)
    place = jnp.where(lax.rem(chip, 2) == 0, chip // 2, chips - 1 - chip // 2)
    lines = heads * queries
    head = lax.broadcasted_iota(jnp.int32, (heads, lines), 0)
    lane = lax.broadcasted_iota(jnp.int32, (heads, lines), 1)
    spread = (lane // queries == head).astype(F32).astype(BF16)
    wide = lax.dot_general(weights, spread, (((0,), (0,)), ((), ())), preferred_element_type=F32)
    lane = lax.broadcasted_iota(jnp.int32, (channels, lines), 1) % queries
    wide = jnp.concatenate(
        [jnp.where(lane == i, wide, 0.0).astype(BF16) for i in range(queries)], axis=0
    )
    at = 0
    for out_ref in out_refs:
        data = []
        for r, c in steps[at : at + out_ref.shape[0] // tokens]:
            block = ring_chip(place + r, chips) * CORES + lax.rem(core + c, CORES)
            start = pl.multiple_of(block * tokens, tokens)
            rows = [pair_ref[i, pl.ds(start, tokens), :] for i in range(queries)]
            data.append(jnp.concatenate(rows, axis=1))
        at += len(data)
        out_ref[...] = matmul(jnp.concatenate(data, axis=0), wide)


def kv_count(ref, rows):
    return ref.shape[0] // (2 * rows + META_ROWS)


def kv_metas(kv_refs, rows):
    found = []
    for r in kv_refs:
        n = kv_count(r, rows)
        found += [r[pl.ds(2 * n * rows + u * META_ROWS, META_ROWS), :] for u in range(n)]
    return found


def full_bias(own, metas, tokens, pair_ref, tab_ref, pad_ref):
    total = pair_ref.shape[0]
    heads, bins = tab_ref.shape
    reach = (bins - 2) // 2
    wide = -(-total // LANES) * LANES
    slot = lax.broadcasted_iota(jnp.int32, (META_ROWS, wide), 1) // tokens
    keys = jnp.zeros((META_ROWS, wide), F32)
    for u, row in enumerate(metas):
        row = row.astype(F32)
        row = jnp.concatenate([row] * (-(-wide // row.shape[1])), axis=1)[:, :wide]
        keys = jnp.where(slot == u, row, keys)
    here = own.astype(F32)[:, :LANES]
    lane = lax.broadcasted_iota(jnp.int32, (tokens, LANES), 1)
    row = lax.broadcasted_iota(jnp.int32, (tokens, LANES), 0)

    def column(values):
        values = jnp.where(lane == row, jnp.broadcast_to(values, (tokens, LANES)), 0.0)
        return jnp.sum(values, axis=-1, keepdims=True)

    chain_q = column(here[0:1, :])
    res_q = column(here[1:2, :] * RADIX + here[2:3, :])
    res_keys = keys[1:2, :] * RADIX + keys[2:3, :]
    offset = jnp.clip(res_q - res_keys, -reach, reach) + reach
    bucket = jnp.where(chain_q == keys[0:1, :], offset, float(bins - 1)).astype(jnp.int32)
    mask = (keys[3:4, :] - 1.0) * MASK_PENALTY
    pad_ref[...] = jnp.zeros_like(pad_ref)
    pad_ref[:, pl.ds(0, bins)] = tab_ref[...]
    out = []
    for h in range(heads):
        table = jnp.broadcast_to(pad_ref[h : h + 1, :], (tokens, LANES))
        rel = [
            jnp.take_along_axis(
                table, bucket[:, at : at + LANES], axis=1, mode="promise_in_bounds"
            )
            for at in range(0, wide, LANES)
        ]
        out.append((jnp.concatenate(rel, axis=1) if len(rel) > 1 else rel[0]) + mask)
    return pair_ref[...] + jnp.transpose(jnp.concatenate(out, axis=0))[:total]


def head_windows(width, hs):
    windows, h = [], 0
    while h * hs < width:
        start = min(h * hs // LANES * LANES, width - TILE)
        last = min((start + TILE) // hs, width // hs) - 1
        windows.append((h, last, start))
        h = last + 1
    return windows


def spread_body(samples, heads, q_ref, out_ref):
    rows, width = q_ref.shape
    tokens = rows // samples
    hs = width // heads
    lines = heads * tokens
    token = lax.broadcasted_iota(jnp.int32, (tokens, lines), 0)
    lane = lax.broadcasted_iota(jnp.int32, (tokens, lines), 1)
    spread = (lane % tokens == token).astype(F32).astype(BF16)
    feature = lax.broadcasted_iota(jnp.int32, (width, lines), 0)
    lane = lax.broadcasted_iota(jnp.int32, (width, lines), 1)
    inside = feature // hs == lane // tokens
    for s in range(samples):
        wide = lax.dot_general(
            q_ref[pl.ds(s * tokens, tokens), :], spread, (((0,), (0,)), ((), ())),
            preferred_element_type=F32,
        )
        out_ref[pl.ds(s * width, width), :] = jnp.where(inside, wide, 0.0).astype(BF16)


def gather(kv_refs, rows, at, tokens, values):
    found = []
    for r in kv_refs:
        n = kv_count(r, rows)
        first = n if values else 0
        found += [r[pl.ds((first + u) * rows + at, tokens), :] for u in range(n)]
    return found


def early_body(samples, scale, *refs):
    q_ref, pair_ref, tab_ref, exp_ref, top_ref, mass_ref, pad_ref = refs[-7:]
    kv_refs = refs[:-7]
    count, lines = pair_ref.shape
    tokens = lines // tab_ref.shape[0]
    rows = tokens * samples
    width = kv_refs[0].shape[1]
    metas = kv_metas(kv_refs, rows)
    bias = full_bias(metas[0], metas, tokens, pair_ref, tab_ref, pad_ref)
    for s in range(samples):
        keys = jnp.concatenate(gather(kv_refs, rows, s * tokens, tokens, False), axis=0)
        scores = matmul(keys, q_ref[pl.ds(s * width, width), :]) * scale + bias
        top = jnp.max(scores, axis=0, keepdims=True)
        weights = jnp.exp(scores - top)
        top_ref[pl.ds(s, 1), :] = top
        mass_ref[pl.ds(s, 1), :] = jnp.sum(weights, axis=0, keepdims=True)
        exp_ref[pl.ds(s * count, count), :] = weights


def finish_body(heads, scale, split, *refs):
    (
        q_ref, gate_ref, exp_ref, top_ref, mass_ref, wk_ref, wv_ref, pair_ref, tab_ref, pay_ref,
        single_ref, wo_ref, out_ref, pad_ref, weight_ref,
    ) = refs[-15:]
    kv_refs, lasts = refs[:-19], refs[-19:-15]
    tokens, samples, width = single_ref.shape
    rows = tokens * samples
    half = rows // 2
    hs = width // heads
    metas = kv_metas(kv_refs[split:], rows) + [r[pl.ds(half, META_ROWS), :] for r in (lasts[0], lasts[2])]
    own = pay_ref[pl.ds(rows, META_ROWS), :]
    data = jnp.concatenate([r[pl.ds(0, half), :] for r in lasts], axis=0)
    k_last = matmul(data, wk_ref[...]).astype(BF16)
    v_last = matmul(data, wv_ref[...]).astype(BF16)
    bias = full_bias(own, metas, tokens, pair_ref, tab_ref, pad_ref)
    count = exp_ref.shape[0] // samples
    lane_head = lax.broadcasted_iota(jnp.int32, (tokens, width), 1) // hs
    lines = heads * tokens
    for s in range(samples):
        new = [slice(u * rows + s * tokens, u * rows + (s + 1) * tokens) for u in range(2)]
        keys = gather(kv_refs[split:], rows, s * tokens, tokens, False)
        keys = jnp.concatenate(keys + [k_last[n] for n in new], axis=0)
        scores = matmul(keys, q_ref[pl.ds(s * width, width), :]) * scale + bias
        before = top_ref[pl.ds(s, 1), :]
        top = jnp.maximum(jnp.max(scores, axis=0, keepdims=True), before)
        shrink = jnp.exp(before - top)
        late = jnp.exp(scores - top)
        mass = jnp.sum(late, axis=0, keepdims=True) + mass_ref[pl.ds(s, 1), :] * shrink
        inv = 1.0 / mass
        old = exp_ref[pl.ds(s * count, count), :] * (shrink * inv)
        weights = jnp.concatenate([old, late * inv], axis=0)
        weight_ref[pl.ds(s * lines, lines), :] = jnp.transpose(weights).astype(BF16)
    gated = []
    for s in range(samples):
        new = [slice(u * rows + s * tokens, u * rows + (s + 1) * tokens) for u in range(2)]
        values = gather(kv_refs, rows, s * tokens, tokens, True)
        values = jnp.concatenate(values + [v_last[n] for n in new], axis=0)
        pieces = {}
        for h0, h1, start in head_windows(width, hs):
            here = pl.ds(s * lines + h0 * tokens, (h1 + 1 - h0) * tokens)
            ot = matmul(weight_ref[here, :], values[:, start : start + TILE])
            for first in range(start, start + TILE, LANES):
                for h in range(h0, h1 + 1):
                    if (h + 1) * hs <= first or h * hs >= first + LANES:
                        continue
                    lanes = slice(first - start, first - start + LANES)
                    part = ot[(h - h0) * tokens : (h + 1 - h0) * tokens, lanes]
                    if first in pieces:
                        mine = lane_head[:, first : first + LANES] == h
                        part = jnp.where(mine, part, pieces[first])
                    pieces[first] = part
        attended = jnp.concatenate([pieces[at] for at in sorted(pieces)], axis=1)
        gated.append((gate_ref[pl.ds(s * tokens, tokens), :] * attended).astype(BF16))
    gated = matmul(token_major(tokens, samples), jnp.concatenate(gated, axis=0)).astype(BF16)
    out = matmul(gated, wo_ref[...]).reshape(tokens, samples, width)
    out_ref[...] = (single_ref[...].astype(F32) + out).astype(BF16)


def call(body, out_shape, args, in_specs=None, flops=0, moved=0, limit=8 << 20, scratch=()):
    return pl.pallas_call(
        body,
        out_shape=out_shape,
        in_specs=in_specs or [VMEM] * len(args),
        out_specs=jax.tree.map(lambda _: VMEM, out_shape),
        scratch_shapes=scratch,
        compiler_params=pltpu.CompilerParams(vmem_limit_bytes=limit),
        cost_estimate=pl.CostEstimate(flops=flops, bytes_accessed=moved, transcendentals=0),
    )(*args)


def shards(
    single, pair, chain, residue, valid, w_query, w_key, w_value, w_gate, w_out, w_pair, rel_table
):
    tokens, samples, width = single.shape
    heads = w_pair.shape[1]
    total = pair.shape[1]
    rows = tokens * samples
    devices = lax.axis_size("tok")
    chips = devices // CORES
    half = chips // 2
    order = list(range(0, chips, 2)) + list(range(1, chips, 2))[::-1]
    me = lax.axis_index("tok").astype(jnp.int32).reshape(1)

    def ring(value, step):
        pairs = [
            (order[i] * CORES + c, order[(i + step) % chips] * CORES + c)
            for i in range(chips)
            for c in range(CORES)
        ]
        return lax.ppermute(value, "tok", pairs)

    def flip(value):
        return lax.ppermute(value, "tok", [(d, d ^ 1) for d in range(devices)])

    steps = [(0, 0), (0, 1)]
    for k in range(1, half):
        steps += [(-k, 0), (k, 0), (-k, 1), (k, 1)]
    steps += [(half, 0), (half, 1)]

    payload = call(
        prep_body,
        jax.ShapeDtypeStruct((rows + META_ROWS, width), BF16),
        (single, *(v.reshape(1, tokens) for v in (chain, residue, valid))),
        in_specs=[ANY] * 4,
        scratch=[
            pltpu.VMEM(single.shape, BF16),
            pltpu.VMEM((3, 1, tokens), jnp.int32),
            pltpu.SemaphoreType.DMA((4,)),
        ],
        flops=rows * width * 16,
        moved=4 * rows * width,
        limit=FULL,
    )
    cw = ring(payload, 1)
    ccw = ring(payload, -1)

    def kv(parts):
        n = len(parts)
        return call(
            kv_body,
            jax.ShapeDtypeStruct((n * (2 * rows + META_ROWS), width), BF16),
            (*parts, w_key, w_value),
            flops=4 * n * rows * width * width,
            moved=4 * width * width + 6 * n * rows * width,
        )

    def piece(value, at, meta):
        count = rows // 2 + (META_ROWS if meta else 0)

        def body(in_ref, out_ref):
            out_ref[pl.ds(0, rows // 2), :] = in_ref[pl.ds(at, rows // 2), :]
            if meta:
                out_ref[pl.ds(rows // 2, META_ROWS), :] = in_ref[pl.ds(rows, META_ROWS), :]

        shape = jax.ShapeDtypeStruct((count, width), BF16)
        return call(body, shape, (value,), moved=2 * rows * width)

    early = len(steps) - 3 * CORES
    split = 2 * (half - 1)
    pair_shapes = tuple(
        jax.ShapeDtypeStruct((n * tokens, heads * tokens), F32) for n in (early, len(steps) - early)
    )
    weight = pltpu.VMEM((width, width), BF16)
    query, gate, kv_own, pair_first, pair_second = call(
        functools.partial(own_body, steps, chips),
        (
            jax.ShapeDtypeStruct((rows, width), BF16),
            jax.ShapeDtypeStruct((rows, width), F32),
            jax.ShapeDtypeStruct((2 * rows + META_ROWS, width), BF16),
            *pair_shapes,
        ),
        (me, payload, w_query, w_key, w_value, w_gate, pair, w_pair.T),
        in_specs=[SMEM] + [ANY] * 7,
        flops=8 * rows * width * width + 2 * pair.size * heads,
        moved=8 * width * width + 12 * rows * width + 2 * pair.size,
        limit=FULL,
        scratch=[
            pltpu.VMEM(payload.shape, BF16),
            weight,
            weight,
            weight,
            weight,
            pltpu.VMEM(pair.shape, BF16),
            pltpu.VMEM(w_pair.shape[::-1], BF16),
            pltpu.SemaphoreType.DMA((7,)),
        ],
    )

    kvs = [kv_own]
    kvs.append(flip(kvs[-1]))
    for k in range(1, half):
        if k + 1 < half:
            cw_next = ring(cw, 1)
            ccw_next = ring(ccw, -1)
        else:
            cw_next = ring(piece(cw, 0, True), 1)
            ccw_next = ring(piece(ccw, rows // 2, False), -1)
        kvs.append(kv([cw, ccw]))
        kvs.append(flip(kvs[-1]))
        cw, ccw = cw_next, ccw_next
    scale = 1.0 / math.sqrt(width // heads)
    lines = heads * tokens
    state = jax.ShapeDtypeStruct((samples, lines), F32)
    query = call(
        functools.partial(spread_body, samples, heads),
        jax.ShapeDtypeStruct((samples * width, lines), BF16),
        (query,),
        flops=2 * rows * width * lines,
        moved=2 * samples * width * lines,
    )
    table = rel_table.T
    pad = [pltpu.VMEM((heads, LANES), F32)]
    limit = (10 << 20) + 4 * samples * total * width
    before = call(
        functools.partial(early_body, samples, scale),
        (jax.ShapeDtypeStruct((samples * early * tokens, lines), F32), state, state),
        (*kvs[:split], query, pair_first, table),
        flops=4 * rows * early * tokens * width,
        moved=4 * samples * early * tokens * width,
        limit=limit,
        scratch=pad,
    )
    cw_other, ccw_other = flip(cw), flip(ccw)
    return call(
        functools.partial(finish_body, heads, scale, split),
        jax.ShapeDtypeStruct(single.shape, BF16),
        (
            *kvs, cw, ccw, cw_other, ccw_other, query, gate, *before, w_key, w_value,
            pair_second, table, payload, single, w_out,
        ),
        flops=4 * rows * total * width,
        moved=2 * samples * total * width,
        limit=limit,
        scratch=[*pad, pltpu.VMEM((samples * lines, total), BF16)],
    )


def solution(mesh):
    placed = (
        P(("groups", "tok"), None, None),
        P(("groups", "tok"), None, None),
        P(("groups", "tok")),
        P(("groups", "tok")),
        P(("groups", "tok")),
        P(),
        P(),
        P(),
        P(),
        P(),
        P(),
        P(),
    )

    step = jax.shard_map(
        shards,
        mesh=mesh,
        in_specs=placed,
        out_specs=P(("groups", "tok"), None, None),
        check_vma=False,
    )
    return step
    return step
    return step
    return step
```

```python
import functools
import math

import jax
import jax.numpy as jnp
from jax import lax
from jax.experimental import pallas as pl
from jax.experimental.pallas import tpu as pltpu
from jax.sharding import PartitionSpec as P


NORM_EPS = 1e-05
MASK_PENALTY = 10000.0
F32 = jnp.float32
BF16 = jnp.bfloat16
CORES = 2
TILE = 256
LANES = 128
FULL = 60 << 20
VMEM = pl.BlockSpec(memory_space=pltpu.VMEM)
ANY = pl.BlockSpec(memory_space=pl.ANY)
SMEM = pl.BlockSpec(memory_space=pltpu.SMEM)
VMEM = pl.BlockSpec(memory_space=pltpu.VMEM)
ANY = pl.BlockSpec(memory_space=pl.ANY)
ANY = pl.BlockSpec(memory_space=pl.ANY)
SMEM = pl.BlockSpec(memory_space=pltpu.SMEM)
VMEM = pl.BlockSpec(memory_space=pltpu.VMEM)
ANY = pl.BlockSpec(memory_space=pl.ANY)
ANY = pl.BlockSpec(memory_space=pl.ANY)
ANY = pl.BlockSpec(memory_space=pl.ANY)
SMEM = pl.BlockSpec(memory_space=pltpu.SMEM)
VMEM = pl.BlockSpec(memory_space=pltpu.VMEM)
ANY = pl.BlockSpec(memory_space=pl.ANY)
ANY = pl.BlockSpec(memory_space=pl.ANY)
ANY = pl.BlockSpec(memory_space=pl.ANY)
SMEM = pl.BlockSpec(memory_space=pltpu.SMEM)
VMEM = pl.BlockSpec(memory_space=pltpu.VMEM)
ANY = pl.BlockSpec(memory_space=pl.ANY)
ANY = pl.BlockSpec(memory_space=pl.ANY)
ANY = pl.BlockSpec(memory_space=pl.ANY)
SMEM = pl.BlockSpec(memory_space=pltpu.SMEM)
VMEM = pl.BlockSpec(memory_space=pltpu.VMEM)
ANY = pl.BlockSpec(memory_space=pl.ANY)
ANY = pl.BlockSpec(memory_space=pl.ANY)
ANY = pl.BlockSpec(memory_space=pl.ANY)
SMEM = pl.BlockSpec(memory_space=pltpu.SMEM)


def normed_rows(block):
    tokens, samples, width = block.shape
    values = block.astype(F32).reshape(tokens * samples, width)
    centred = values - jnp.mean(values, axis=-1, keepdims=True)
    spread = jnp.mean(centred * centred, axis=-1, keepdims=True)
    return (centred * lax.rsqrt(spread + NORM_EPS)).astype(BF16)


def sample_major(tokens, samples):
    rows = tokens * samples
    to = lax.broadcasted_iota(jnp.int32, (rows, rows), 0)
    frm = lax.broadcasted_iota(jnp.int32, (rows, rows), 1)
    want = (to % tokens) * samples + to // tokens
    return (want == frm).astype(F32).astype(BF16)


def token_major(tokens, samples):
    rows = tokens * samples
    to = lax.broadcasted_iota(jnp.int32, (rows, rows), 0)
    frm = lax.broadcasted_iota(jnp.int32, (rows, rows), 1)
    want = (to % samples) * tokens + to // samples
    return (want == frm).astype(F32).astype(BF16)


def matmul(a, b):
    return jnp.dot(a, b, preferred_element_type=F32)


META_ROWS = 8
RADIX = 128


def prep_body(single_ref, chain_ref, residue_ref, valid_ref, out_ref):
    tokens, samples, width = single_ref.shape
    rows = tokens * samples
    normed = normed_rows(single_ref[...])
    out_ref[pl.ds(0, rows), :] = matmul(sample_major(tokens, samples), normed).astype(BF16)
    residue = residue_ref[...]
    row = lax.broadcasted_iota(jnp.int32, (META_ROWS, tokens), 0)
    meta = jnp.where(row == 0, chain_ref[...], 0)
    meta = jnp.where(row == 1, residue // RADIX, meta)
    meta = jnp.where(row == 2, residue % RADIX, meta)
    meta = jnp.where(row == 3, valid_ref[...], meta)
    token = lax.broadcasted_iota(jnp.int32, (tokens, width), 0)
    lane = lax.broadcasted_iota(jnp.int32, (tokens, width), 1)
    spread = (lane % tokens == token).astype(F32).astype(BF16)
    tiled = matmul(meta.astype(F32).astype(BF16), spread)
    out_ref[pl.ds(rows, META_ROWS), :] = tiled.astype(BF16)
    meta_ref[...] = tiled.astype(BF16)


def join_body(single_ref, meta_ref, out_ref):
    tokens, samples, _ = single_ref.shape
    rows = tokens * samples
    normed = normed_rows(single_ref[...])
    out_ref[pl.ds(0, rows), :] = matmul(sample_major(tokens, samples), normed).astype(BF16)
    out_ref[pl.ds(rows, META_ROWS), :] = meta_ref[...]


META_ROWS = 8
RADIX = 128


def prep_body(single_ref, chain_ref, residue_ref, valid_ref, out_ref):
    tokens, samples, width = single_ref.shape
    rows = tokens * samples
    normed = normed_rows(single_ref[...])
    out_ref[pl.ds(0, rows), :] = matmul(sample_major(tokens, samples), normed).astype(BF16)
    residue = residue_ref[...]
    row = lax.broadcasted_iota(jnp.int32, (META_ROWS, tokens), 0)
    meta = jnp.where(row == 0, chain_ref[...], 0)
    meta = jnp.where(row == 1, residue // RADIX, meta)
    meta = jnp.where(row == 2, residue % RADIX, meta)
    meta = jnp.where(row == 3, valid_ref[...], meta)
    token = lax.broadcasted_iota(jnp.int32, (tokens, width), 0)
    lane = lax.broadcasted_iota(jnp.int32, (tokens, width), 1)
    spread = (lane % tokens == token).astype(F32).astype(BF16)
    tiled = matmul(meta.astype(F32).astype(BF16), spread)
    out_ref[pl.ds(rows, META_ROWS), :] = tiled.astype(BF16)
    meta_ref[...] = tiled.astype(BF16)


def join_body(single_ref, meta_ref, out_ref):
    tokens, samples, _ = single_ref.shape
    rows = tokens * samples
    normed = normed_rows(single_ref[...])
    out_ref[pl.ds(0, rows), :] = matmul(sample_major(tokens, samples), normed).astype(BF16)
    out_ref[pl.ds(rows, META_ROWS), :] = meta_ref[...]


META_ROWS = 8
RADIX = 128


def prep_body(single_ref, chain_ref, residue_ref, valid_ref, out_ref):
    tokens, samples, width = single_ref.shape
    rows = tokens * samples
    normed = normed_rows(single_ref[...])
    out_ref[pl.ds(0, rows), :] = matmul(sample_major(tokens, samples), normed).astype(BF16)
    residue = residue_ref[...]
    row = lax.broadcasted_iota(jnp.int32, (META_ROWS, tokens), 0)
    meta = jnp.where(row == 0, chain_ref[...], 0)
    meta = jnp.where(row == 1, residue // RADIX, meta)
    meta = jnp.where(row == 2, residue % RADIX, meta)
    meta = jnp.where(row == 3, valid_ref[...], meta)
    token = lax.broadcasted_iota(jnp.int32, (tokens, width), 0)
    lane = lax.broadcasted_iota(jnp.int32, (tokens, width), 1)
    spread = (lane % tokens == token).astype(F32).astype(BF16)
    tiled = matmul(meta.astype(F32).astype(BF16), spread)
    out_ref[pl.ds(rows, META_ROWS), :] = tiled.astype(BF16)
    meta_ref[...] = tiled.astype(BF16)


def join_body(single_ref, meta_ref, out_ref):
    tokens, samples, _ = single_ref.shape
    rows = tokens * samples
    normed = normed_rows(single_ref[...])
    out_ref[pl.ds(0, rows), :] = matmul(sample_major(tokens, samples), normed).astype(BF16)
    out_ref[pl.ds(rows, META_ROWS), :] = meta_ref[...]


META_ROWS = 8
RADIX = 128


def prep_body(
    single_hbm, chain_hbm, residue_hbm, valid_hbm, out_ref, meta_ref, single_ref, ints_ref, sems
):
    copies = [pltpu.make_async_copy(single_hbm, single_ref, sems.at[0])]
    for i, ref in enumerate((chain_hbm, residue_hbm, valid_hbm)):
        copies.append(pltpu.make_async_copy(ref, ints_ref.at[i], sems.at[i + 1]))
    for copy in copies:
        copy.start()
    tokens, samples, width = single_ref.shape
    rows = tokens * samples
    token = lax.broadcasted_iota(jnp.int32, (tokens, width), 0)
    lane = lax.broadcasted_iota(jnp.int32, (tokens, width), 1)
    spread = (lane % tokens == token).astype(F32).astype(BF16)
    perm = sample_major(tokens, samples)
    for copy in copies:
        copy.wait()
    normed = normed_rows(single_ref[...])
    out_ref[pl.ds(0, rows), :] = matmul(perm, normed).astype(BF16)
    residue = ints_ref[1]
    row = lax.broadcasted_iota(jnp.int32, (META_ROWS, tokens), 0)
    meta = jnp.where(row == 0, ints_ref[0], 0)
    meta = jnp.where(row == 1, residue // RADIX, meta)
    meta = jnp.where(row == 2, residue % RADIX, meta)
    meta = jnp.where(row == 3, ints_ref[2], meta)
    tiled = matmul(meta.astype(F32).astype(BF16), spread)
    out_ref[pl.ds(rows, META_ROWS), :] = tiled.astype(BF16)
    meta_ref[...] = tiled.astype(BF16)


def join_body(single_ref, meta_ref, out_ref):
    tokens, samples, _ = single_ref.shape
    rows = tokens * samples
    normed = normed_rows(single_ref[...])
    out_ref[pl.ds(0, rows), :] = matmul(sample_major(tokens, samples), normed).astype(BF16)
    out_ref[pl.ds(rows, META_ROWS), :] = meta_ref[...]


META_ROWS = 8
RADIX = 128


def prep_body(single_hbm, chain_hbm, residue_hbm, valid_hbm, out_ref, meta_ref, single_ref, ints_ref, sems):
    copies = [pltpu.make_async_copy(single_hbm, single_ref, sems.at[0])]
    for i, ref in enumerate((chain_hbm, residue_hbm, valid_hbm)):
        copies.append(pltpu.make_async_copy(ref, ints_ref.at[i], sems.at[i + 1]))
    for copy in copies:
        copy.start()
    tokens, samples, width = single_ref.shape
    rows = tokens * samples
    token = lax.broadcasted_iota(jnp.int32, (tokens, width), 0)
    lane = lax.broadcasted_iota(jnp.int32, (tokens, width), 1)
    spread = (lane % tokens == token).astype(F32).astype(BF16)
    perm = sample_major(tokens, samples)
    for copy in copies:
        copy.wait()
    normed = normed_rows(single_ref[...])
    out_ref[pl.ds(0, rows), :] = matmul(perm, normed).astype(BF16)
    residue = ints_ref[1]
    row = lax.broadcasted_iota(jnp.int32, (META_ROWS, tokens), 0)
    meta = jnp.where(row == 0, ints_ref[0], 0)
    meta = jnp.where(row == 1, residue // RADIX, meta)
    meta = jnp.where(row == 2, residue % RADIX, meta)
    meta = jnp.where(row == 3, ints_ref[2], meta)
    tiled = matmul(meta.astype(F32).astype(BF16), spread)
    out_ref[pl.ds(rows, META_ROWS), :] = tiled.astype(BF16)
    meta_ref[...] = tiled.astype(BF16)


def join_body(single_ref, meta_ref, out_ref):
    tokens, samples, _ = single_ref.shape
    rows = tokens * samples
    normed = normed_rows(single_ref[...])
    out_ref[pl.ds(0, rows), :] = matmul(sample_major(tokens, samples), normed).astype(BF16)
    out_ref[pl.ds(rows, META_ROWS), :] = meta_ref[...]
    meta_ref[...] = tiled.astype(BF16)


META_ROWS = 8
RADIX = 128


def prep_body(
    single_hbm, chain_hbm, residue_hbm, valid_hbm, out_ref, meta_ref, single_ref, ints_ref, sems
):
    copies = [pltpu.make_async_copy(single_hbm, single_ref, sems.at[0])]
    for i, ref in enumerate((chain_hbm, residue_hbm, valid_hbm)):
        copies.append(pltpu.make_async_copy(ref, ints_ref.at[i], sems.at[i + 1]))
    for copy in copies:
        copy.start()
    tokens, samples, width = single_ref.shape
    rows = tokens * samples
    token = lax.broadcasted_iota(jnp.int32, (tokens, width), 0)
    lane = lax.broadcasted_iota(jnp.int32, (tokens, width), 1)
    spread = (lane % tokens == token).astype(F32).astype(BF16)
    perm = sample_major(tokens, samples)
    for copy in copies:
        copy.wait()
    normed = normed_rows(single_ref[...])
    out_ref[pl.ds(0, rows), :] = matmul(perm, normed).astype(BF16)
    residue = ints_ref[1]
    row = lax.broadcasted_iota(jnp.int32, (META_ROWS, tokens), 0)
    meta = jnp.where(row == 0, ints_ref[0], 0)
    meta = jnp.where(row == 1, residue // RADIX, meta)
    meta = jnp.where(row == 2, residue % RADIX, meta)
    meta = jnp.where(row == 3, ints_ref[2], meta)
    tiled = matmul(meta.astype(F32).astype(BF16), spread)
    out_ref[pl.ds(rows, META_ROWS), :] = tiled.astype(BF16)
    meta_ref[...] = tiled.astype(BF16)


def join_body(single_ref, meta_ref, out_ref):
    tokens, samples, _ = single_ref.shape
    rows = tokens * samples
    normed = normed_rows(single_ref[...])
    out_ref[pl.ds(0, rows), :] = matmul(sample_major(tokens, samples), normed).astype(BF16)
    out_ref[pl.ds(rows, META_ROWS), :] = meta_ref[...]


def query_body(samples, heads, pay_hbm, wq_hbm, out_ref, pay_ref, wq_ref, q_ref, sems):
    copies = []
    for i, (source, target) in enumerate(((pay_hbm, pay_ref), (wq_hbm, wq_ref))):
        copies.append(pltpu.make_async_copy(source, target, sems.at[i]))
        copies[i].start()
    for copy in copies:
        copy.wait()
    q_ref[...] = matmul(pay_ref[pl.ds(0, q_ref.shape[0]), :], wq_ref[...]).astype(BF16)
    spread_queries(samples, heads, q_ref, out_ref)


def own_body(
    steps, chips, me_ref, pay_hbm, wg_hbm, pair_hbm, wp_hbm, gate_ref, *refs
):
    pay_ref, wg_ref, pair_ref, wp_ref, sems = refs[-5:]
    copies = []
    moves = ((wp_hbm, wp_ref), (pair_hbm, pair_ref), (pay_hbm, pay_ref), (wg_hbm, wg_ref))
    for i, (source, target) in enumerate(moves):
        copies.append(pltpu.make_async_copy(source, target, sems.at[i]))
        copies[i].start()
    copies[0].wait()
    copies[1].wait()
    pair_rows(steps, chips, me_ref[0], pair_ref, wp_ref[...], refs[:-5])
    copies[2].wait()
    copies[3].wait()
    data = pay_ref[pl.ds(0, gate_ref.shape[0]), :]
    gate_ref[...] = jax.nn.sigmoid(matmul(data, wg_ref[...]))


def kv_body(*refs):
    wk_ref, wv_ref, out_ref = refs[-3:]
    blocks = refs[:-3]
    n = len(blocks)
    rows = blocks[0].shape[0] - META_ROWS
    parts = [b[pl.ds(0, rows), :] for b in blocks]
    data = jnp.concatenate(parts, axis=0) if n > 1 else parts[0]
    out_ref[pl.ds(0, n * rows), :] = matmul(data, wk_ref[...]).astype(BF16)
    out_ref[pl.ds(n * rows, n * rows), :] = matmul(data, wv_ref[...]).astype(BF16)
    for i, b in enumerate(blocks):
        out_ref[pl.ds(2 * n * rows + i * META_ROWS, META_ROWS), :] = b[pl.ds(rows, META_ROWS), :]


def ring_chip(place, chips):
    place = lax.rem(place + 2 * chips, chips)
    return jnp.where(place < chips // 2, 2 * place, 2 * (chips - 1 - place) + 1)


def pair_rows(steps, chips, me, pair_ref, weights, out_refs):
    queries, total, channels = pair_ref.shape
    heads = weights.shape[0]
    tokens = total // len(steps)
    chip = me // CORES
    core = lax.rem(me, CORES)
    place = jnp.where(lax.rem(chip, 2) == 0, chip // 2, chips - 1 - chip // 2)
    lines = heads * queries
    head = lax.broadcasted_iota(jnp.int32, (heads, lines), 0)
    lane = lax.broadcasted_iota(jnp.int32, (heads, lines), 1)
    spread = (lane // queries == head).astype(F32).astype(BF16)
    wide = lax.dot_general(weights, spread, (((0,), (0,)), ((), ())), preferred_element_type=F32)
    lane = lax.broadcasted_iota(jnp.int32, (channels, lines), 1) % queries
    wide = jnp.concatenate(
        [jnp.where(lane == i, wide, 0.0).astype(BF16) for i in range(queries)], axis=0
    )
    at = 0
    for out_ref in out_refs:
        data = []
        for r, c in steps[at : at + out_ref.shape[0] // tokens]:
            block = ring_chip(place + r, chips) * CORES + lax.rem(core + c, CORES)
            start = pl.multiple_of(block * tokens, tokens)
            rows = [pair_ref[i, pl.ds(start, tokens), :] for i in range(queries)]
            data.append(jnp.concatenate(rows, axis=1))
        at += len(data)
        out_ref[...] = matmul(jnp.concatenate(data, axis=0), wide)


def kv_count(ref, rows):
    return ref.shape[0] // (2 * rows + META_ROWS)


def kv_metas(kv_refs, rows):
    found = []
    for r in kv_refs:
        n = kv_count(r, rows)
        found += [r[pl.ds(2 * n * rows + u * META_ROWS, META_ROWS), :] for u in range(n)]
    return found


def full_bias(own, metas, tokens, pair_ref, tab_ref, pad_ref):
    total = pair_ref.shape[0]
    heads, bins = tab_ref.shape
    reach = (bins - 2) // 2
    wide = -(-total // LANES) * LANES
    slot = lax.broadcasted_iota(jnp.int32, (META_ROWS, wide), 1) // tokens
    keys = jnp.zeros((META_ROWS, wide), F32)
    for u, row in enumerate(metas):
        row = row.astype(F32)
        row = jnp.concatenate([row] * (-(-wide // row.shape[1])), axis=1)[:, :wide]
        keys = jnp.where(slot == u, row, keys)
    here = own.astype(F32)[:, :LANES]
    lane = lax.broadcasted_iota(jnp.int32, (tokens, LANES), 1)
    row = lax.broadcasted_iota(jnp.int32, (tokens, LANES), 0)

    def column(values):
        values = jnp.where(lane == row, jnp.broadcast_to(values, (tokens, LANES)), 0.0)
        return jnp.sum(values, axis=-1, keepdims=True)

    chain_q = column(here[0:1, :])
    res_q = column(here[1:2, :] * RADIX + here[2:3, :])
    res_keys = keys[1:2, :] * RADIX + keys[2:3, :]
    offset = jnp.clip(res_q - res_keys, -reach, reach) + reach
    bucket = jnp.where(chain_q == keys[0:1, :], offset, float(bins - 1)).astype(jnp.int32)
    mask = (keys[3:4, :] - 1.0) * MASK_PENALTY
    pad_ref[...] = jnp.zeros_like(pad_ref)
    pad_ref[:, pl.ds(0, bins)] = tab_ref[...]
    out = []
    for h in range(heads):
        table = jnp.broadcast_to(pad_ref[h : h + 1, :], (tokens, LANES))
        rel = [
            jnp.take_along_axis(
                table, bucket[:, at : at + LANES], axis=1, mode="promise_in_bounds"
            )
            for at in range(0, wide, LANES)
        ]
        out.append((jnp.concatenate(rel, axis=1) if len(rel) > 1 else rel[0]) + mask)
    return pair_ref[...] + jnp.transpose(jnp.concatenate(out, axis=0))[:total]


def head_windows(width, hs):
    windows, h = [], 0
    while h * hs < width:
        start = min(h * hs // LANES * LANES, width - TILE)
        last = min((start + TILE) // hs, width // hs) - 1
        windows.append((h, last, start))
        h = last + 1
    return windows


def spread_queries(samples, heads, q_ref, out_ref):
    rows, width = q_ref.shape
    tokens = rows // samples
    hs = width // heads
    lines = heads * tokens
    token = lax.broadcasted_iota(jnp.int32, (tokens, lines), 0)
    lane = lax.broadcasted_iota(jnp.int32, (tokens, lines), 1)
    spread = (lane % tokens == token).astype(F32).astype(BF16)
    feature = lax.broadcasted_iota(jnp.int32, (width, lines), 0)
    lane = lax.broadcasted_iota(jnp.int32, (width, lines), 1)
    inside = feature // hs == lane // tokens
    for s in range(samples):
        wide = lax.dot_general(
            q_ref[pl.ds(s * tokens, tokens), :], spread, (((0,), (0,)), ((), ())),
            preferred_element_type=F32,
        )
        out_ref[pl.ds(s * width, width), :] = jnp.where(inside, wide, 0.0).astype(BF16)


def gather(kv_refs, rows, at, tokens, values):
    found = []
    for r in kv_refs:
        n = kv_count(r, rows)
        first = n if values else 0
        found += [r[pl.ds((first + u) * rows + at, tokens), :] for u in range(n)]
    return found


def weights_body(samples, scale, more, *refs):
    exp_ref, top_ref, mass_ref, pad_ref = refs[-4:]
    q_ref, pair_ref, tab_ref, own_ref = refs[-8:-4]
    kv_refs = refs[:-8]
    if more:
        kv_refs, before_ref, mass_before_ref = refs[:-10], refs[-10], refs[-9]
    count, lines = pair_ref.shape
    tokens = lines // tab_ref.shape[0]
    rows = tokens * samples
    width = kv_refs[0].shape[1]
    metas = kv_metas(kv_refs, rows)
    bias = full_bias(own_ref[...], metas, tokens, pair_ref, tab_ref, pad_ref)
    for s in range(samples):
        here = pl.ds(s, 1)
        keys = jnp.concatenate(gather(kv_refs, rows, s * tokens, tokens, False), axis=0)
        scores = matmul(keys, q_ref[pl.ds(s * width, width), :]) * scale + bias
        top = jnp.max(scores, axis=0, keepdims=True)
        if more:
            top = jnp.maximum(top, before_ref[here, :])
        weights = jnp.exp(scores - top)
        mass = jnp.sum(weights, axis=0, keepdims=True)
        if more:
            mass = mass + mass_before_ref[here, :] * jnp.exp(before_ref[here, :] - top)
        top_ref[here, :] = top
        mass_ref[here, :] = mass
        exp_ref[pl.ds(s * count, count), :] = weights


def finish_body(heads, scale, *refs):
    (
        q_ref, gate_ref, first_ref, first_top_ref, second_ref, top_ref, mass_ref, wk_ref, wv_ref,
        pair_ref, tab_ref, own_ref, single_ref, wo_ref, out_ref, pad_ref, weight_ref,
    ) = refs[-17:]
    kv_refs, lasts = refs[:-21], refs[-21:-17]
    tokens, samples, width = single_ref.shape
    rows = tokens * samples
    half = rows // 2
    hs = width // heads
    metas = [r[pl.ds(half, META_ROWS), :] for r in (lasts[0], lasts[2])]
    data = jnp.concatenate([r[pl.ds(0, half), :] for r in lasts], axis=0)
    k_last = matmul(data, wk_ref[...]).astype(BF16)
    v_last = matmul(data, wv_ref[...]).astype(BF16)
    bias = full_bias(own_ref[...], metas, tokens, pair_ref, tab_ref, pad_ref)
    lane_head = lax.broadcasted_iota(jnp.int32, (tokens, width), 1) // hs
    lines = heads * tokens
    for s in range(samples):
        new = [slice(u * rows + s * tokens, u * rows + (s + 1) * tokens) for u in range(2)]
        keys = jnp.concatenate([k_last[n] for n in new], axis=0)
        scores = matmul(keys, q_ref[pl.ds(s * width, width), :]) * scale + bias
        before = top_ref[pl.ds(s, 1), :]
        top = jnp.maximum(jnp.max(scores, axis=0, keepdims=True), before)
        shrink = jnp.exp(before - top)
        late = jnp.exp(scores - top)
        mass = jnp.sum(late, axis=0, keepdims=True) + mass_ref[pl.ds(s, 1), :] * shrink
        inv = 1.0 / mass
        weights = []
        for ref, old in ((first_ref, first_top_ref[pl.ds(s, 1), :]), (second_ref, before)):
            count = ref.shape[0] // samples
            weights.append(ref[pl.ds(s * count, count), :] * (jnp.exp(old - top) * inv))
        weights = jnp.concatenate(weights + [late * inv], axis=0)
        weight_ref[pl.ds(s * lines, lines), :] = jnp.transpose(weights).astype(BF16)
    gated = []
    for s in range(samples):
        new = [slice(u * rows + s * tokens, u * rows + (s + 1) * tokens) for u in range(2)]
        values = gather(kv_refs, rows, s * tokens, tokens, True)
        values = jnp.concatenate(values + [v_last[n] for n in new], axis=0)
        pieces = {}
        for h0, h1, start in head_windows(width, hs):
            here = pl.ds(s * lines + h0 * tokens, (h1 + 1 - h0) * tokens)
            ot = matmul(weight_ref[here, :], values[:, start : start + TILE])
            for first in range(start, start + TILE, LANES):
                for h in range(h0, h1 + 1):
                    if (h + 1) * hs <= first or h * hs >= first + LANES:
                        continue
                    lanes = slice(first - start, first - start + LANES)
                    part = ot[(h - h0) * tokens : (h + 1 - h0) * tokens, lanes]
                    if first in pieces:
                        mine = lane_head[:, first : first + LANES] == h
                        part = jnp.where(mine, part, pieces[first])
                    pieces[first] = part
        attended = jnp.concatenate([pieces[at] for at in sorted(pieces)], axis=1)
        gated.append((gate_ref[pl.ds(s * tokens, tokens), :] * attended).astype(BF16))
    gated = matmul(token_major(tokens, samples), jnp.concatenate(gated, axis=0)).astype(BF16)
    out = matmul(gated, wo_ref[...]).reshape(tokens, samples, width)
    out_ref[...] = (single_ref[...].astype(F32) + out).astype(BF16)


def call(body, out_shape, args, in_specs=None, flops=0, moved=0, limit=8 << 20, scratch=()):
    return pl.pallas_call(
        body,
        out_shape=out_shape,
        in_specs=in_specs or [VMEM] * len(args),
        out_specs=jax.tree.map(lambda _: VMEM, out_shape),
        scratch_shapes=scratch,
        compiler_params=pltpu.CompilerParams(vmem_limit_bytes=limit),
        cost_estimate=pl.CostEstimate(flops=flops, bytes_accessed=moved, transcendentals=0),
    )(*args)


def shards(
    single, pair, chain, residue, valid, w_query, w_key, w_value, w_gate, w_out, w_pair, rel_table
):
    tokens, samples, width = single.shape
    heads = w_pair.shape[1]
    total = pair.shape[1]
    rows = tokens * samples
    devices = lax.axis_size("tok")
    chips = devices // CORES
    half = chips // 2
    order = list(range(0, chips, 2)) + list(range(1, chips, 2))[::-1]
    me = lax.axis_index("tok").astype(jnp.int32).reshape(1)

    def ring(value, step):
        pairs = [
            (order[i] * CORES + c, order[(i + step) % chips] * CORES + c)
            for i in range(chips)
            for c in range(CORES)
        ]
        return lax.ppermute(value, "tok", pairs)

    def flip(value):
        return lax.ppermute(value, "tok", [(d, d ^ 1) for d in range(devices)])

    steps = [(0, 0), (0, 1)]
    for k in range(1, half):
        steps += [(-k, 0), (k, 0), (-k, 1), (k, 1)]
    steps += [(half, 0), (half, 1)]

    cw = ring(single, 1)
    ccw = ring(single, -1)
    blocks = jax.ShapeDtypeStruct((rows + META_ROWS, width), BF16)
    payload, meta = call(
        prep_body,
        (blocks, jax.ShapeDtypeStruct((META_ROWS, width), BF16)),
        (single, *(v.reshape(1, tokens) for v in (chain, residue, valid))),
        in_specs=[ANY] * 4,
        scratch=[
            pltpu.VMEM(single.shape, BF16),
            pltpu.VMEM((3, 1, tokens), jnp.int32),
            pltpu.SemaphoreType.DMA((4,)),
        ],
        flops=rows * width * 16,
        moved=4 * rows * width,
        limit=FULL,
    )
    cw_meta = ring(meta, 1)
    ccw_meta = ring(meta, -1)
    other = flip(payload)
    lines = heads * tokens
    query = call(
        functools.partial(query_body, samples, heads),
        jax.ShapeDtypeStruct((samples * width, lines), BF16),
        (payload, w_query),
        in_specs=[ANY] * 2,
        flops=2 * rows * width * (width + lines),
        moved=2 * width * width + 2 * samples * width * lines,
        limit=FULL,
        scratch=[
            pltpu.VMEM(blocks.shape, BF16),
            pltpu.VMEM((width, width), BF16),
            pltpu.VMEM((rows, width), BF16),
            pltpu.SemaphoreType.DMA((2,)),
        ],
    )

    def join(value, extra):
        return call(join_body, blocks, (value, extra), moved=4 * rows * width)

    cw = join(cw, cw_meta)
    ccw = join(ccw, ccw_meta)

    def kv(parts):
        n = len(parts)
        return call(
            kv_body,
            jax.ShapeDtypeStruct((n * (2 * rows + META_ROWS), width), BF16),
            (*parts, w_key, w_value),
            flops=4 * n * rows * width * width,
            moved=4 * width * width + 6 * n * rows * width,
        )

    def piece(value, at, meta):
        count = rows // 2 + (META_ROWS if meta else 0)

        def body(in_ref, out_ref):
            out_ref[pl.ds(0, rows // 2), :] = in_ref[pl.ds(at, rows // 2), :]
            if meta:
                out_ref[pl.ds(rows // 2, META_ROWS), :] = in_ref[pl.ds(rows, META_ROWS), :]

        shape = jax.ShapeDtypeStruct((count, width), BF16)
        return call(body, shape, (value,), moved=2 * rows * width)

    sizes = [len(steps) - 3 * CORES, 2 * CORES, CORES]
    gate, *pair_bias = call(
        functools.partial(own_body, steps, chips),
        (
            jax.ShapeDtypeStruct((rows, width), F32),
            *(jax.ShapeDtypeStruct((n * tokens, lines), F32) for n in sizes),
        ),
        (me, payload, w_gate, pair, w_pair.T),
        in_specs=[SMEM] + [ANY] * 4,
        flops=2 * rows * width * width + 2 * pair.size * lines,
        moved=2 * width * width + 6 * rows * width + 2 * pair.size,
        limit=(6 << 20) + 4 * pair.size,
        scratch=[
            pltpu.VMEM(blocks.shape, BF16),
            pltpu.VMEM((width, width), BF16),
            pltpu.VMEM(pair.shape, BF16),
            pltpu.VMEM(w_pair.shape[::-1], BF16),
            pltpu.SemaphoreType.DMA((4,)),
        ],
    )
    kvs = [kv([payload, other])]
    for k in range(1, half):
        if k + 1 < half:
            cw_next = ring(cw, 1)
            ccw_next = ring(ccw, -1)
        else:
            cw_next = ring(piece(cw, 0, True), 1)
            ccw_next = ring(piece(ccw, rows // 2, False), -1)
        cw_other, ccw_other = flip(cw), flip(ccw)
        kvs.append(kv([cw, ccw, cw_other, ccw_other]))
        cw, ccw = cw_next, ccw_next
    scale = 1.0 / math.sqrt(width // heads)
    state = jax.ShapeDtypeStruct((samples, lines), F32)
    table = rel_table.T
    pad = [pltpu.VMEM((heads, LANES), F32)]
    limit = (10 << 20) + 4 * samples * total * width

    def weights(at, parts, before):
        keys = sizes[at] * tokens
        return call(
            functools.partial(weights_body, samples, scale, bool(before)),
            (jax.ShapeDtypeStruct((samples * keys, lines), F32), state, state),
            (*parts, *before, query, pair_bias[at], table, meta),
            flops=2 * samples * keys * width * lines,
            moved=6 * samples * keys * width,
            limit=limit,
            scratch=pad,
        )

    first = weights(0, kvs[:-1], ())
    second = weights(1, kvs[-1:], first[1:])
    cw_other, ccw_other = flip(cw), flip(ccw)
    return call(
        functools.partial(finish_body, heads, scale),
        jax.ShapeDtypeStruct(single.shape, BF16),
        (
            *kvs, cw, ccw, cw_other, ccw_other, query, gate, *first[:2], *second, w_key, w_value,
            pair_bias[2], table, meta, single, w_out,
        ),
        flops=4 * rows * total * width,
        moved=2 * samples * total * width,
        limit=limit,
        scratch=[*pad, pltpu.VMEM((samples * lines, total), BF16)],
    )


def solution(mesh):
    placed = (
        P(("groups", "tok"), None, None),
        P(("groups", "tok"), None, None),
        P(("groups", "tok")),
        P(("groups", "tok")),
        P(("groups", "tok")),
        P(),
        P(),
        P(),
        P(),
        P(),
        P(),
        P(),
    )

    step = jax.shard_map(
        shards,
        mesh=mesh,
        in_specs=placed,
        out_specs=P(("groups", "tok"), None, None),
        check_vma=False,
    )
    return step
    return step
    return step
    return step
```

```python
import functools
import math

import jax
import jax.numpy as jnp
from jax import lax
from jax.experimental import pallas as pl
from jax.experimental.pallas import tpu as pltpu
from jax.sharding import PartitionSpec as P


NORM_EPS = 1e-05
MASK_PENALTY = 10000.0
F32 = jnp.float32
BF16 = jnp.bfloat16
CORES = 2
TILE = 256
LANES = 128
FULL = 60 << 20
VMEM = pl.BlockSpec(memory_space=pltpu.VMEM)
ANY = pl.BlockSpec(memory_space=pl.ANY)
SMEM = pl.BlockSpec(memory_space=pltpu.SMEM)
VMEM = pl.BlockSpec(memory_space=pltpu.VMEM)
ANY = pl.BlockSpec(memory_space=pl.ANY)
ANY = pl.BlockSpec(memory_space=pl.ANY)
SMEM = pl.BlockSpec(memory_space=pltpu.SMEM)
VMEM = pl.BlockSpec(memory_space=pltpu.VMEM)
ANY = pl.BlockSpec(memory_space=pl.ANY)
ANY = pl.BlockSpec(memory_space=pl.ANY)
ANY = pl.BlockSpec(memory_space=pl.ANY)
SMEM = pl.BlockSpec(memory_space=pltpu.SMEM)
VMEM = pl.BlockSpec(memory_space=pltpu.VMEM)
ANY = pl.BlockSpec(memory_space=pl.ANY)
ANY = pl.BlockSpec(memory_space=pl.ANY)
ANY = pl.BlockSpec(memory_space=pl.ANY)
SMEM = pl.BlockSpec(memory_space=pltpu.SMEM)
VMEM = pl.BlockSpec(memory_space=pltpu.VMEM)
ANY = pl.BlockSpec(memory_space=pl.ANY)
ANY = pl.BlockSpec(memory_space=pl.ANY)
ANY = pl.BlockSpec(memory_space=pl.ANY)
SMEM = pl.BlockSpec(memory_space=pltpu.SMEM)
VMEM = pl.BlockSpec(memory_space=pltpu.VMEM)
ANY = pl.BlockSpec(memory_space=pl.ANY)
ANY = pl.BlockSpec(memory_space=pl.ANY)
ANY = pl.BlockSpec(memory_space=pl.ANY)
SMEM = pl.BlockSpec(memory_space=pltpu.SMEM)


def normed_rows(block):
    tokens, samples, width = block.shape
    values = block.astype(F32).reshape(tokens * samples, width)
    centred = values - jnp.mean(values, axis=-1, keepdims=True)
    spread = jnp.mean(centred * centred, axis=-1, keepdims=True)
    return (centred * lax.rsqrt(spread + NORM_EPS)).astype(BF16)


def sample_major(tokens, samples):
    rows = tokens * samples
    to = lax.broadcasted_iota(jnp.int32, (rows, rows), 0)
    frm = lax.broadcasted_iota(jnp.int32, (rows, rows), 1)
    want = (to % tokens) * samples + to // tokens
    return (want == frm).astype(F32).astype(BF16)


def token_major(tokens, samples):
    rows = tokens * samples
    to = lax.broadcasted_iota(jnp.int32, (rows, rows), 0)
    frm = lax.broadcasted_iota(jnp.int32, (rows, rows), 1)
    want = (to % samples) * tokens + to // samples
    return (want == frm).astype(F32).astype(BF16)


def matmul(a, b):
    return jnp.dot(a, b, preferred_element_type=F32)


META_ROWS = 8
RADIX = 128


def prep_body(single_ref, chain_ref, residue_ref, valid_ref, out_ref):
    tokens, samples, width = single_ref.shape
    rows = tokens * samples
    normed = normed_rows(single_ref[...])
    out_ref[pl.ds(0, rows), :] = matmul(sample_major(tokens, samples), normed).astype(BF16)
    residue = residue_ref[...]
    row = lax.broadcasted_iota(jnp.int32, (META_ROWS, tokens), 0)
    meta = jnp.where(row == 0, chain_ref[...], 0)
    meta = jnp.where(row == 1, residue // RADIX, meta)
    meta = jnp.where(row == 2, residue % RADIX, meta)
    meta = jnp.where(row == 3, valid_ref[...], meta)
    token = lax.broadcasted_iota(jnp.int32, (tokens, width), 0)
    lane = lax.broadcasted_iota(jnp.int32, (tokens, width), 1)
    spread = (lane % tokens == token).astype(F32).astype(BF16)
    tiled = matmul(meta.astype(F32).astype(BF16), spread)
    out_ref[pl.ds(rows, META_ROWS), :] = tiled.astype(BF16)
    meta_ref[...] = tiled.astype(BF16)


def join_body(single_ref, meta_ref, out_ref):
    tokens, samples, _ = single_ref.shape
    rows = tokens * samples
    normed = normed_rows(single_ref[...])
    out_ref[pl.ds(0, rows), :] = matmul(sample_major(tokens, samples), normed).astype(BF16)
    out_ref[pl.ds(rows, META_ROWS), :] = meta_ref[...]


META_ROWS = 8
RADIX = 128


def prep_body(single_ref, chain_ref, residue_ref, valid_ref, out_ref):
    tokens, samples, width = single_ref.shape
    rows = tokens * samples
    normed = normed_rows(single_ref[...])
    out_ref[pl.ds(0, rows), :] = matmul(sample_major(tokens, samples), normed).astype(BF16)
    residue = residue_ref[...]
    row = lax.broadcasted_iota(jnp.int32, (META_ROWS, tokens), 0)
    meta = jnp.where(row == 0, chain_ref[...], 0)
    meta = jnp.where(row == 1, residue // RADIX, meta)
    meta = jnp.where(row == 2, residue % RADIX, meta)
    meta = jnp.where(row == 3, valid_ref[...], meta)
    token = lax.broadcasted_iota(jnp.int32, (tokens, width), 0)
    lane = lax.broadcasted_iota(jnp.int32, (tokens, width), 1)
    spread = (lane % tokens == token).astype(F32).astype(BF16)
    tiled = matmul(meta.astype(F32).astype(BF16), spread)
    out_ref[pl.ds(rows, META_ROWS), :] = tiled.astype(BF16)
    meta_ref[...] = tiled.astype(BF16)


def join_body(single_ref, meta_ref, out_ref):
    tokens, samples, _ = single_ref.shape
    rows = tokens * samples
    normed = normed_rows(single_ref[...])
    out_ref[pl.ds(0, rows), :] = matmul(sample_major(tokens, samples), normed).astype(BF16)
    out_ref[pl.ds(rows, META_ROWS), :] = meta_ref[...]


META_ROWS = 8
RADIX = 128


def prep_body(single_ref, chain_ref, residue_ref, valid_ref, out_ref):
    tokens, samples, width = single_ref.shape
    rows = tokens * samples
    normed = normed_rows(single_ref[...])
    out_ref[pl.ds(0, rows), :] = matmul(sample_major(tokens, samples), normed).astype(BF16)
    residue = residue_ref[...]
    row = lax.broadcasted_iota(jnp.int32, (META_ROWS, tokens), 0)
    meta = jnp.where(row == 0, chain_ref[...], 0)
    meta = jnp.where(row == 1, residue // RADIX, meta)
    meta = jnp.where(row == 2, residue % RADIX, meta)
    meta = jnp.where(row == 3, valid_ref[...], meta)
    token = lax.broadcasted_iota(jnp.int32, (tokens, width), 0)
    lane = lax.broadcasted_iota(jnp.int32, (tokens, width), 1)
    spread = (lane % tokens == token).astype(F32).astype(BF16)
    tiled = matmul(meta.astype(F32).astype(BF16), spread)
    out_ref[pl.ds(rows, META_ROWS), :] = tiled.astype(BF16)
    meta_ref[...] = tiled.astype(BF16)


def join_body(single_ref, meta_ref, out_ref):
    tokens, samples, _ = single_ref.shape
    rows = tokens * samples
    normed = normed_rows(single_ref[...])
    out_ref[pl.ds(0, rows), :] = matmul(sample_major(tokens, samples), normed).astype(BF16)
    out_ref[pl.ds(rows, META_ROWS), :] = meta_ref[...]


META_ROWS = 8
RADIX = 128


def prep_body(
    single_hbm, chain_hbm, residue_hbm, valid_hbm, out_ref, meta_ref, single_ref, ints_ref, sems
):
    copies = [pltpu.make_async_copy(single_hbm, single_ref, sems.at[0])]
    for i, ref in enumerate((chain_hbm, residue_hbm, valid_hbm)):
        copies.append(pltpu.make_async_copy(ref, ints_ref.at[i], sems.at[i + 1]))
    for copy in copies:
        copy.start()
    tokens, samples, width = single_ref.shape
    rows = tokens * samples
    token = lax.broadcasted_iota(jnp.int32, (tokens, width), 0)
    lane = lax.broadcasted_iota(jnp.int32, (tokens, width), 1)
    spread = (lane % tokens == token).astype(F32).astype(BF16)
    perm = sample_major(tokens, samples)
    for copy in copies:
        copy.wait()
    normed = normed_rows(single_ref[...])
    out_ref[pl.ds(0, rows), :] = matmul(perm, normed).astype(BF16)
    residue = ints_ref[1]
    row = lax.broadcasted_iota(jnp.int32, (META_ROWS, tokens), 0)
    meta = jnp.where(row == 0, ints_ref[0], 0)
    meta = jnp.where(row == 1, residue // RADIX, meta)
    meta = jnp.where(row == 2, residue % RADIX, meta)
    meta = jnp.where(row == 3, ints_ref[2], meta)
    tiled = matmul(meta.astype(F32).astype(BF16), spread)
    out_ref[pl.ds(rows, META_ROWS), :] = tiled.astype(BF16)
    meta_ref[...] = tiled.astype(BF16)


def join_body(single_ref, meta_ref, out_ref):
    tokens, samples, _ = single_ref.shape
    rows = tokens * samples
    normed = normed_rows(single_ref[...])
    out_ref[pl.ds(0, rows), :] = matmul(sample_major(tokens, samples), normed).astype(BF16)
    out_ref[pl.ds(rows, META_ROWS), :] = meta_ref[...]


META_ROWS = 8
RADIX = 128


def prep_body(single_hbm, chain_hbm, residue_hbm, valid_hbm, out_ref, meta_ref, single_ref, ints_ref, sems):
    copies = [pltpu.make_async_copy(single_hbm, single_ref, sems.at[0])]
    for i, ref in enumerate((chain_hbm, residue_hbm, valid_hbm)):
        copies.append(pltpu.make_async_copy(ref, ints_ref.at[i], sems.at[i + 1]))
    for copy in copies:
        copy.start()
    tokens, samples, width = single_ref.shape
    rows = tokens * samples
    token = lax.broadcasted_iota(jnp.int32, (tokens, width), 0)
    lane = lax.broadcasted_iota(jnp.int32, (tokens, width), 1)
    spread = (lane % tokens == token).astype(F32).astype(BF16)
    perm = sample_major(tokens, samples)
    for copy in copies:
        copy.wait()
    normed = normed_rows(single_ref[...])
    out_ref[pl.ds(0, rows), :] = matmul(perm, normed).astype(BF16)
    residue = ints_ref[1]
    row = lax.broadcasted_iota(jnp.int32, (META_ROWS, tokens), 0)
    meta = jnp.where(row == 0, ints_ref[0], 0)
    meta = jnp.where(row == 1, residue // RADIX, meta)
    meta = jnp.where(row == 2, residue % RADIX, meta)
    meta = jnp.where(row == 3, ints_ref[2], meta)
    tiled = matmul(meta.astype(F32).astype(BF16), spread)
    out_ref[pl.ds(rows, META_ROWS), :] = tiled.astype(BF16)
    meta_ref[...] = tiled.astype(BF16)


def join_body(single_ref, meta_ref, out_ref):
    tokens, samples, _ = single_ref.shape
    rows = tokens * samples
    normed = normed_rows(single_ref[...])
    out_ref[pl.ds(0, rows), :] = matmul(sample_major(tokens, samples), normed).astype(BF16)
    out_ref[pl.ds(rows, META_ROWS), :] = meta_ref[...]
    meta_ref[...] = tiled.astype(BF16)


META_ROWS = 8
RADIX = 128


def prep_body(
    single_hbm, chain_hbm, residue_hbm, valid_hbm, out_ref, meta_ref, single_ref, ints_ref, sems
):
    copies = [pltpu.make_async_copy(single_hbm, single_ref, sems.at[0])]
    for i, ref in enumerate((chain_hbm, residue_hbm, valid_hbm)):
        copies.append(pltpu.make_async_copy(ref, ints_ref.at[i], sems.at[i + 1]))
    for copy in copies:
        copy.start()
    tokens, samples, width = single_ref.shape
    rows = tokens * samples
    token = lax.broadcasted_iota(jnp.int32, (tokens, width), 0)
    lane = lax.broadcasted_iota(jnp.int32, (tokens, width), 1)
    spread = (lane % tokens == token).astype(F32).astype(BF16)
    perm = sample_major(tokens, samples)
    for copy in copies:
        copy.wait()
    normed = normed_rows(single_ref[...])
    out_ref[pl.ds(0, rows), :] = matmul(perm, normed).astype(BF16)
    residue = ints_ref[1]
    row = lax.broadcasted_iota(jnp.int32, (META_ROWS, tokens), 0)
    meta = jnp.where(row == 0, ints_ref[0], 0)
    meta = jnp.where(row == 1, residue // RADIX, meta)
    meta = jnp.where(row == 2, residue % RADIX, meta)
    meta = jnp.where(row == 3, ints_ref[2], meta)
    tiled = matmul(meta.astype(F32).astype(BF16), spread)
    out_ref[pl.ds(rows, META_ROWS), :] = tiled.astype(BF16)
    meta_ref[...] = tiled.astype(BF16)


def join_body(single_ref, meta_ref, out_ref):
    tokens, samples, _ = single_ref.shape
    rows = tokens * samples
    normed = normed_rows(single_ref[...])
    out_ref[pl.ds(0, rows), :] = matmul(sample_major(tokens, samples), normed).astype(BF16)
    out_ref[pl.ds(rows, META_ROWS), :] = meta_ref[...]


def query_body(samples, heads, me_ref, pay_ref, wq_ref, out_ref, q_ref):
    q_ref[...] = matmul(pay_ref[pl.ds(0, q_ref.shape[0]), :], wq_ref[...]).astype(BF16)
    spread_queries(samples, heads, q_ref, out_ref)


def pair_body(steps, chips, me_ref, pair_ref, wp_ref, *out_refs):
    pair_rows(steps, chips, me_ref[0], pair_ref, wp_ref[...], out_refs)


def gate_body(pay_ref, wg_ref, gate_ref):
    data = pay_ref[pl.ds(0, gate_ref.shape[0]), :]
    gate_ref[...] = jax.nn.sigmoid(matmul(data, wg_ref[...]))


def kv_body(*refs):
    wk_ref, wv_ref, out_ref = refs[-3:]
    blocks = refs[:-3]
    n = len(blocks)
    rows = blocks[0].shape[0] - META_ROWS
    parts = [b[pl.ds(0, rows), :] for b in blocks]
    data = jnp.concatenate(parts, axis=0) if n > 1 else parts[0]
    out_ref[pl.ds(0, n * rows), :] = matmul(data, wk_ref[...]).astype(BF16)
    out_ref[pl.ds(n * rows, n * rows), :] = matmul(data, wv_ref[...]).astype(BF16)
    for i, b in enumerate(blocks):
        out_ref[pl.ds(2 * n * rows + i * META_ROWS, META_ROWS), :] = b[pl.ds(rows, META_ROWS), :]


def ring_chip(place, chips):
    place = lax.rem(place + 2 * chips, chips)
    return jnp.where(place < chips // 2, 2 * place, 2 * (chips - 1 - place) + 1)


def pair_rows(steps, chips, me, pair_ref, weights, out_refs):
    queries, total, channels = pair_ref.shape
    heads = weights.shape[0]
    tokens = total // len(steps)
    chip = me // CORES
    core = lax.rem(me, CORES)
    place = jnp.where(lax.rem(chip, 2) == 0, chip // 2, chips - 1 - chip // 2)
    lines = heads * queries
    head = lax.broadcasted_iota(jnp.int32, (heads, lines), 0)
    lane = lax.broadcasted_iota(jnp.int32, (heads, lines), 1)
    spread = (lane // queries == head).astype(F32).astype(BF16)
    wide = lax.dot_general(weights, spread, (((0,), (0,)), ((), ())), preferred_element_type=F32)
    lane = lax.broadcasted_iota(jnp.int32, (channels, lines), 1) % queries
    wide = jnp.concatenate(
        [jnp.where(lane == i, wide, 0.0).astype(BF16) for i in range(queries)], axis=0
    )
    at = 0
    for out_ref in out_refs:
        data = []
        for r, c in steps[at : at + out_ref.shape[0] // tokens]:
            block = ring_chip(place + r, chips) * CORES + lax.rem(core + c, CORES)
            start = pl.multiple_of(block * tokens, tokens)
            rows = [pair_ref[i, pl.ds(start, tokens), :] for i in range(queries)]
            data.append(jnp.concatenate(rows, axis=1))
        at += len(data)
        out_ref[...] = matmul(jnp.concatenate(data, axis=0), wide)


def kv_count(ref, rows):
    return ref.shape[0] // (2 * rows + META_ROWS)


def kv_metas(kv_refs, rows):
    found = []
    for r in kv_refs:
        n = kv_count(r, rows)
        found += [r[pl.ds(2 * n * rows + u * META_ROWS, META_ROWS), :] for u in range(n)]
    return found


def full_bias(own, metas, tokens, pair_ref, tab_ref, pad_ref):
    total = pair_ref.shape[0]
    heads, bins = tab_ref.shape
    reach = (bins - 2) // 2
    wide = -(-total // LANES) * LANES
    slot = lax.broadcasted_iota(jnp.int32, (META_ROWS, wide), 1) // tokens
    keys = jnp.zeros((META_ROWS, wide), F32)
    for u, row in enumerate(metas):
        row = row.astype(F32)
        row = jnp.concatenate([row] * (-(-wide // row.shape[1])), axis=1)[:, :wide]
        keys = jnp.where(slot == u, row, keys)
    here = own.astype(F32)[:, :LANES]
    lane = lax.broadcasted_iota(jnp.int32, (tokens, LANES), 1)
    row = lax.broadcasted_iota(jnp.int32, (tokens, LANES), 0)

    def column(values):
        values = jnp.where(lane == row, jnp.broadcast_to(values, (tokens, LANES)), 0.0)
        return jnp.sum(values, axis=-1, keepdims=True)

    chain_q = column(here[0:1, :])
    res_q = column(here[1:2, :] * RADIX + here[2:3, :])
    res_keys = keys[1:2, :] * RADIX + keys[2:3, :]
    offset = jnp.clip(res_q - res_keys, -reach, reach) + reach
    bucket = jnp.where(chain_q == keys[0:1, :], offset, float(bins - 1)).astype(jnp.int32)
    mask = (keys[3:4, :] - 1.0) * MASK_PENALTY
    pad_ref[...] = jnp.zeros_like(pad_ref)
    pad_ref[:, pl.ds(0, bins)] = tab_ref[...]
    out = []
    for h in range(heads):
        table = jnp.broadcast_to(pad_ref[h : h + 1, :], (tokens, LANES))
        rel = [
            jnp.take_along_axis(
                table, bucket[:, at : at + LANES], axis=1, mode="promise_in_bounds"
            )
            for at in range(0, wide, LANES)
        ]
        out.append((jnp.concatenate(rel, axis=1) if len(rel) > 1 else rel[0]) + mask)
    return pair_ref[...] + jnp.transpose(jnp.concatenate(out, axis=0))[:total]


def head_windows(width, hs):
    windows, h = [], 0
    while h * hs < width:
        start = min(h * hs // LANES * LANES, width - TILE)
        last = min((start + TILE) // hs, width // hs) - 1
        windows.append((h, last, start))
        h = last + 1
    return windows


def spread_queries(samples, heads, q_ref, out_ref):
    rows, width = q_ref.shape
    tokens = rows // samples
    hs = width // heads
    lines = heads * tokens
    token = lax.broadcasted_iota(jnp.int32, (tokens, lines), 0)
    lane = lax.broadcasted_iota(jnp.int32, (tokens, lines), 1)
    spread = (lane % tokens == token).astype(F32).astype(BF16)
    feature = lax.broadcasted_iota(jnp.int32, (width, lines), 0)
    lane = lax.broadcasted_iota(jnp.int32, (width, lines), 1)
    inside = feature // hs == lane // tokens
    for s in range(samples):
        wide = lax.dot_general(
            q_ref[pl.ds(s * tokens, tokens), :], spread, (((0,), (0,)), ((), ())),
            preferred_element_type=F32,
        )
        out_ref[pl.ds(s * width, width), :] = jnp.where(inside, wide, 0.0).astype(BF16)


def gather(kv_refs, rows, at, tokens, values):
    found = []
    for r in kv_refs:
        n = kv_count(r, rows)
        first = n if values else 0
        found += [r[pl.ds((first + u) * rows + at, tokens), :] for u in range(n)]
    return found


def weights_body(samples, scale, more, *refs):
    exp_ref, top_ref, mass_ref, pad_ref = refs[-4:]
    q_ref, pair_ref, tab_ref, own_ref = refs[-8:-4]
    kv_refs = refs[:-8]
    if more:
        kv_refs, before_ref, mass_before_ref = refs[:-10], refs[-10], refs[-9]
    count, lines = pair_ref.shape
    tokens = lines // tab_ref.shape[0]
    rows = tokens * samples
    width = kv_refs[0].shape[1]
    metas = kv_metas(kv_refs, rows)
    bias = full_bias(own_ref[...], metas, tokens, pair_ref, tab_ref, pad_ref)
    for s in range(samples):
        here = pl.ds(s, 1)
        keys = jnp.concatenate(gather(kv_refs, rows, s * tokens, tokens, False), axis=0)
        scores = matmul(keys, q_ref[pl.ds(s * width, width), :]) * scale + bias
        top = jnp.max(scores, axis=0, keepdims=True)
        if more:
            top = jnp.maximum(top, before_ref[here, :])
        weights = jnp.exp(scores - top)
        mass = jnp.sum(weights, axis=0, keepdims=True)
        if more:
            mass = mass + mass_before_ref[here, :] * jnp.exp(before_ref[here, :] - top)
        top_ref[here, :] = top
        mass_ref[here, :] = mass
        exp_ref[pl.ds(s * count, count), :] = weights


def finish_body(heads, scale, split, *refs):
    (
        q_ref, gate_ref, exp_ref, top_ref, mass_ref, wk_ref, wv_ref, pair_ref, tab_ref, own_ref,
        single_ref, wo_ref, out_ref, pad_ref, weight_ref,
    ) = refs[-15:]
    kv_refs, lasts = refs[:-19], refs[-19:-15]
    tokens, samples, width = single_ref.shape
    rows = tokens * samples
    half = rows // 2
    hs = width // heads
    metas = kv_metas(kv_refs[split:], rows) + [r[pl.ds(half, META_ROWS), :] for r in (lasts[0], lasts[2])]
    data = jnp.concatenate([r[pl.ds(0, half), :] for r in lasts], axis=0)
    k_last = matmul(data, wk_ref[...]).astype(BF16)
    v_last = matmul(data, wv_ref[...]).astype(BF16)
    bias = full_bias(own_ref[...], metas, tokens, pair_ref, tab_ref, pad_ref)
    count = exp_ref.shape[0] // samples
    lane_head = lax.broadcasted_iota(jnp.int32, (tokens, width), 1) // hs
    lines = heads * tokens
    for s in range(samples):
        new = [slice(u * rows + s * tokens, u * rows + (s + 1) * tokens) for u in range(2)]
        keys = gather(kv_refs[split:], rows, s * tokens, tokens, False)
        keys = jnp.concatenate(keys + [k_last[n] for n in new], axis=0)
        scores = matmul(keys, q_ref[pl.ds(s * width, width), :]) * scale + bias
        before = top_ref[pl.ds(s, 1), :]
        top = jnp.maximum(jnp.max(scores, axis=0, keepdims=True), before)
        shrink = jnp.exp(before - top)
        late = jnp.exp(scores - top)
        mass = jnp.sum(late, axis=0, keepdims=True) + mass_ref[pl.ds(s, 1), :] * shrink
        inv = 1.0 / mass
        old = exp_ref[pl.ds(s * count, count), :] * (shrink * inv)
        weights = jnp.concatenate([old, late * inv], axis=0)
        weight_ref[pl.ds(s * lines, lines), :] = jnp.transpose(weights).astype(BF16)
    gated = []
    for s in range(samples):
        new = [slice(u * rows + s * tokens, u * rows + (s + 1) * tokens) for u in range(2)]
        values = gather(kv_refs, rows, s * tokens, tokens, True)
        values = jnp.concatenate(values + [v_last[n] for n in new], axis=0)
        pieces = {}
        for h0, h1, start in head_windows(width, hs):
            here = pl.ds(s * lines + h0 * tokens, (h1 + 1 - h0) * tokens)
            ot = matmul(weight_ref[here, :], values[:, start : start + TILE])
            for first in range(start, start + TILE, LANES):
                for h in range(h0, h1 + 1):
                    if (h + 1) * hs <= first or h * hs >= first + LANES:
                        continue
                    lanes = slice(first - start, first - start + LANES)
                    part = ot[(h - h0) * tokens : (h + 1 - h0) * tokens, lanes]
                    if first in pieces:
                        mine = lane_head[:, first : first + LANES] == h
                        part = jnp.where(mine, part, pieces[first])
                    pieces[first] = part
        attended = jnp.concatenate([pieces[at] for at in sorted(pieces)], axis=1)
        gated.append((gate_ref[pl.ds(s * tokens, tokens), :] * attended).astype(BF16))
    gated = matmul(token_major(tokens, samples), jnp.concatenate(gated, axis=0)).astype(BF16)
    out = matmul(gated, wo_ref[...]).reshape(tokens, samples, width)
    out_ref[...] = (single_ref[...].astype(F32) + out).astype(BF16)


def call(body, out_shape, args, in_specs=None, flops=0, moved=0, limit=8 << 20, scratch=()):
    return pl.pallas_call(
        body,
        out_shape=out_shape,
        in_specs=in_specs or [VMEM] * len(args),
        out_specs=jax.tree.map(lambda _: VMEM, out_shape),
        scratch_shapes=scratch,
        compiler_params=pltpu.CompilerParams(vmem_limit_bytes=limit),
        cost_estimate=pl.CostEstimate(flops=flops, bytes_accessed=moved, transcendentals=0),
    )(*args)


def shards(
    single, pair, chain, residue, valid, w_query, w_key, w_value, w_gate, w_out, w_pair, rel_table
):
    tokens, samples, width = single.shape
    heads = w_pair.shape[1]
    total = pair.shape[1]
    rows = tokens * samples
    devices = lax.axis_size("tok")
    chips = devices // CORES
    half = chips // 2
    order = list(range(0, chips, 2)) + list(range(1, chips, 2))[::-1]
    me = lax.axis_index("tok").astype(jnp.int32).reshape(1)

    def ring(value, step):
        pairs = [
            (order[i] * CORES + c, order[(i + step) % chips] * CORES + c)
            for i in range(chips)
            for c in range(CORES)
        ]
        return lax.ppermute(value, "tok", pairs)

    def flip(value):
        return lax.ppermute(value, "tok", [(d, d ^ 1) for d in range(devices)])

    steps = [(0, 0), (0, 1)]
    for k in range(1, half):
        steps += [(-k, 0), (k, 0), (-k, 1), (k, 1)]
    steps += [(half, 0), (half, 1)]

    cw = ring(single, 1)
    ccw = ring(single, -1)
    blocks = jax.ShapeDtypeStruct((rows + META_ROWS, width), BF16)
    payload, meta = call(
        prep_body,
        (blocks, jax.ShapeDtypeStruct((META_ROWS, width), BF16)),
        (single, *(v.reshape(1, tokens) for v in (chain, residue, valid))),
        in_specs=[ANY] * 4,
        scratch=[
            pltpu.VMEM(single.shape, BF16),
            pltpu.VMEM((3, 1, tokens), jnp.int32),
            pltpu.SemaphoreType.DMA((4,)),
        ],
        flops=rows * width * 16,
        moved=4 * rows * width,
        limit=FULL,
    )
    cw_meta = ring(meta, 1)
    ccw_meta = ring(meta, -1)
    lines = heads * tokens
    query = call(
        functools.partial(query_body, samples, heads),
        jax.ShapeDtypeStruct((samples * width, lines), BF16),
        (me, payload, w_query),
        in_specs=[SMEM, VMEM, VMEM],
        flops=2 * rows * width * (width + lines),
        moved=2 * width * width + 2 * samples * width * lines,
        scratch=[pltpu.VMEM((rows, width), BF16)],
    )
    gate = call(
        gate_body,
        jax.ShapeDtypeStruct((rows, width), F32),
        (payload, w_gate),
        flops=2 * rows * width * width,
        moved=2 * width * width + 6 * rows * width,
    )

    def join(value, extra):
        return call(join_body, blocks, (value, extra), moved=4 * rows * width)

    cw = join(cw, cw_meta)
    ccw = join(ccw, ccw_meta)

    def kv(parts):
        n = len(parts)
        return call(
            kv_body,
            jax.ShapeDtypeStruct((n * (2 * rows + META_ROWS), width), BF16),
            (*parts, w_key, w_value),
            flops=4 * n * rows * width * width,
            moved=4 * width * width + 6 * n * rows * width,
        )

    def piece(value, at, meta):
        count = rows // 2 + (META_ROWS if meta else 0)

        def body(in_ref, out_ref):
            out_ref[pl.ds(0, rows // 2), :] = in_ref[pl.ds(at, rows // 2), :]
            if meta:
                out_ref[pl.ds(rows // 2, META_ROWS), :] = in_ref[pl.ds(rows, META_ROWS), :]

        shape = jax.ShapeDtypeStruct((count, width), BF16)
        return call(body, shape, (value,), moved=2 * rows * width)

    sizes = [len(steps) - 3 * CORES, 3 * CORES]
    pair_bias = call(
        functools.partial(pair_body, steps, chips),
        tuple(jax.ShapeDtypeStruct((n * tokens, lines), F32) for n in sizes),
        (me, pair, w_pair.T),
        in_specs=[SMEM, VMEM, VMEM],
        flops=2 * pair.size * lines,
        moved=2 * pair.size + 4 * total * lines,
        limit=(6 << 20) + 4 * pair.size,
    )
    kvs = [kv([payload])]
    kvs.append(flip(kvs[-1]))
    for k in range(1, half):
        if k + 1 < half:
            cw_next = ring(cw, 1)
            ccw_next = ring(ccw, -1)
        else:
            cw_next = ring(piece(cw, 0, True), 1)
            ccw_next = ring(piece(ccw, rows // 2, False), -1)
        kvs.append(kv([cw, ccw]))
        kvs.append(flip(kvs[-1]))
        cw, ccw = cw_next, ccw_next
    scale = 1.0 / math.sqrt(width // heads)
    state = jax.ShapeDtypeStruct((samples, lines), F32)
    table = rel_table.T
    pad = [pltpu.VMEM((heads, LANES), F32)]
    limit = (10 << 20) + 4 * samples * total * width

    split = 2 * (half - 1)
    keys = sizes[0] * tokens
    first = call(
        functools.partial(weights_body, samples, scale, False),
        (jax.ShapeDtypeStruct((samples * keys, lines), F32), state, state),
        (*kvs[:split], query, pair_bias[0], table, meta),
        flops=2 * samples * keys * width * lines,
        moved=6 * samples * keys * width,
        limit=limit,
        scratch=pad,
    )
    cw_other, ccw_other = flip(cw), flip(ccw)
    return call(
        functools.partial(finish_body, heads, scale, split),
        jax.ShapeDtypeStruct(single.shape, BF16),
        (
            *kvs, cw, ccw, cw_other, ccw_other, query, gate, *first, w_key, w_value,
            pair_bias[1], table, meta, single, w_out,
        ),
        flops=4 * rows * total * width,
        moved=2 * samples * total * width,
        limit=limit,
        scratch=[*pad, pltpu.VMEM((samples * lines, total), BF16)],
    )


def solution(mesh):
    placed = (
        P(("groups", "tok"), None, None),
        P(("groups", "tok"), None, None),
        P(("groups", "tok")),
        P(("groups", "tok")),
        P(("groups", "tok")),
        P(),
        P(),
        P(),
        P(),
        P(),
        P(),
        P(),
    )

    step = jax.shard_map(
        shards,
        mesh=mesh,
        in_specs=placed,
        out_specs=P(("groups", "tok"), None, None),
        check_vma=False,
    )
    return step
    return step
    return step
    return step
```

```python
import functools
import math

import jax
import jax.numpy as jnp
from jax import lax
from jax.experimental import pallas as pl
from jax.experimental.pallas import tpu as pltpu
from jax.sharding import PartitionSpec as P


NORM_EPS = 1e-05
MASK_PENALTY = 10000.0
F32 = jnp.float32
BF16 = jnp.bfloat16
CORES = 2
TILE = 256
LANES = 128
FULL = 60 << 20
VMEM = pl.BlockSpec(memory_space=pltpu.VMEM)
ANY = pl.BlockSpec(memory_space=pl.ANY)
SMEM = pl.BlockSpec(memory_space=pltpu.SMEM)
VMEM = pl.BlockSpec(memory_space=pltpu.VMEM)
ANY = pl.BlockSpec(memory_space=pl.ANY)
ANY = pl.BlockSpec(memory_space=pl.ANY)
SMEM = pl.BlockSpec(memory_space=pltpu.SMEM)
VMEM = pl.BlockSpec(memory_space=pltpu.VMEM)
ANY = pl.BlockSpec(memory_space=pl.ANY)
ANY = pl.BlockSpec(memory_space=pl.ANY)
ANY = pl.BlockSpec(memory_space=pl.ANY)
SMEM = pl.BlockSpec(memory_space=pltpu.SMEM)
VMEM = pl.BlockSpec(memory_space=pltpu.VMEM)
ANY = pl.BlockSpec(memory_space=pl.ANY)
ANY = pl.BlockSpec(memory_space=pl.ANY)
ANY = pl.BlockSpec(memory_space=pl.ANY)
SMEM = pl.BlockSpec(memory_space=pltpu.SMEM)
VMEM = pl.BlockSpec(memory_space=pltpu.VMEM)
ANY = pl.BlockSpec(memory_space=pl.ANY)
ANY = pl.BlockSpec(memory_space=pl.ANY)
ANY = pl.BlockSpec(memory_space=pl.ANY)
SMEM = pl.BlockSpec(memory_space=pltpu.SMEM)
VMEM = pl.BlockSpec(memory_space=pltpu.VMEM)
ANY = pl.BlockSpec(memory_space=pl.ANY)
ANY = pl.BlockSpec(memory_space=pl.ANY)
ANY = pl.BlockSpec(memory_space=pl.ANY)
SMEM = pl.BlockSpec(memory_space=pltpu.SMEM)


def normed_rows(block):
    tokens, samples, width = block.shape
    values = block.astype(F32).reshape(tokens * samples, width)
    centred = values - jnp.mean(values, axis=-1, keepdims=True)
    spread = jnp.mean(centred * centred, axis=-1, keepdims=True)
    return (centred * lax.rsqrt(spread + NORM_EPS)).astype(BF16)


def sample_major(tokens, samples):
    rows = tokens * samples
    to = lax.broadcasted_iota(jnp.int32, (rows, rows), 0)
    frm = lax.broadcasted_iota(jnp.int32, (rows, rows), 1)
    want = (to % tokens) * samples + to // tokens
    return (want == frm).astype(F32).astype(BF16)


def token_major(tokens, samples):
    rows = tokens * samples
    to = lax.broadcasted_iota(jnp.int32, (rows, rows), 0)
    frm = lax.broadcasted_iota(jnp.int32, (rows, rows), 1)
    want = (to % samples) * tokens + to // samples
    return (want == frm).astype(F32).astype(BF16)


def matmul(a, b):
    return jnp.dot(a, b, preferred_element_type=F32)


META_ROWS = 8
RADIX = 128


def prep_body(single_ref, chain_ref, residue_ref, valid_ref, out_ref):
    tokens, samples, width = single_ref.shape
    rows = tokens * samples
    normed = normed_rows(single_ref[...])
    out_ref[pl.ds(0, rows), :] = matmul(sample_major(tokens, samples), normed).astype(BF16)
    residue = residue_ref[...]
    row = lax.broadcasted_iota(jnp.int32, (META_ROWS, tokens), 0)
    meta = jnp.where(row == 0, chain_ref[...], 0)
    meta = jnp.where(row == 1, residue // RADIX, meta)
    meta = jnp.where(row == 2, residue % RADIX, meta)
    meta = jnp.where(row == 3, valid_ref[...], meta)
    token = lax.broadcasted_iota(jnp.int32, (tokens, width), 0)
    lane = lax.broadcasted_iota(jnp.int32, (tokens, width), 1)
    spread = (lane % tokens == token).astype(F32).astype(BF16)
    tiled = matmul(meta.astype(F32).astype(BF16), spread)
    out_ref[pl.ds(rows, META_ROWS), :] = tiled.astype(BF16)
    meta_ref[...] = tiled.astype(BF16)
    weight.wait()
    q_ref[...] = matmul(data, wq_ref[...]).astype(BF16)


def join_body(single_ref, meta_ref, out_ref):
    tokens, samples, _ = single_ref.shape
    rows = tokens * samples
    normed = normed_rows(single_ref[...])
    out_ref[pl.ds(0, rows), :] = matmul(sample_major(tokens, samples), normed).astype(BF16)
    out_ref[pl.ds(rows, META_ROWS), :] = meta_ref[...]


META_ROWS = 8
RADIX = 128


def prep_body(single_ref, chain_ref, residue_ref, valid_ref, out_ref):
    tokens, samples, width = single_ref.shape
    rows = tokens * samples
    normed = normed_rows(single_ref[...])
    out_ref[pl.ds(0, rows), :] = matmul(sample_major(tokens, samples), normed).astype(BF16)
    residue = residue_ref[...]
    row = lax.broadcasted_iota(jnp.int32, (META_ROWS, tokens), 0)
    meta = jnp.where(row == 0, chain_ref[...], 0)
    meta = jnp.where(row == 1, residue // RADIX, meta)
    meta = jnp.where(row == 2, residue % RADIX, meta)
    meta = jnp.where(row == 3, valid_ref[...], meta)
    token = lax.broadcasted_iota(jnp.int32, (tokens, width), 0)
    lane = lax.broadcasted_iota(jnp.int32, (tokens, width), 1)
    spread = (lane % tokens == token).astype(F32).astype(BF16)
    tiled = matmul(meta.astype(F32).astype(BF16), spread)
    out_ref[pl.ds(rows, META_ROWS), :] = tiled.astype(BF16)
    meta_ref[...] = tiled.astype(BF16)
    weight.wait()
    q_ref[...] = matmul(data, wq_ref[...]).astype(BF16)


def join_body(single_ref, meta_ref, out_ref):
    tokens, samples, _ = single_ref.shape
    rows = tokens * samples
    normed = normed_rows(single_ref[...])
    out_ref[pl.ds(0, rows), :] = matmul(sample_major(tokens, samples), normed).astype(BF16)
    out_ref[pl.ds(rows, META_ROWS), :] = meta_ref[...]


META_ROWS = 8
RADIX = 128


def prep_body(single_ref, chain_ref, residue_ref, valid_ref, out_ref):
    tokens, samples, width = single_ref.shape
    rows = tokens * samples
    normed = normed_rows(single_ref[...])
    out_ref[pl.ds(0, rows), :] = matmul(sample_major(tokens, samples), normed).astype(BF16)
    residue = residue_ref[...]
    row = lax.broadcasted_iota(jnp.int32, (META_ROWS, tokens), 0)
    meta = jnp.where(row == 0, chain_ref[...], 0)
    meta = jnp.where(row == 1, residue // RADIX, meta)
    meta = jnp.where(row == 2, residue % RADIX, meta)
    meta = jnp.where(row == 3, valid_ref[...], meta)
    token = lax.broadcasted_iota(jnp.int32, (tokens, width), 0)
    lane = lax.broadcasted_iota(jnp.int32, (tokens, width), 1)
    spread = (lane % tokens == token).astype(F32).astype(BF16)
    tiled = matmul(meta.astype(F32).astype(BF16), spread)
    out_ref[pl.ds(rows, META_ROWS), :] = tiled.astype(BF16)
    meta_ref[...] = tiled.astype(BF16)
    weight.wait()
    q_ref[...] = matmul(data, wq_ref[...]).astype(BF16)


def join_body(single_ref, meta_ref, out_ref):
    tokens, samples, _ = single_ref.shape
    rows = tokens * samples
    normed = normed_rows(single_ref[...])
    out_ref[pl.ds(0, rows), :] = matmul(sample_major(tokens, samples), normed).astype(BF16)
    out_ref[pl.ds(rows, META_ROWS), :] = meta_ref[...]


META_ROWS = 8
RADIX = 128


def prep_body(
    single_hbm, chain_hbm, residue_hbm, valid_hbm, wq_hbm, out_ref, meta_ref, q_ref,
    single_ref, ints_ref, wq_ref, sems,
):
    copies = [pltpu.make_async_copy(single_hbm, single_ref, sems.at[0])]
    for i, ref in enumerate((chain_hbm, residue_hbm, valid_hbm)):
        copies.append(pltpu.make_async_copy(ref, ints_ref.at[i], sems.at[i + 1]))
    weight = pltpu.make_async_copy(wq_hbm, wq_ref, sems.at[4])
    for copy in (*copies, weight):
        copy.start()
    tokens, samples, width = single_ref.shape
    rows = tokens * samples
    token = lax.broadcasted_iota(jnp.int32, (tokens, width), 0)
    lane = lax.broadcasted_iota(jnp.int32, (tokens, width), 1)
    spread = (lane % tokens == token).astype(F32).astype(BF16)
    perm = sample_major(tokens, samples)
    for copy in copies:
        copy.wait()
    data = matmul(perm, normed_rows(single_ref[...])).astype(BF16)
    out_ref[pl.ds(0, rows), :] = data
    residue = ints_ref[1]
    row = lax.broadcasted_iota(jnp.int32, (META_ROWS, tokens), 0)
    meta = jnp.where(row == 0, ints_ref[0], 0)
    meta = jnp.where(row == 1, residue // RADIX, meta)
    meta = jnp.where(row == 2, residue % RADIX, meta)
    meta = jnp.where(row == 3, ints_ref[2], meta)
    tiled = matmul(meta.astype(F32).astype(BF16), spread)
    out_ref[pl.ds(rows, META_ROWS), :] = tiled.astype(BF16)
    meta_ref[...] = tiled.astype(BF16)
    weight.wait()
    q_ref[...] = matmul(data, wq_ref[...]).astype(BF16)


def join_body(single_ref, meta_ref, out_ref):
    tokens, samples, _ = single_ref.shape
    rows = tokens * samples
    normed = normed_rows(single_ref[...])
    out_ref[pl.ds(0, rows), :] = matmul(sample_major(tokens, samples), normed).astype(BF16)
    out_ref[pl.ds(rows, META_ROWS), :] = meta_ref[...]


META_ROWS = 8
RADIX = 128


def prep_body(single_hbm, chain_hbm, residue_hbm, valid_hbm, out_ref, meta_ref, single_ref, ints_ref, sems):
    copies = [pltpu.make_async_copy(single_hbm, single_ref, sems.at[0])]
    for i, ref in enumerate((chain_hbm, residue_hbm, valid_hbm)):
        copies.append(pltpu.make_async_copy(ref, ints_ref.at[i], sems.at[i + 1]))
    weight = pltpu.make_async_copy(wq_hbm, wq_ref, sems.at[4])
    for copy in (*copies, weight):
        copy.start()
    tokens, samples, width = single_ref.shape
    rows = tokens * samples
    token = lax.broadcasted_iota(jnp.int32, (tokens, width), 0)
    lane = lax.broadcasted_iota(jnp.int32, (tokens, width), 1)
    spread = (lane % tokens == token).astype(F32).astype(BF16)
    perm = sample_major(tokens, samples)
    for copy in copies:
        copy.wait()
    data = matmul(perm, normed_rows(single_ref[...])).astype(BF16)
    out_ref[pl.ds(0, rows), :] = data
    residue = ints_ref[1]
    row = lax.broadcasted_iota(jnp.int32, (META_ROWS, tokens), 0)
    meta = jnp.where(row == 0, ints_ref[0], 0)
    meta = jnp.where(row == 1, residue // RADIX, meta)
    meta = jnp.where(row == 2, residue % RADIX, meta)
    meta = jnp.where(row == 3, ints_ref[2], meta)
    tiled = matmul(meta.astype(F32).astype(BF16), spread)
    out_ref[pl.ds(rows, META_ROWS), :] = tiled.astype(BF16)
    meta_ref[...] = tiled.astype(BF16)
    weight.wait()
    q_ref[...] = matmul(data, wq_ref[...]).astype(BF16)


def join_body(single_ref, meta_ref, out_ref):
    tokens, samples, _ = single_ref.shape
    rows = tokens * samples
    normed = normed_rows(single_ref[...])
    out_ref[pl.ds(0, rows), :] = matmul(sample_major(tokens, samples), normed).astype(BF16)
    out_ref[pl.ds(rows, META_ROWS), :] = meta_ref[...]
    meta_ref[...] = tiled.astype(BF16)
    weight.wait()
    q_ref[...] = matmul(data, wq_ref[...]).astype(BF16)


META_ROWS = 8
RADIX = 128


def prep_body(
    single_hbm, chain_hbm, residue_hbm, valid_hbm, wq_hbm, out_ref, meta_ref, q_ref,
    single_ref, ints_ref, wq_ref, sems,
):
    copies = [pltpu.make_async_copy(single_hbm, single_ref, sems.at[0])]
    for i, ref in enumerate((chain_hbm, residue_hbm, valid_hbm)):
        copies.append(pltpu.make_async_copy(ref, ints_ref.at[i], sems.at[i + 1]))
    weight = pltpu.make_async_copy(wq_hbm, wq_ref, sems.at[4])
    for copy in (*copies, weight):
        copy.start()
    tokens, samples, width = single_ref.shape
    rows = tokens * samples
    token = lax.broadcasted_iota(jnp.int32, (tokens, width), 0)
    lane = lax.broadcasted_iota(jnp.int32, (tokens, width), 1)
    spread = (lane % tokens == token).astype(F32).astype(BF16)
    perm = sample_major(tokens, samples)
    for copy in copies:
        copy.wait()
    data = matmul(perm, normed_rows(single_ref[...])).astype(BF16)
    out_ref[pl.ds(0, rows), :] = data
    residue = ints_ref[1]
    row = lax.broadcasted_iota(jnp.int32, (META_ROWS, tokens), 0)
    meta = jnp.where(row == 0, ints_ref[0], 0)
    meta = jnp.where(row == 1, residue // RADIX, meta)
    meta = jnp.where(row == 2, residue % RADIX, meta)
    meta = jnp.where(row == 3, ints_ref[2], meta)
    tiled = matmul(meta.astype(F32).astype(BF16), spread)
    out_ref[pl.ds(rows, META_ROWS), :] = tiled.astype(BF16)
    meta_ref[...] = tiled.astype(BF16)
    weight.wait()
    q_ref[...] = matmul(data, wq_ref[...]).astype(BF16)


def join_body(single_ref, meta_ref, out_ref):
    tokens, samples, _ = single_ref.shape
    rows = tokens * samples
    normed = normed_rows(single_ref[...])
    out_ref[pl.ds(0, rows), :] = matmul(sample_major(tokens, samples), normed).astype(BF16)
    out_ref[pl.ds(rows, META_ROWS), :] = meta_ref[...]


def spread_body(samples, heads, me_ref, q_ref, out_ref):
    spread_queries(samples, heads, q_ref, out_ref)


def pair_body(steps, chips, me_ref, pair_ref, wp_ref, *out_refs):
    pair_rows(steps, chips, me_ref[0], pair_ref, wp_ref[...], out_refs)


def gate_body(pay_ref, wg_ref, gate_ref):
    data = pay_ref[pl.ds(0, gate_ref.shape[0]), :]
    gate_ref[...] = jax.nn.sigmoid(matmul(data, wg_ref[...]))


def kv_body(*refs):
    wk_ref, wv_ref, out_ref = refs[-3:]
    blocks = refs[:-3]
    n = len(blocks)
    rows = blocks[0].shape[0] - META_ROWS
    parts = [b[pl.ds(0, rows), :] for b in blocks]
    data = jnp.concatenate(parts, axis=0) if n > 1 else parts[0]
    out_ref[pl.ds(0, n * rows), :] = matmul(data, wk_ref[...]).astype(BF16)
    out_ref[pl.ds(n * rows, n * rows), :] = matmul(data, wv_ref[...]).astype(BF16)
    for i, b in enumerate(blocks):
        out_ref[pl.ds(2 * n * rows + i * META_ROWS, META_ROWS), :] = b[pl.ds(rows, META_ROWS), :]


def ring_chip(place, chips):
    place = lax.rem(place + 2 * chips, chips)
    return jnp.where(place < chips // 2, 2 * place, 2 * (chips - 1 - place) + 1)


def pair_rows(steps, chips, me, pair_ref, weights, out_refs):
    queries, total, channels = pair_ref.shape
    heads = weights.shape[0]
    tokens = total // len(steps)
    chip = me // CORES
    core = lax.rem(me, CORES)
    place = jnp.where(lax.rem(chip, 2) == 0, chip // 2, chips - 1 - chip // 2)
    lines = heads * queries
    head = lax.broadcasted_iota(jnp.int32, (heads, lines), 0)
    lane = lax.broadcasted_iota(jnp.int32, (heads, lines), 1)
    spread = (lane // queries == head).astype(F32).astype(BF16)
    wide = lax.dot_general(weights, spread, (((0,), (0,)), ((), ())), preferred_element_type=F32)
    lane = lax.broadcasted_iota(jnp.int32, (channels, lines), 1) % queries
    wide = jnp.concatenate(
        [jnp.where(lane == i, wide, 0.0).astype(BF16) for i in range(queries)], axis=0
    )
    at = 0
    for out_ref in out_refs:
        data = []
        for r, c in steps[at : at + out_ref.shape[0] // tokens]:
            block = ring_chip(place + r, chips) * CORES + lax.rem(core + c, CORES)
            start = pl.multiple_of(block * tokens, tokens)
            rows = [pair_ref[i, pl.ds(start, tokens), :] for i in range(queries)]
            data.append(jnp.concatenate(rows, axis=1))
        at += len(data)
        out_ref[...] = matmul(jnp.concatenate(data, axis=0), wide)


def kv_count(ref, rows):
    return ref.shape[0] // (2 * rows + META_ROWS)


def kv_metas(kv_refs, rows):
    found = []
    for r in kv_refs:
        n = kv_count(r, rows)
        found += [r[pl.ds(2 * n * rows + u * META_ROWS, META_ROWS), :] for u in range(n)]
    return found


def full_bias(own, metas, tokens, pair_ref, tab_ref, pad_ref):
    total = pair_ref.shape[0]
    heads, bins = tab_ref.shape
    reach = (bins - 2) // 2
    wide = -(-total // LANES) * LANES
    slot = lax.broadcasted_iota(jnp.int32, (META_ROWS, wide), 1) // tokens
    keys = jnp.zeros((META_ROWS, wide), F32)
    for u, row in enumerate(metas):
        row = row.astype(F32)
        row = jnp.concatenate([row] * (-(-wide // row.shape[1])), axis=1)[:, :wide]
        keys = jnp.where(slot == u, row, keys)
    here = own.astype(F32)[:, :LANES]
    lane = lax.broadcasted_iota(jnp.int32, (tokens, LANES), 1)
    row = lax.broadcasted_iota(jnp.int32, (tokens, LANES), 0)

    def column(values):
        values = jnp.where(lane == row, jnp.broadcast_to(values, (tokens, LANES)), 0.0)
        return jnp.sum(values, axis=-1, keepdims=True)

    chain_q = column(here[0:1, :])
    res_q = column(here[1:2, :] * RADIX + here[2:3, :])
    res_keys = keys[1:2, :] * RADIX + keys[2:3, :]
    offset = jnp.clip(res_q - res_keys, -reach, reach) + reach
    bucket = jnp.where(chain_q == keys[0:1, :], offset, float(bins - 1)).astype(jnp.int32)
    mask = (keys[3:4, :] - 1.0) * MASK_PENALTY
    pad_ref[...] = jnp.zeros_like(pad_ref)
    pad_ref[:, pl.ds(0, bins)] = tab_ref[...]
    out = []
    for h in range(heads):
        table = jnp.broadcast_to(pad_ref[h : h + 1, :], (tokens, LANES))
        rel = [
            jnp.take_along_axis(
                table, bucket[:, at : at + LANES], axis=1, mode="promise_in_bounds"
            )
            for at in range(0, wide, LANES)
        ]
        out.append((jnp.concatenate(rel, axis=1) if len(rel) > 1 else rel[0]) + mask)
    return pair_ref[...] + jnp.transpose(jnp.concatenate(out, axis=0))[:total]


def head_windows(width, hs):
    windows, h = [], 0
    while h * hs < width:
        start = min(h * hs // LANES * LANES, width - TILE)
        last = min((start + TILE) // hs, width // hs) - 1
        windows.append((h, last, start))
        h = last + 1
    return windows


def spread_queries(samples, heads, q_ref, out_ref):
    rows, width = q_ref.shape
    tokens = rows // samples
    hs = width // heads
    lines = heads * tokens
    token = lax.broadcasted_iota(jnp.int32, (tokens, lines), 0)
    lane = lax.broadcasted_iota(jnp.int32, (tokens, lines), 1)
    spread = (lane % tokens == token).astype(F32).astype(BF16)
    feature = lax.broadcasted_iota(jnp.int32, (width, lines), 0)
    lane = lax.broadcasted_iota(jnp.int32, (width, lines), 1)
    inside = feature // hs == lane // tokens
    for s in range(samples):
        wide = lax.dot_general(
            q_ref[pl.ds(s * tokens, tokens), :], spread, (((0,), (0,)), ((), ())),
            preferred_element_type=F32,
        )
        out_ref[pl.ds(s * width, width), :] = jnp.where(inside, wide, 0.0).astype(BF16)


def gather(kv_refs, rows, at, tokens, values):
    found = []
    for r in kv_refs:
        n = kv_count(r, rows)
        first = n if values else 0
        found += [r[pl.ds((first + u) * rows + at, tokens), :] for u in range(n)]
    return found


def weights_body(samples, scale, more, *refs):
    exp_ref, top_ref, mass_ref, pad_ref = refs[-4:]
    q_ref, pair_ref, tab_ref, own_ref = refs[-8:-4]
    kv_refs = refs[:-8]
    if more:
        kv_refs, before_ref, mass_before_ref = refs[:-10], refs[-10], refs[-9]
    count, lines = pair_ref.shape
    tokens = lines // tab_ref.shape[0]
    rows = tokens * samples
    width = kv_refs[0].shape[1]
    metas = kv_metas(kv_refs, rows)
    bias = full_bias(own_ref[...], metas, tokens, pair_ref, tab_ref, pad_ref)
    for s in range(samples):
        here = pl.ds(s, 1)
        keys = jnp.concatenate(gather(kv_refs, rows, s * tokens, tokens, False), axis=0)
        scores = matmul(keys, q_ref[pl.ds(s * width, width), :]) * scale + bias
        top = jnp.max(scores, axis=0, keepdims=True)
        if more:
            top = jnp.maximum(top, before_ref[here, :])
        weights = jnp.exp(scores - top)
        mass = jnp.sum(weights, axis=0, keepdims=True)
        if more:
            mass = mass + mass_before_ref[here, :] * jnp.exp(before_ref[here, :] - top)
        top_ref[here, :] = top
        mass_ref[here, :] = mass
        exp_ref[pl.ds(s * count, count), :] = weights


def finish_body(heads, scale, split, *refs):
    (
        q_ref, gate_ref, exp_ref, top_ref, mass_ref, wk_ref, wv_ref, pair_ref, tab_ref, own_ref,
        single_ref, wo_ref, out_ref, pad_ref, weight_ref,
    ) = refs[-15:]
    kv_refs, lasts = refs[:-19], refs[-19:-15]
    tokens, samples, width = single_ref.shape
    rows = tokens * samples
    half = rows // 2
    hs = width // heads
    metas = kv_metas(kv_refs[split:], rows) + [r[pl.ds(half, META_ROWS), :] for r in (lasts[0], lasts[2])]
    data = jnp.concatenate([r[pl.ds(0, half), :] for r in lasts], axis=0)
    k_last = matmul(data, wk_ref[...]).astype(BF16)
    v_last = matmul(data, wv_ref[...]).astype(BF16)
    bias = full_bias(own_ref[...], metas, tokens, pair_ref, tab_ref, pad_ref)
    count = exp_ref.shape[0] // samples
    lane_head = lax.broadcasted_iota(jnp.int32, (tokens, width), 1) // hs
    lines = heads * tokens
    for s in range(samples):
        new = [slice(u * rows + s * tokens, u * rows + (s + 1) * tokens) for u in range(2)]
        keys = gather(kv_refs[split:], rows, s * tokens, tokens, False)
        keys = jnp.concatenate(keys + [k_last[n] for n in new], axis=0)
        scores = matmul(keys, q_ref[pl.ds(s * width, width), :]) * scale + bias
        before = top_ref[pl.ds(s, 1), :]
        top = jnp.maximum(jnp.max(scores, axis=0, keepdims=True), before)
        shrink = jnp.exp(before - top)
        late = jnp.exp(scores - top)
        mass = jnp.sum(late, axis=0, keepdims=True) + mass_ref[pl.ds(s, 1), :] * shrink
        inv = 1.0 / mass
        old = exp_ref[pl.ds(s * count, count), :] * (shrink * inv)
        weights = jnp.concatenate([old, late * inv], axis=0)
        weight_ref[pl.ds(s * lines, lines), :] = jnp.transpose(weights).astype(BF16)
    gated = []
    for s in range(samples):
        new = [slice(u * rows + s * tokens, u * rows + (s + 1) * tokens) for u in range(2)]
        values = gather(kv_refs, rows, s * tokens, tokens, True)
        values = jnp.concatenate(values + [v_last[n] for n in new], axis=0)
        pieces = {}
        for h0, h1, start in head_windows(width, hs):
            here = pl.ds(s * lines + h0 * tokens, (h1 + 1 - h0) * tokens)
            ot = matmul(weight_ref[here, :], values[:, start : start + TILE])
            for first in range(start, start + TILE, LANES):
                for h in range(h0, h1 + 1):
                    if (h + 1) * hs <= first or h * hs >= first + LANES:
                        continue
                    lanes = slice(first - start, first - start + LANES)
                    part = ot[(h - h0) * tokens : (h + 1 - h0) * tokens, lanes]
                    if first in pieces:
                        mine = lane_head[:, first : first + LANES] == h
                        part = jnp.where(mine, part, pieces[first])
                    pieces[first] = part
        attended = jnp.concatenate([pieces[at] for at in sorted(pieces)], axis=1)
        gated.append((gate_ref[pl.ds(s * tokens, tokens), :] * attended).astype(BF16))
    gated = matmul(token_major(tokens, samples), jnp.concatenate(gated, axis=0)).astype(BF16)
    out = matmul(gated, wo_ref[...]).reshape(tokens, samples, width)
    out_ref[...] = (single_ref[...].astype(F32) + out).astype(BF16)


def call(body, out_shape, args, in_specs=None, flops=0, moved=0, limit=8 << 20, scratch=()):
    return pl.pallas_call(
        body,
        out_shape=out_shape,
        in_specs=in_specs or [VMEM] * len(args),
        out_specs=jax.tree.map(lambda _: VMEM, out_shape),
        scratch_shapes=scratch,
        compiler_params=pltpu.CompilerParams(vmem_limit_bytes=limit),
        cost_estimate=pl.CostEstimate(flops=flops, bytes_accessed=moved, transcendentals=0),
    )(*args)


def shards(
    single, pair, chain, residue, valid, w_query, w_key, w_value, w_gate, w_out, w_pair, rel_table
):
    tokens, samples, width = single.shape
    heads = w_pair.shape[1]
    total = pair.shape[1]
    rows = tokens * samples
    devices = lax.axis_size("tok")
    chips = devices // CORES
    half = chips // 2
    order = list(range(0, chips, 2)) + list(range(1, chips, 2))[::-1]
    me = lax.axis_index("tok").astype(jnp.int32).reshape(1)

    def ring(value, step):
        pairs = [
            (order[i] * CORES + c, order[(i + step) % chips] * CORES + c)
            for i in range(chips)
            for c in range(CORES)
        ]
        return lax.ppermute(value, "tok", pairs)

    def flip(value):
        return lax.ppermute(value, "tok", [(d, d ^ 1) for d in range(devices)])

    steps = [(0, 0), (0, 1)]
    for k in range(1, half):
        steps += [(-k, 0), (k, 0), (-k, 1), (k, 1)]
    steps += [(half, 0), (half, 1)]

    cw = ring(single, 1)
    ccw = ring(single, -1)
    blocks = jax.ShapeDtypeStruct((rows + META_ROWS, width), BF16)
    payload, meta, query = call(
        prep_body,
        (
            blocks,
            jax.ShapeDtypeStruct((META_ROWS, width), BF16),
            jax.ShapeDtypeStruct((rows, width), BF16),
        ),
        (single, *(v.reshape(1, tokens) for v in (chain, residue, valid)), w_query),
        in_specs=[ANY] * 5,
        scratch=[
            pltpu.VMEM(single.shape, BF16),
            pltpu.VMEM((3, 1, tokens), jnp.int32),
            pltpu.VMEM((width, width), BF16),
            pltpu.SemaphoreType.DMA((5,)),
        ],
        flops=2 * rows * width * width,
        moved=6 * rows * width + 2 * width * width,
        limit=FULL,
    )
    cw_meta = ring(meta, 1)
    ccw_meta = ring(meta, -1)
    lines = heads * tokens
    query = call(
        functools.partial(spread_body, samples, heads),
        jax.ShapeDtypeStruct((samples * width, lines), BF16),
        (me, query),
        in_specs=[SMEM, VMEM],
        flops=2 * rows * width * lines,
        moved=2 * samples * width * lines,
    )
    gate = call(
        gate_body,
        jax.ShapeDtypeStruct((rows, width), F32),
        (payload, w_gate),
        flops=2 * rows * width * width,
        moved=2 * width * width + 6 * rows * width,
    )

    def join(value, extra):
        return call(join_body, blocks, (value, extra), moved=4 * rows * width)

    cw = join(cw, cw_meta)
    ccw = join(ccw, ccw_meta)

    def kv(parts):
        n = len(parts)
        return call(
            kv_body,
            jax.ShapeDtypeStruct((n * (2 * rows + META_ROWS), width), BF16),
            (*parts, w_key, w_value),
            flops=4 * n * rows * width * width,
            moved=4 * width * width + 6 * n * rows * width,
        )

    def piece(value, at, meta):
        count = rows // 2 + (META_ROWS if meta else 0)

        def body(in_ref, out_ref):
            out_ref[pl.ds(0, rows // 2), :] = in_ref[pl.ds(at, rows // 2), :]
            if meta:
                out_ref[pl.ds(rows // 2, META_ROWS), :] = in_ref[pl.ds(rows, META_ROWS), :]

        shape = jax.ShapeDtypeStruct((count, width), BF16)
        return call(body, shape, (value,), moved=2 * rows * width)

    sizes = [len(steps) - 3 * CORES, 3 * CORES]
    pair_bias = call(
        functools.partial(pair_body, steps, chips),
        tuple(jax.ShapeDtypeStruct((n * tokens, lines), F32) for n in sizes),
        (me, pair, w_pair.T),
        in_specs=[SMEM, VMEM, VMEM],
        flops=2 * pair.size * lines,
        moved=2 * pair.size + 4 * total * lines,
        limit=(6 << 20) + 4 * pair.size,
    )
    kvs = [kv([payload])]
    kvs.append(flip(kvs[-1]))
    for k in range(1, half):
        if k + 1 < half:
            cw_next = ring(cw, 1)
            ccw_next = ring(ccw, -1)
        else:
            cw_next = ring(piece(cw, 0, True), 1)
            ccw_next = ring(piece(ccw, rows // 2, False), -1)
        kvs.append(kv([cw, ccw]))
        kvs.append(flip(kvs[-1]))
        cw, ccw = cw_next, ccw_next
    scale = 1.0 / math.sqrt(width // heads)
    state = jax.ShapeDtypeStruct((samples, lines), F32)
    table = rel_table.T
    pad = [pltpu.VMEM((heads, LANES), F32)]
    limit = (10 << 20) + 4 * samples * total * width

    split = 2 * (half - 1)
    keys = sizes[0] * tokens
    first = call(
        functools.partial(weights_body, samples, scale, False),
        (jax.ShapeDtypeStruct((samples * keys, lines), F32), state, state),
        (*kvs[:split], query, pair_bias[0], table, meta),
        flops=2 * samples * keys * width * lines,
        moved=6 * samples * keys * width,
        limit=limit,
        scratch=pad,
    )
    cw_other, ccw_other = flip(cw), flip(ccw)
    return call(
        functools.partial(finish_body, heads, scale, split),
        jax.ShapeDtypeStruct(single.shape, BF16),
        (
            *kvs, cw, ccw, cw_other, ccw_other, query, gate, *first, w_key, w_value,
            pair_bias[1], table, meta, single, w_out,
        ),
        flops=4 * rows * total * width,
        moved=2 * samples * total * width,
        limit=limit,
        scratch=[*pad, pltpu.VMEM((samples * lines, total), BF16)],
    )


def solution(mesh):
    placed = (
        P(("groups", "tok"), None, None),
        P(("groups", "tok"), None, None),
        P(("groups", "tok")),
        P(("groups", "tok")),
        P(("groups", "tok")),
        P(),
        P(),
        P(),
        P(),
        P(),
        P(),
        P(),
    )

    step = jax.shard_map(
        shards,
        mesh=mesh,
        in_specs=placed,
        out_specs=P(("groups", "tok"), None, None),
        check_vma=False,
    )
    return step
    return step
    return step
    return step
```

```python
import functools
import math

import jax
import jax.numpy as jnp
from jax import lax
from jax.experimental import pallas as pl
from jax.experimental.pallas import tpu as pltpu
from jax.sharding import PartitionSpec as P


NORM_EPS = 1e-05
MASK_PENALTY = 10000.0
F32 = jnp.float32
BF16 = jnp.bfloat16
CORES = 2
TILE = 256
LANES = 128
META_ROWS = 8
RADIX = 128
FULL = 60 << 20
VMEM = pl.BlockSpec(memory_space=pltpu.VMEM)
ANY = pl.BlockSpec(memory_space=pl.ANY)
SMEM = pl.BlockSpec(memory_space=pltpu.SMEM)


def normed_rows(block):
    tokens, samples, width = block.shape
    values = block.astype(F32).reshape(tokens * samples, width)
    centred = values - jnp.mean(values, axis=-1, keepdims=True)
    spread = jnp.mean(centred * centred, axis=-1, keepdims=True)
    return (centred * lax.rsqrt(spread + NORM_EPS)).astype(BF16)


def sample_major(tokens, samples):
    rows = tokens * samples
    to = lax.broadcasted_iota(jnp.int32, (rows, rows), 0)
    frm = lax.broadcasted_iota(jnp.int32, (rows, rows), 1)
    want = (to % tokens) * samples + to // tokens
    return (want == frm).astype(F32).astype(BF16)


def token_major(tokens, samples):
    rows = tokens * samples
    to = lax.broadcasted_iota(jnp.int32, (rows, rows), 0)
    frm = lax.broadcasted_iota(jnp.int32, (rows, rows), 1)
    want = (to % samples) * tokens + to // samples
    return (want == frm).astype(F32).astype(BF16)


def matmul(a, b):
    return jnp.dot(a, b, preferred_element_type=F32)


def tags_body(chain_hbm, residue_hbm, valid_hbm, out_ref, ints_ref, sems):
    copies = []
    for i, ref in enumerate((chain_hbm, residue_hbm, valid_hbm)):
        copies.append(pltpu.make_async_copy(ref, ints_ref.at[i], sems.at[i]))
        copies[i].start()
    tokens, width = ints_ref.shape[2], out_ref.shape[1]
    token = lax.broadcasted_iota(jnp.int32, (tokens, width), 0)
    lane = lax.broadcasted_iota(jnp.int32, (tokens, width), 1)
    spread = (lane % tokens == token).astype(F32).astype(BF16)
    for copy in copies:
        copy.wait()
    residue = ints_ref[1]
    row = lax.broadcasted_iota(jnp.int32, (META_ROWS, tokens), 0)
    meta = jnp.where(row == 0, ints_ref[0], 0)
    meta = jnp.where(row == 1, residue // RADIX, meta)
    meta = jnp.where(row == 2, residue % RADIX, meta)
    meta = jnp.where(row == 3, ints_ref[2], meta)
    out_ref[...] = matmul(meta.astype(F32).astype(BF16), spread).astype(BF16)


def prep_body(
    single_hbm, meta_hbm, wq_hbm, out_ref, q_ref, single_ref, meta_ref, wq_ref, sems
):
    copies = []
    moves = ((single_hbm, single_ref), (meta_hbm, meta_ref), (wq_hbm, wq_ref))
    for i, (source, target) in enumerate(moves):
        copies.append(pltpu.make_async_copy(source, target, sems.at[i]))
        copies[i].start()
    tokens, samples, _ = single_ref.shape
    rows = tokens * samples
    perm = sample_major(tokens, samples)
    copies[0].wait()
    data = matmul(perm, normed_rows(single_ref[...])).astype(BF16)
    out_ref[pl.ds(0, rows), :] = data
    copies[1].wait()
    out_ref[pl.ds(rows, META_ROWS), :] = meta_ref[...]
    copies[2].wait()
    q_ref[...] = matmul(data, wq_ref[...]).astype(BF16)


def join_body(single_ref, meta_ref, out_ref):
    tokens, samples, _ = single_ref.shape
    rows = tokens * samples
    normed = normed_rows(single_ref[...])
    out_ref[pl.ds(0, rows), :] = matmul(sample_major(tokens, samples), normed).astype(BF16)
    out_ref[pl.ds(rows, META_ROWS), :] = meta_ref[...]


def spread_body(samples, heads, me_ref, q_ref, out_ref):
    spread_queries(samples, heads, q_ref, out_ref)


def pair_body(steps, chips, me_ref, pair_ref, wp_ref, *out_refs):
    pair_rows(steps, chips, me_ref[0], pair_ref, wp_ref[...], out_refs)


def gate_body(pay_ref, wg_ref, gate_ref):
    data = pay_ref[pl.ds(0, gate_ref.shape[0]), :]
    gate_ref[...] = jax.nn.sigmoid(matmul(data, wg_ref[...]))


def kv_body(*refs):
    wk_ref, wv_ref, out_ref = refs[-3:]
    blocks = refs[:-3]
    n = len(blocks)
    rows = blocks[0].shape[0] - META_ROWS
    parts = [b[pl.ds(0, rows), :] for b in blocks]
    data = jnp.concatenate(parts, axis=0) if n > 1 else parts[0]
    out_ref[pl.ds(0, n * rows), :] = matmul(data, wk_ref[...]).astype(BF16)
    out_ref[pl.ds(n * rows, n * rows), :] = matmul(data, wv_ref[...]).astype(BF16)
    for i, b in enumerate(blocks):
        out_ref[pl.ds(2 * n * rows + i * META_ROWS, META_ROWS), :] = b[pl.ds(rows, META_ROWS), :]


def ring_chip(place, chips):
    place = lax.rem(place + 2 * chips, chips)
    return jnp.where(place < chips // 2, 2 * place, 2 * (chips - 1 - place) + 1)


def pair_rows(steps, chips, me, pair_ref, weights, out_refs):
    queries, total, channels = pair_ref.shape
    heads = weights.shape[0]
    tokens = total // len(steps)
    chip = me // CORES
    core = lax.rem(me, CORES)
    place = jnp.where(lax.rem(chip, 2) == 0, chip // 2, chips - 1 - chip // 2)
    lines = heads * queries
    head = lax.broadcasted_iota(jnp.int32, (heads, lines), 0)
    lane = lax.broadcasted_iota(jnp.int32, (heads, lines), 1)
    spread = (lane // queries == head).astype(F32).astype(BF16)
    wide = lax.dot_general(weights, spread, (((0,), (0,)), ((), ())), preferred_element_type=F32)
    lane = lax.broadcasted_iota(jnp.int32, (channels, lines), 1) % queries
    wide = jnp.concatenate(
        [jnp.where(lane == i, wide, 0.0).astype(BF16) for i in range(queries)], axis=0
    )
    at = 0
    for out_ref in out_refs:
        data = []
        for r, c in steps[at : at + out_ref.shape[0] // tokens]:
            block = ring_chip(place + r, chips) * CORES + lax.rem(core + c, CORES)
            start = pl.multiple_of(block * tokens, tokens)
            rows = [pair_ref[i, pl.ds(start, tokens), :] for i in range(queries)]
            data.append(jnp.concatenate(rows, axis=1))
        at += len(data)
        out_ref[...] = matmul(jnp.concatenate(data, axis=0), wide)


def kv_count(ref, rows):
    return ref.shape[0] // (2 * rows + META_ROWS)


def kv_metas(kv_refs, rows):
    found = []
    for r in kv_refs:
        n = kv_count(r, rows)
        found += [r[pl.ds(2 * n * rows + u * META_ROWS, META_ROWS), :] for u in range(n)]
    return found


def full_bias(own, metas, tokens, pair_ref, tab_ref, pad_ref):
    total = pair_ref.shape[0]
    heads, bins = tab_ref.shape
    reach = (bins - 2) // 2
    wide = -(-total // LANES) * LANES
    slot = lax.broadcasted_iota(jnp.int32, (META_ROWS, wide), 1) // tokens
    keys = jnp.zeros((META_ROWS, wide), F32)
    for u, row in enumerate(metas):
        row = row.astype(F32)
        row = jnp.concatenate([row] * (-(-wide // row.shape[1])), axis=1)[:, :wide]
        keys = jnp.where(slot == u, row, keys)
    here = own.astype(F32)[:, :LANES]
    lane = lax.broadcasted_iota(jnp.int32, (tokens, LANES), 1)
    row = lax.broadcasted_iota(jnp.int32, (tokens, LANES), 0)

    def column(values):
        values = jnp.where(lane == row, jnp.broadcast_to(values, (tokens, LANES)), 0.0)
        return jnp.sum(values, axis=-1, keepdims=True)

    chain_q = column(here[0:1, :])
    res_q = column(here[1:2, :] * RADIX + here[2:3, :])
    res_keys = keys[1:2, :] * RADIX + keys[2:3, :]
    offset = jnp.clip(res_q - res_keys, -reach, reach) + reach
    bucket = jnp.where(chain_q == keys[0:1, :], offset, float(bins - 1)).astype(jnp.int32)
    mask = (keys[3:4, :] - 1.0) * MASK_PENALTY
    pad_ref[...] = jnp.zeros_like(pad_ref)
    pad_ref[:, pl.ds(0, bins)] = tab_ref[...]
    out = []
    for h in range(heads):
        table = jnp.broadcast_to(pad_ref[h : h + 1, :], (tokens, LANES))
        rel = [
            jnp.take_along_axis(
                table, bucket[:, at : at + LANES], axis=1, mode="promise_in_bounds"
            )
            for at in range(0, wide, LANES)
        ]
        out.append((jnp.concatenate(rel, axis=1) if len(rel) > 1 else rel[0]) + mask)
    return pair_ref[...] + jnp.transpose(jnp.concatenate(out, axis=0))[:total]


def head_windows(width, hs):
    windows, h = [], 0
    while h * hs < width:
        start = min(h * hs // LANES * LANES, width - TILE)
        last = min((start + TILE) // hs, width // hs) - 1
        windows.append((h, last, start))
        h = last + 1
    return windows


def spread_queries(samples, heads, q_ref, out_ref):
    rows, width = q_ref.shape
    tokens = rows // samples
    hs = width // heads
    lines = heads * tokens
    token = lax.broadcasted_iota(jnp.int32, (tokens, lines), 0)
    lane = lax.broadcasted_iota(jnp.int32, (tokens, lines), 1)
    spread = (lane % tokens == token).astype(F32).astype(BF16)
    feature = lax.broadcasted_iota(jnp.int32, (width, lines), 0)
    lane = lax.broadcasted_iota(jnp.int32, (width, lines), 1)
    inside = feature // hs == lane // tokens
    for s in range(samples):
        wide = lax.dot_general(
            q_ref[pl.ds(s * tokens, tokens), :], spread, (((0,), (0,)), ((), ())),
            preferred_element_type=F32,
        )
        out_ref[pl.ds(s * width, width), :] = jnp.where(inside, wide, 0.0).astype(BF16)


def gather(kv_refs, rows, at, tokens, values):
    found = []
    for r in kv_refs:
        n = kv_count(r, rows)
        first = n if values else 0
        found += [r[pl.ds((first + u) * rows + at, tokens), :] for u in range(n)]
    return found


def weights_body(samples, scale, more, *refs):
    exp_ref, top_ref, mass_ref, pad_ref = refs[-4:]
    q_ref, pair_ref, tab_ref, own_ref = refs[-8:-4]
    kv_refs = refs[:-8]
    if more:
        kv_refs, before_ref, mass_before_ref = refs[:-10], refs[-10], refs[-9]
    count, lines = pair_ref.shape
    tokens = lines // tab_ref.shape[0]
    rows = tokens * samples
    width = kv_refs[0].shape[1]
    metas = kv_metas(kv_refs, rows)
    bias = full_bias(own_ref[...], metas, tokens, pair_ref, tab_ref, pad_ref)
    for s in range(samples):
        here = pl.ds(s, 1)
        keys = jnp.concatenate(gather(kv_refs, rows, s * tokens, tokens, False), axis=0)
        scores = matmul(keys, q_ref[pl.ds(s * width, width), :]) * scale + bias
        top = jnp.max(scores, axis=0, keepdims=True)
        if more:
            top = jnp.maximum(top, before_ref[here, :])
        weights = jnp.exp(scores - top)
        mass = jnp.sum(weights, axis=0, keepdims=True)
        if more:
            mass = mass + mass_before_ref[here, :] * jnp.exp(before_ref[here, :] - top)
        top_ref[here, :] = top
        mass_ref[here, :] = mass
        exp_ref[pl.ds(s * count, count), :] = weights


def finish_body(heads, scale, split, *refs):
    (
        q_ref, gate_ref, exp_ref, top_ref, mass_ref, wk_ref, wv_ref, pair_ref, tab_ref, own_ref,
        single_ref, wo_ref, out_ref, pad_ref, weight_ref,
    ) = refs[-15:]
    kv_refs, lasts = refs[:-19], refs[-19:-15]
    tokens, samples, width = single_ref.shape
    rows = tokens * samples
    hs = width // heads
    share = lasts[0].shape[0] - META_ROWS
    metas = kv_metas(kv_refs[split:], rows) + [r[pl.ds(share, META_ROWS), :] for r in (lasts[0], lasts[2])]
    sizes = (share, rows - share) * 2
    data = jnp.concatenate([r[pl.ds(0, n), :] for r, n in zip(lasts, sizes)], axis=0)
    k_last = matmul(data, wk_ref[...]).astype(BF16)
    v_last = matmul(data, wv_ref[...]).astype(BF16)
    bias = full_bias(own_ref[...], metas, tokens, pair_ref, tab_ref, pad_ref)
    count = exp_ref.shape[0] // samples
    lane_head = lax.broadcasted_iota(jnp.int32, (tokens, width), 1) // hs
    lines = heads * tokens
    for s in range(samples):
        new = [slice(u * rows + s * tokens, u * rows + (s + 1) * tokens) for u in range(2)]
        keys = gather(kv_refs[split:], rows, s * tokens, tokens, False)
        keys = jnp.concatenate(keys + [k_last[n] for n in new], axis=0)
        scores = matmul(keys, q_ref[pl.ds(s * width, width), :]) * scale + bias
        before = top_ref[pl.ds(s, 1), :]
        top = jnp.maximum(jnp.max(scores, axis=0, keepdims=True), before)
        shrink = jnp.exp(before - top)
        late = jnp.exp(scores - top)
        mass = jnp.sum(late, axis=0, keepdims=True) + mass_ref[pl.ds(s, 1), :] * shrink
        inv = 1.0 / mass
        old = exp_ref[pl.ds(s * count, count), :] * (shrink * inv)
        weights = jnp.concatenate([old, late * inv], axis=0)
        weight_ref[pl.ds(s * lines, lines), :] = jnp.transpose(weights).astype(BF16)
    gated = []
    for s in range(samples):
        new = [slice(u * rows + s * tokens, u * rows + (s + 1) * tokens) for u in range(2)]
        values = gather(kv_refs, rows, s * tokens, tokens, True)
        values = jnp.concatenate(values + [v_last[n] for n in new], axis=0)
        pieces = {}
        for h0, h1, start in head_windows(width, hs):
            here = pl.ds(s * lines + h0 * tokens, (h1 + 1 - h0) * tokens)
            ot = matmul(weight_ref[here, :], values[:, start : start + TILE])
            for first in range(start, start + TILE, LANES):
                for h in range(h0, h1 + 1):
                    if (h + 1) * hs <= first or h * hs >= first + LANES:
                        continue
                    lanes = slice(first - start, first - start + LANES)
                    part = ot[(h - h0) * tokens : (h + 1 - h0) * tokens, lanes]
                    if first in pieces:
                        mine = lane_head[:, first : first + LANES] == h
                        part = jnp.where(mine, part, pieces[first])
                    pieces[first] = part
        attended = jnp.concatenate([pieces[at] for at in sorted(pieces)], axis=1)
        gated.append((gate_ref[pl.ds(s * tokens, tokens), :] * attended).astype(BF16))
    gated = matmul(token_major(tokens, samples), jnp.concatenate(gated, axis=0)).astype(BF16)
    out = matmul(gated, wo_ref[...]).reshape(tokens, samples, width)
    out_ref[...] = (single_ref[...].astype(F32) + out).astype(BF16)


def call(body, out_shape, args, in_specs=None, flops=0, moved=0, limit=8 << 20, scratch=()):
    return pl.pallas_call(
        body,
        out_shape=out_shape,
        in_specs=in_specs or [VMEM] * len(args),
        out_specs=jax.tree.map(lambda _: VMEM, out_shape),
        scratch_shapes=scratch,
        compiler_params=pltpu.CompilerParams(vmem_limit_bytes=limit),
        cost_estimate=pl.CostEstimate(flops=flops, bytes_accessed=moved, transcendentals=0),
    )(*args)


def shards(
    single, pair, chain, residue, valid, w_query, w_key, w_value, w_gate, w_out, w_pair, rel_table
):
    tokens, samples, width = single.shape
    heads = w_pair.shape[1]
    total = pair.shape[1]
    rows = tokens * samples
    devices = lax.axis_size("tok")
    chips = devices // CORES
    half = chips // 2
    order = list(range(0, chips, 2)) + list(range(1, chips, 2))[::-1]
    me = lax.axis_index("tok").astype(jnp.int32).reshape(1)

    def ring(value, step):
        pairs = [
            (order[i] * CORES + c, order[(i + step) % chips] * CORES + c)
            for i in range(chips)
            for c in range(CORES)
        ]
        return lax.ppermute(value, "tok", pairs)

    def flip(value):
        return lax.ppermute(value, "tok", [(d, d ^ 1) for d in range(devices)])

    steps = [(0, 0), (0, 1)]
    for k in range(1, half):
        steps += [(-k, 0), (k, 0), (-k, 1), (k, 1)]
    steps += [(half, 0), (half, 1)]

    cw = ring(single, 1)
    ccw = ring(single, -1)
    blocks = jax.ShapeDtypeStruct((rows + META_ROWS, width), BF16)
    meta = call(
        tags_body,
        jax.ShapeDtypeStruct((META_ROWS, width), BF16),
        tuple(v.reshape(1, tokens) for v in (chain, residue, valid)),
        in_specs=[ANY] * 3,
        scratch=[pltpu.VMEM((3, 1, tokens), jnp.int32), pltpu.SemaphoreType.DMA((3,))],
        moved=2 * META_ROWS * width,
        limit=FULL,
    )
    payload, query = call(
        prep_body,
        (blocks, jax.ShapeDtypeStruct((rows, width), BF16)),
        (single, meta, w_query),
        in_specs=[ANY] * 3,
        scratch=[
            pltpu.VMEM(single.shape, BF16),
            pltpu.VMEM(meta.shape, BF16),
            pltpu.VMEM((width, width), BF16),
            pltpu.SemaphoreType.DMA((3,)),
        ],
        flops=2 * rows * width * width,
        moved=6 * rows * width + 2 * width * width,
        limit=FULL,
    )
    cw_meta = ring(meta, 1)
    ccw_meta = ring(meta, -1)
    lines = heads * tokens
    query = call(
        functools.partial(spread_body, samples, heads),
        jax.ShapeDtypeStruct((samples * width, lines), BF16),
        (me, query),
        in_specs=[SMEM, VMEM],
        flops=2 * rows * width * lines,
        moved=2 * samples * width * lines,
    )
    gate = call(
        gate_body,
        jax.ShapeDtypeStruct((rows, width), F32),
        (payload, w_gate),
        flops=2 * rows * width * width,
        moved=2 * width * width + 6 * rows * width,
    )

    def join(value, extra):
        return call(join_body, blocks, (value, extra), moved=4 * rows * width)

    cw = join(cw, cw_meta)
    ccw = join(ccw, ccw_meta)

    def kv(parts):
        n = len(parts)
        return call(
            kv_body,
            jax.ShapeDtypeStruct((n * (2 * rows + META_ROWS), width), BF16),
            (*parts, w_key, w_value),
            flops=4 * n * rows * width * width,
            moved=4 * width * width + 6 * n * rows * width,
        )

    def piece(value, at, size, meta):
        count = size + (META_ROWS if meta else 0)

        def body(in_ref, out_ref):
            out_ref[pl.ds(0, size), :] = in_ref[pl.ds(at, size), :]
            if meta:
                out_ref[pl.ds(size, META_ROWS), :] = in_ref[pl.ds(rows, META_ROWS), :]

        shape = jax.ShapeDtypeStruct((count, width), BF16)
        return call(body, shape, (value,), moved=2 * rows * width)

    sizes = [len(steps) - 3 * CORES, 3 * CORES]
    pair_bias = call(
        functools.partial(pair_body, steps, chips),
        tuple(jax.ShapeDtypeStruct((n * tokens, lines), F32) for n in sizes),
        (me, pair, w_pair.T),
        in_specs=[SMEM, VMEM, VMEM],
        flops=2 * pair.size * lines,
        moved=2 * pair.size + 4 * total * lines,
        limit=(6 << 20) + 4 * pair.size,
    )
    share = samples * 3 // 4 * tokens
    kvs = [kv([payload])]
    kvs.append(flip(kvs[-1]))
    for k in range(1, half):
        if k + 1 < half:
            cw_next = ring(cw, 1)
            ccw_next = ring(ccw, -1)
        else:
            cw_next = ring(piece(cw, 0, share, True), 1)
            ccw_next = ring(piece(ccw, share, rows - share, False), -1)
        kvs.append(kv([cw, ccw]))
        kvs.append(flip(kvs[-1]))
        cw, ccw = cw_next, ccw_next
    scale = 1.0 / math.sqrt(width // heads)
    state = jax.ShapeDtypeStruct((samples, lines), F32)
    table = rel_table.T
    pad = [pltpu.VMEM((heads, LANES), F32)]
    limit = (10 << 20) + 4 * samples * total * width

    split = 2 * (half - 1)
    keys = sizes[0] * tokens
    first = call(
        functools.partial(weights_body, samples, scale, False),
        (jax.ShapeDtypeStruct((samples * keys, lines), F32), state, state),
        (*kvs[:split], query, pair_bias[0], table, meta),
        flops=2 * samples * keys * width * lines,
        moved=6 * samples * keys * width,
        limit=limit,
        scratch=pad,
    )
    cw_other, ccw_other = flip(cw), flip(ccw)
    return call(
        functools.partial(finish_body, heads, scale, split),
        jax.ShapeDtypeStruct(single.shape, BF16),
        (
            *kvs, cw, ccw, cw_other, ccw_other, query, gate, *first, w_key, w_value,
            pair_bias[1], table, meta, single, w_out,
        ),
        flops=4 * rows * total * width,
        moved=2 * samples * total * width,
        limit=limit,
        scratch=[*pad, pltpu.VMEM((samples * lines, total), BF16)],
    )


def solution(mesh):
    placed = (
        P(("groups", "tok"), None, None),
        P(("groups", "tok"), None, None),
        P(("groups", "tok")),
        P(("groups", "tok")),
        P(("groups", "tok")),
        P(),
        P(),
        P(),
        P(),
        P(),
        P(),
        P(),
    )

    return jax.shard_map(
        shards,
        mesh=mesh,
        in_specs=placed,
        out_specs=P(("groups", "tok"), None, None),
        check_vma=False,
    )
```

```python
import functools
import math

import jax
import jax.numpy as jnp
from jax import lax
from jax.experimental import pallas as pl
from jax.experimental.pallas import tpu as pltpu
from jax.sharding import PartitionSpec as P


NORM_EPS = 1e-05
MASK_PENALTY = 10000.0
F32 = jnp.float32
BF16 = jnp.bfloat16
CORES = 2
TILE = 256
LANES = 128
META_ROWS = 8
RADIX = 128
FULL = 60 << 20
VMEM = pl.BlockSpec(memory_space=pltpu.VMEM)
ANY = pl.BlockSpec(memory_space=pl.ANY)
SMEM = pl.BlockSpec(memory_space=pltpu.SMEM)


def normed_rows(block):
    tokens, samples, width = block.shape
    values = block.astype(F32).reshape(tokens * samples, width)
    centred = values - jnp.mean(values, axis=-1, keepdims=True)
    spread = jnp.mean(centred * centred, axis=-1, keepdims=True)
    return (centred * lax.rsqrt(spread + NORM_EPS)).astype(BF16)


def sample_major(tokens, samples):
    rows = tokens * samples
    to = lax.broadcasted_iota(jnp.int32, (rows, rows), 0)
    frm = lax.broadcasted_iota(jnp.int32, (rows, rows), 1)
    want = (to % tokens) * samples + to // tokens
    return (want == frm).astype(F32).astype(BF16)


def token_major(tokens, samples):
    rows = tokens * samples
    to = lax.broadcasted_iota(jnp.int32, (rows, rows), 0)
    frm = lax.broadcasted_iota(jnp.int32, (rows, rows), 1)
    want = (to % samples) * tokens + to // samples
    return (want == frm).astype(F32).astype(BF16)


def matmul(a, b):
    return jnp.dot(a, b, preferred_element_type=F32)


def prep_body(
    single_hbm, chain_hbm, residue_hbm, valid_hbm, wq_hbm, out_ref, meta_ref, q_ref,
    single_ref, ints_ref, wq_ref, sems,
):
    copies = [pltpu.make_async_copy(single_hbm, single_ref, sems.at[0])]
    for i, ref in enumerate((chain_hbm, residue_hbm, valid_hbm)):
        copies.append(pltpu.make_async_copy(ref, ints_ref.at[i], sems.at[i + 1]))
    weight = pltpu.make_async_copy(wq_hbm, wq_ref, sems.at[4])
    for copy in (*copies, weight):
        copy.start()
    tokens, samples, width = single_ref.shape
    rows = tokens * samples
    token = lax.broadcasted_iota(jnp.int32, (tokens, width), 0)
    lane = lax.broadcasted_iota(jnp.int32, (tokens, width), 1)
    spread = (lane % tokens == token).astype(F32).astype(BF16)
    perm = sample_major(tokens, samples)
    for copy in copies:
        copy.wait()
    data = matmul(perm, normed_rows(single_ref[...])).astype(BF16)
    out_ref[pl.ds(0, rows), :] = data
    residue = ints_ref[1]
    row = lax.broadcasted_iota(jnp.int32, (META_ROWS, tokens), 0)
    meta = jnp.where(row == 0, ints_ref[0], 0)
    meta = jnp.where(row == 1, residue // RADIX, meta)
    meta = jnp.where(row == 2, residue % RADIX, meta)
    meta = jnp.where(row == 3, ints_ref[2], meta)
    tiled = matmul(meta.astype(F32).astype(BF16), spread)
    out_ref[pl.ds(rows, META_ROWS), :] = tiled.astype(BF16)
    meta_ref[...] = tiled.astype(BF16)
    weight.wait()
    q_ref[...] = matmul(data, wq_ref[...]).astype(BF16)


def join_body(single_ref, meta_ref, out_ref):
    tokens, samples, _ = single_ref.shape
    rows = tokens * samples
    normed = normed_rows(single_ref[...])
    out_ref[pl.ds(0, rows), :] = matmul(sample_major(tokens, samples), normed).astype(BF16)
    out_ref[pl.ds(rows, META_ROWS), :] = meta_ref[...]


def spread_body(samples, heads, me_ref, q_ref, out_ref):
    spread_queries(samples, heads, q_ref, out_ref)


def pair_body(steps, chips, me_ref, pair_ref, wp_ref, *out_refs):
    pair_rows(steps, chips, me_ref[0], pair_ref, wp_ref[...], out_refs)


def gate_body(pay_ref, wg_ref, gate_ref):
    data = pay_ref[pl.ds(0, gate_ref.shape[0]), :]
    gate_ref[...] = jax.nn.sigmoid(matmul(data, wg_ref[...]))


def kv_body(*refs):
    wk_ref, wv_ref, out_ref = refs[-3:]
    blocks = refs[:-3]
    n = len(blocks)
    rows = blocks[0].shape[0] - META_ROWS
    parts = [b[pl.ds(0, rows), :] for b in blocks]
    data = jnp.concatenate(parts, axis=0) if n > 1 else parts[0]
    out_ref[pl.ds(0, n * rows), :] = matmul(data, wk_ref[...]).astype(BF16)
    out_ref[pl.ds(n * rows, n * rows), :] = matmul(data, wv_ref[...]).astype(BF16)
    for i, b in enumerate(blocks):
        out_ref[pl.ds(2 * n * rows + i * META_ROWS, META_ROWS), :] = b[pl.ds(rows, META_ROWS), :]


def ring_chip(place, chips):
    place = lax.rem(place + 2 * chips, chips)
    return jnp.where(place < chips // 2, 2 * place, 2 * (chips - 1 - place) + 1)


def pair_rows(steps, chips, me, pair_ref, weights, out_refs):
    queries, total, channels = pair_ref.shape
    heads = weights.shape[0]
    tokens = total // len(steps)
    chip = me // CORES
    core = lax.rem(me, CORES)
    place = jnp.where(lax.rem(chip, 2) == 0, chip // 2, chips - 1 - chip // 2)
    lines = heads * queries
    head = lax.broadcasted_iota(jnp.int32, (heads, lines), 0)
    lane = lax.broadcasted_iota(jnp.int32, (heads, lines), 1)
    spread = (lane // queries == head).astype(F32).astype(BF16)
    wide = lax.dot_general(weights, spread, (((0,), (0,)), ((), ())), preferred_element_type=F32)
    lane = lax.broadcasted_iota(jnp.int32, (channels, lines), 1) % queries
    wide = jnp.concatenate(
        [jnp.where(lane == i, wide, 0.0).astype(BF16) for i in range(queries)], axis=0
    )
    at = 0
    for out_ref in out_refs:
        data = []
        for r, c in steps[at : at + out_ref.shape[0] // tokens]:
            block = ring_chip(place + r, chips) * CORES + lax.rem(core + c, CORES)
            start = pl.multiple_of(block * tokens, tokens)
            rows = [pair_ref[i, pl.ds(start, tokens), :] for i in range(queries)]
            data.append(jnp.concatenate(rows, axis=1))
        at += len(data)
        out_ref[...] = matmul(jnp.concatenate(data, axis=0), wide)


def kv_count(ref, rows):
    return ref.shape[0] // (2 * rows + META_ROWS)


def kv_metas(kv_refs, rows):
    found = []
    for r in kv_refs:
        n = kv_count(r, rows)
        found += [r[pl.ds(2 * n * rows + u * META_ROWS, META_ROWS), :] for u in range(n)]
    return found


def full_bias(own, metas, tokens, pair_ref, tab_ref, pad_ref):
    total = pair_ref.shape[0]
    heads, bins = tab_ref.shape
    reach = (bins - 2) // 2
    wide = -(-total // LANES) * LANES
    slot = lax.broadcasted_iota(jnp.int32, (META_ROWS, wide), 1) // tokens
    keys = jnp.zeros((META_ROWS, wide), F32)
    for u, row in enumerate(metas):
        row = row.astype(F32)
        row = jnp.concatenate([row] * (-(-wide // row.shape[1])), axis=1)[:, :wide]
        keys = jnp.where(slot == u, row, keys)
    here = own.astype(F32)[:, :LANES]
    lane = lax.broadcasted_iota(jnp.int32, (tokens, LANES), 1)
    row = lax.broadcasted_iota(jnp.int32, (tokens, LANES), 0)

    def column(values):
        values = jnp.where(lane == row, jnp.broadcast_to(values, (tokens, LANES)), 0.0)
        return jnp.sum(values, axis=-1, keepdims=True)

    chain_q = column(here[0:1, :])
    res_q = column(here[1:2, :] * RADIX + here[2:3, :])
    res_keys = keys[1:2, :] * RADIX + keys[2:3, :]
    offset = jnp.clip(res_q - res_keys, -reach, reach) + reach
    bucket = jnp.where(chain_q == keys[0:1, :], offset, float(bins - 1)).astype(jnp.int32)
    mask = (keys[3:4, :] - 1.0) * MASK_PENALTY
    pad_ref[...] = jnp.zeros_like(pad_ref)
    pad_ref[:, pl.ds(0, bins)] = tab_ref[...]
    out = []
    for h in range(heads):
        table = jnp.broadcast_to(pad_ref[h : h + 1, :], (tokens, LANES))
        rel = [
            jnp.take_along_axis(
                table, bucket[:, at : at + LANES], axis=1, mode="promise_in_bounds"
            )
            for at in range(0, wide, LANES)
        ]
        out.append((jnp.concatenate(rel, axis=1) if len(rel) > 1 else rel[0]) + mask)
    return pair_ref[...] + jnp.transpose(jnp.concatenate(out, axis=0))[:total]


def head_windows(width, hs):
    windows, h = [], 0
    while h * hs < width:
        start = min(h * hs // LANES * LANES, width - TILE)
        last = min((start + TILE) // hs, width // hs) - 1
        windows.append((h, last, start))
        h = last + 1
    return windows


def spread_queries(samples, heads, q_ref, out_ref):
    rows, width = q_ref.shape
    tokens = rows // samples
    hs = width // heads
    lines = heads * tokens
    token = lax.broadcasted_iota(jnp.int32, (tokens, lines), 0)
    lane = lax.broadcasted_iota(jnp.int32, (tokens, lines), 1)
    spread = (lane % tokens == token).astype(F32).astype(BF16)
    feature = lax.broadcasted_iota(jnp.int32, (width, lines), 0)
    lane = lax.broadcasted_iota(jnp.int32, (width, lines), 1)
    inside = feature // hs == lane // tokens
    for s in range(samples):
        wide = lax.dot_general(
            q_ref[pl.ds(s * tokens, tokens), :], spread, (((0,), (0,)), ((), ())),
            preferred_element_type=F32,
        )
        out_ref[pl.ds(s * width, width), :] = jnp.where(inside, wide, 0.0).astype(BF16)


def gather(kv_refs, rows, at, tokens, values):
    found = []
    for r in kv_refs:
        n = kv_count(r, rows)
        first = n if values else 0
        found += [r[pl.ds((first + u) * rows + at, tokens), :] for u in range(n)]
    return found


def weights_body(samples, scale, more, *refs):
    exp_ref, top_ref, mass_ref, pad_ref = refs[-4:]
    q_ref, pair_ref, tab_ref, own_ref = refs[-8:-4]
    kv_refs = refs[:-8]
    if more:
        kv_refs, before_ref, mass_before_ref = refs[:-10], refs[-10], refs[-9]
    count, lines = pair_ref.shape
    tokens = lines // tab_ref.shape[0]
    rows = tokens * samples
    width = kv_refs[0].shape[1]
    metas = kv_metas(kv_refs, rows)
    bias = full_bias(own_ref[...], metas, tokens, pair_ref, tab_ref, pad_ref)
    for s in range(samples):
        here = pl.ds(s, 1)
        keys = jnp.concatenate(gather(kv_refs, rows, s * tokens, tokens, False), axis=0)
        scores = matmul(keys, q_ref[pl.ds(s * width, width), :]) * scale + bias
        top = jnp.max(scores, axis=0, keepdims=True)
        if more:
            top = jnp.maximum(top, before_ref[here, :])
        weights = jnp.exp(scores - top)
        mass = jnp.sum(weights, axis=0, keepdims=True)
        if more:
            mass = mass + mass_before_ref[here, :] * jnp.exp(before_ref[here, :] - top)
        top_ref[here, :] = top
        mass_ref[here, :] = mass
        exp_ref[pl.ds(s * count, count), :] = weights


def finish_body(heads, scale, split, *refs):
    (
        q_ref, gate_ref, exp_ref, top_ref, mass_ref, wk_ref, wv_ref, pair_ref, tab_ref, own_ref,
        single_ref, wo_ref, out_ref, pad_ref, weight_ref,
    ) = refs[-15:]
    kv_refs, lasts = refs[:-19], refs[-19:-15]
    tokens, samples, width = single_ref.shape
    rows = tokens * samples
    hs = width // heads
    share = lasts[0].shape[0] - META_ROWS
    metas = kv_metas(kv_refs[split:], rows) + [r[pl.ds(share, META_ROWS), :] for r in (lasts[0], lasts[2])]
    sizes = (share, rows - share) * 2
    data = jnp.concatenate([r[pl.ds(0, n), :] for r, n in zip(lasts, sizes)], axis=0)
    k_last = matmul(data, wk_ref[...]).astype(BF16)
    v_last = matmul(data, wv_ref[...]).astype(BF16)
    bias = full_bias(own_ref[...], metas, tokens, pair_ref, tab_ref, pad_ref)
    count = exp_ref.shape[0] // samples
    lane_head = lax.broadcasted_iota(jnp.int32, (tokens, width), 1) // hs
    lines = heads * tokens
    for s in range(samples):
        new = [slice(u * rows + s * tokens, u * rows + (s + 1) * tokens) for u in range(2)]
        keys = gather(kv_refs[split:], rows, s * tokens, tokens, False)
        keys = jnp.concatenate(keys + [k_last[n] for n in new], axis=0)
        scores = matmul(keys, q_ref[pl.ds(s * width, width), :]) * scale + bias
        before = top_ref[pl.ds(s, 1), :]
        top = jnp.maximum(jnp.max(scores, axis=0, keepdims=True), before)
        shrink = jnp.exp(before - top)
        late = jnp.exp(scores - top)
        mass = jnp.sum(late, axis=0, keepdims=True) + mass_ref[pl.ds(s, 1), :] * shrink
        inv = 1.0 / mass
        old = exp_ref[pl.ds(s * count, count), :] * (shrink * inv)
        weights = jnp.concatenate([old, late * inv], axis=0)
        weight_ref[pl.ds(s * lines, lines), :] = jnp.transpose(weights).astype(BF16)
    gated = []
    for s in range(samples):
        new = [slice(u * rows + s * tokens, u * rows + (s + 1) * tokens) for u in range(2)]
        values = gather(kv_refs, rows, s * tokens, tokens, True)
        values = jnp.concatenate(values + [v_last[n] for n in new], axis=0)
        pieces = {}
        for h0, h1, start in head_windows(width, hs):
            here = pl.ds(s * lines + h0 * tokens, (h1 + 1 - h0) * tokens)
            ot = matmul(weight_ref[here, :], values[:, start : start + TILE])
            for first in range(start, start + TILE, LANES):
                for h in range(h0, h1 + 1):
                    if (h + 1) * hs <= first or h * hs >= first + LANES:
                        continue
                    lanes = slice(first - start, first - start + LANES)
                    part = ot[(h - h0) * tokens : (h + 1 - h0) * tokens, lanes]
                    if first in pieces:
                        mine = lane_head[:, first : first + LANES] == h
                        part = jnp.where(mine, part, pieces[first])
                    pieces[first] = part
        attended = jnp.concatenate([pieces[at] for at in sorted(pieces)], axis=1)
        gated.append((gate_ref[pl.ds(s * tokens, tokens), :] * attended).astype(BF16))
    gated = matmul(token_major(tokens, samples), jnp.concatenate(gated, axis=0)).astype(BF16)
    out = matmul(gated, wo_ref[...]).reshape(tokens, samples, width)
    out_ref[...] = (single_ref[...].astype(F32) + out).astype(BF16)


def call(body, out_shape, args, in_specs=None, flops=0, moved=0, limit=8 << 20, scratch=()):
    return pl.pallas_call(
        body,
        out_shape=out_shape,
        in_specs=in_specs or [VMEM] * len(args),
        out_specs=jax.tree.map(lambda _: VMEM, out_shape),
        scratch_shapes=scratch,
        compiler_params=pltpu.CompilerParams(vmem_limit_bytes=limit),
        cost_estimate=pl.CostEstimate(flops=flops, bytes_accessed=moved, transcendentals=0),
    )(*args)


def shards(
    single, pair, chain, residue, valid, w_query, w_key, w_value, w_gate, w_out, w_pair, rel_table
):
    tokens, samples, width = single.shape
    heads = w_pair.shape[1]
    total = pair.shape[1]
    rows = tokens * samples
    devices = lax.axis_size("tok")
    chips = devices // CORES
    half = chips // 2
    order = list(range(0, chips, 2)) + list(range(1, chips, 2))[::-1]
    me = lax.axis_index("tok").astype(jnp.int32).reshape(1)

    def ring(value, step):
        pairs = [
            (order[i] * CORES + c, order[(i + step) % chips] * CORES + c)
            for i in range(chips)
            for c in range(CORES)
        ]
        return lax.ppermute(value, "tok", pairs)

    def flip(value):
        return lax.ppermute(value, "tok", [(d, d ^ 1) for d in range(devices)])

    steps = [(0, 0), (0, 1)]
    for k in range(1, half):
        steps += [(-k, 0), (k, 0), (-k, 1), (k, 1)]
    steps += [(half, 0), (half, 1)]

    cw = ring(single, 1)
    ccw = ring(single, -1)
    blocks = jax.ShapeDtypeStruct((rows + META_ROWS, width), BF16)
    payload, meta, query = call(
        prep_body,
        (
            blocks,
            jax.ShapeDtypeStruct((META_ROWS, width), BF16),
            jax.ShapeDtypeStruct((rows, width), BF16),
        ),
        (single, *(v.reshape(1, tokens) for v in (chain, residue, valid)), w_query),
        in_specs=[ANY] * 5,
        scratch=[
            pltpu.VMEM(single.shape, BF16),
            pltpu.VMEM((3, 1, tokens), jnp.int32),
            pltpu.VMEM((width, width), BF16),
            pltpu.SemaphoreType.DMA((5,)),
        ],
        flops=2 * rows * width * width,
        moved=6 * rows * width + 2 * width * width,
        limit=FULL,
    )
    cw_meta = ring(meta, 1)
    ccw_meta = ring(meta, -1)
    lines = heads * tokens
    query = call(
        functools.partial(spread_body, samples, heads),
        jax.ShapeDtypeStruct((samples * width, lines), BF16),
        (me, query),
        in_specs=[SMEM, VMEM],
        flops=2 * rows * width * lines,
        moved=2 * samples * width * lines,
    )
    gate = call(
        gate_body,
        jax.ShapeDtypeStruct((rows, width), F32),
        (payload, w_gate),
        flops=2 * rows * width * width,
        moved=2 * width * width + 6 * rows * width,
    )

    def join(value, extra):
        return call(join_body, blocks, (value, extra), moved=4 * rows * width)

    cw = join(cw, cw_meta)
    ccw = join(ccw, ccw_meta)

    def kv(parts):
        n = len(parts)
        return call(
            kv_body,
            jax.ShapeDtypeStruct((n * (2 * rows + META_ROWS), width), BF16),
            (*parts, w_key, w_value),
            flops=4 * n * rows * width * width,
            moved=4 * width * width + 6 * n * rows * width,
        )

    def piece(value, at, size, meta):
        count = size + (META_ROWS if meta else 0)

        def body(in_ref, out_ref):
            out_ref[pl.ds(0, size), :] = in_ref[pl.ds(at, size), :]
            if meta:
                out_ref[pl.ds(size, META_ROWS), :] = in_ref[pl.ds(rows, META_ROWS), :]

        shape = jax.ShapeDtypeStruct((count, width), BF16)
        return call(body, shape, (value,), moved=2 * rows * width)

    sizes = [len(steps) - 3 * CORES, 3 * CORES]
    pair_bias = call(
        functools.partial(pair_body, steps, chips),
        tuple(jax.ShapeDtypeStruct((n * tokens, lines), F32) for n in sizes),
        (me, pair, w_pair.T),
        in_specs=[SMEM, VMEM, VMEM],
        flops=2 * pair.size * lines,
        moved=2 * pair.size + 4 * total * lines,
        limit=(6 << 20) + 4 * pair.size,
    )
    share = samples * 3 // 4 * tokens
    kvs = [kv([payload])]
    kvs.append(flip(kvs[-1]))
    for k in range(1, half):
        if k + 1 < half:
            cw_next = ring(cw, 1)
            ccw_next = ring(ccw, -1)
        else:
            cw_next = ring(piece(cw, 0, share, True), 1)
            ccw_next = ring(piece(ccw, share, rows - share, False), -1)
        kvs.append(kv([cw, ccw]))
        kvs.append(flip(kvs[-1]))
        cw, ccw = cw_next, ccw_next
    scale = 1.0 / math.sqrt(width // heads)
    state = jax.ShapeDtypeStruct((samples, lines), F32)
    table = rel_table.T
    pad = [pltpu.VMEM((heads, LANES), F32)]
    limit = (10 << 20) + 4 * samples * total * width

    split = 2 * (half - 1)
    keys = sizes[0] * tokens
    first = call(
        functools.partial(weights_body, samples, scale, False),
        (jax.ShapeDtypeStruct((samples * keys, lines), F32), state, state),
        (*kvs[:split], query, pair_bias[0], table, meta),
        flops=2 * samples * keys * width * lines,
        moved=6 * samples * keys * width,
        limit=limit,
        scratch=pad,
    )
    cw_other, ccw_other = flip(cw), flip(ccw)
    return call(
        functools.partial(finish_body, heads, scale, split),
        jax.ShapeDtypeStruct(single.shape, BF16),
        (
            *kvs, cw, ccw, cw_other, ccw_other, query, gate, *first, w_key, w_value,
            pair_bias[1], table, meta, single, w_out,
        ),
        flops=4 * rows * total * width,
        moved=2 * samples * total * width,
        limit=limit,
        scratch=[*pad, pltpu.VMEM((samples * lines, total), BF16)],
    )


def solution(mesh):
    placed = (
        P(("groups", "tok"), None, None),
        P(("groups", "tok"), None, None),
        P(("groups", "tok")),
        P(("groups", "tok")),
        P(("groups", "tok")),
        P(),
        P(),
        P(),
        P(),
        P(),
        P(),
        P(),
    )

    return jax.shard_map(
        shards,
        mesh=mesh,
        in_specs=placed,
        out_specs=P(("groups", "tok"), None, None),
        check_vma=False,
    )
```

```python
import functools
import math

import jax
import jax.numpy as jnp
from jax import lax
from jax.experimental import pallas as pl
from jax.experimental.pallas import tpu as pltpu
from jax.sharding import PartitionSpec as P


NORM_EPS = 1e-05
MASK_PENALTY = 10000.0
F32 = jnp.float32
BF16 = jnp.bfloat16
CORES = 2
TILE = 256
LANES = 128
META_ROWS = 8
RADIX = 128
FULL = 60 << 20
VMEM = pl.BlockSpec(memory_space=pltpu.VMEM)
ANY = pl.BlockSpec(memory_space=pl.ANY)
SMEM = pl.BlockSpec(memory_space=pltpu.SMEM)


def normed_rows(block):
    tokens, samples, width = block.shape
    values = block.astype(F32).reshape(tokens * samples, width)
    centred = values - jnp.mean(values, axis=-1, keepdims=True)
    spread = jnp.mean(centred * centred, axis=-1, keepdims=True)
    return (centred * lax.rsqrt(spread + NORM_EPS)).astype(BF16)


def sample_major(tokens, samples):
    rows = tokens * samples
    to = lax.broadcasted_iota(jnp.int32, (rows, rows), 0)
    frm = lax.broadcasted_iota(jnp.int32, (rows, rows), 1)
    want = (to % tokens) * samples + to // tokens
    return (want == frm).astype(F32).astype(BF16)


def token_major(tokens, samples):
    rows = tokens * samples
    to = lax.broadcasted_iota(jnp.int32, (rows, rows), 0)
    frm = lax.broadcasted_iota(jnp.int32, (rows, rows), 1)
    want = (to % samples) * tokens + to // samples
    return (want == frm).astype(F32).astype(BF16)


def matmul(a, b):
    return jnp.dot(a, b, preferred_element_type=F32)


def prep_body(
    single_hbm, chain_hbm, residue_hbm, valid_hbm, wq_hbm, out_ref, meta_ref, q_ref,
    single_ref, ints_ref, wq_ref, sems,
):
    copies = [pltpu.make_async_copy(single_hbm, single_ref, sems.at[0])]
    for i, ref in enumerate((chain_hbm, residue_hbm, valid_hbm)):
        copies.append(pltpu.make_async_copy(ref, ints_ref.at[i], sems.at[i + 1]))
    weight = pltpu.make_async_copy(wq_hbm, wq_ref, sems.at[4])
    for copy in (*copies, weight):
        copy.start()
    tokens, samples, width = single_ref.shape
    rows = tokens * samples
    token = lax.broadcasted_iota(jnp.int32, (tokens, width), 0)
    lane = lax.broadcasted_iota(jnp.int32, (tokens, width), 1)
    spread = (lane % tokens == token).astype(F32).astype(BF16)
    perm = sample_major(tokens, samples)
    for copy in copies:
        copy.wait()
    data = matmul(perm, normed_rows(single_ref[...])).astype(BF16)
    out_ref[pl.ds(0, rows), :] = data
    residue = ints_ref[1]
    row = lax.broadcasted_iota(jnp.int32, (META_ROWS, tokens), 0)
    meta = jnp.where(row == 0, ints_ref[0], 0)
    meta = jnp.where(row == 1, residue // RADIX, meta)
    meta = jnp.where(row == 2, residue % RADIX, meta)
    meta = jnp.where(row == 3, ints_ref[2], meta)
    tiled = matmul(meta.astype(F32).astype(BF16), spread)
    out_ref[pl.ds(rows, META_ROWS), :] = tiled.astype(BF16)
    meta_ref[...] = tiled.astype(BF16)
    weight.wait()
    q_ref[...] = matmul(data, wq_ref[...]).astype(BF16)


def join_body(single_ref, meta_ref, out_ref):
    tokens, samples, _ = single_ref.shape
    rows = tokens * samples
    normed = normed_rows(single_ref[...])
    out_ref[pl.ds(0, rows), :] = matmul(sample_major(tokens, samples), normed).astype(BF16)
    out_ref[pl.ds(rows, META_ROWS), :] = meta_ref[...]


def spread_body(samples, heads, me_ref, q_ref, out_ref):
    spread_queries(samples, heads, q_ref, out_ref)


def pair_body(steps, chips, me_ref, pair_ref, wp_ref, *out_refs):
    pair_rows(steps, chips, me_ref[0], pair_ref, wp_ref[...], out_refs)


def gate_body(pay_ref, wg_ref, gate_ref):
    data = pay_ref[pl.ds(0, gate_ref.shape[0]), :]
    gate_ref[...] = jax.nn.sigmoid(matmul(data, wg_ref[...]))


def kv_body(*refs):
    wk_ref, wv_ref, out_ref = refs[-3:]
    blocks = refs[:-3]
    n = len(blocks)
    rows = blocks[0].shape[0] - META_ROWS
    parts = [b[pl.ds(0, rows), :] for b in blocks]
    data = jnp.concatenate(parts, axis=0) if n > 1 else parts[0]
    out_ref[pl.ds(0, n * rows), :] = matmul(data, wk_ref[...]).astype(BF16)
    out_ref[pl.ds(n * rows, n * rows), :] = matmul(data, wv_ref[...]).astype(BF16)
    for i, b in enumerate(blocks):
        out_ref[pl.ds(2 * n * rows + i * META_ROWS, META_ROWS), :] = b[pl.ds(rows, META_ROWS), :]


def ring_chip(place, chips):
    place = lax.rem(place + 2 * chips, chips)
    return jnp.where(place < chips // 2, 2 * place, 2 * (chips - 1 - place) + 1)


def pair_rows(steps, chips, me, pair_ref, weights, out_refs):
    queries, total, channels = pair_ref.shape
    heads = weights.shape[0]
    tokens = total // len(steps)
    chip = me // CORES
    core = lax.rem(me, CORES)
    place = jnp.where(lax.rem(chip, 2) == 0, chip // 2, chips - 1 - chip // 2)
    lines = heads * queries
    head = lax.broadcasted_iota(jnp.int32, (heads, lines), 0)
    lane = lax.broadcasted_iota(jnp.int32, (heads, lines), 1)
    spread = (lane // queries == head).astype(F32).astype(BF16)
    wide = lax.dot_general(weights, spread, (((0,), (0,)), ((), ())), preferred_element_type=F32)
    lane = lax.broadcasted_iota(jnp.int32, (channels, lines), 1) % queries
    wide = jnp.concatenate(
        [jnp.where(lane == i, wide, 0.0).astype(BF16) for i in range(queries)], axis=0
    )
    at = 0
    for out_ref in out_refs:
        data = []
        for r, c in steps[at : at + out_ref.shape[0] // tokens]:
            block = ring_chip(place + r, chips) * CORES + lax.rem(core + c, CORES)
            start = pl.multiple_of(block * tokens, tokens)
            rows = [pair_ref[i, pl.ds(start, tokens), :] for i in range(queries)]
            data.append(jnp.concatenate(rows, axis=1))
        at += len(data)
        out_ref[...] = matmul(jnp.concatenate(data, axis=0), wide)


def kv_count(ref, rows):
    return ref.shape[0] // (2 * rows + META_ROWS)


def kv_metas(kv_refs, rows):
    found = []
    for r in kv_refs:
        n = kv_count(r, rows)
        found += [r[pl.ds(2 * n * rows + u * META_ROWS, META_ROWS), :] for u in range(n)]
    return found


def full_bias(own, metas, tokens, pair_ref, tab_ref, pad_ref):
    total = pair_ref.shape[0]
    heads, bins = tab_ref.shape
    reach = (bins - 2) // 2
    wide = -(-total // LANES) * LANES
    slot = lax.broadcasted_iota(jnp.int32, (META_ROWS, wide), 1) // tokens
    keys = jnp.zeros((META_ROWS, wide), F32)
    for u, row in enumerate(metas):
        row = row.astype(F32)
        row = jnp.concatenate([row] * (-(-wide // row.shape[1])), axis=1)[:, :wide]
        keys = jnp.where(slot == u, row, keys)
    here = own.astype(F32)[:, :LANES]
    lane = lax.broadcasted_iota(jnp.int32, (tokens, LANES), 1)
    row = lax.broadcasted_iota(jnp.int32, (tokens, LANES), 0)

    def column(values):
        values = jnp.where(lane == row, jnp.broadcast_to(values, (tokens, LANES)), 0.0)
        return jnp.sum(values, axis=-1, keepdims=True)

    chain_q = column(here[0:1, :])
    res_q = column(here[1:2, :] * RADIX + here[2:3, :])
    res_keys = keys[1:2, :] * RADIX + keys[2:3, :]
    offset = jnp.clip(res_q - res_keys, -reach, reach) + reach
    bucket = jnp.where(chain_q == keys[0:1, :], offset, float(bins - 1)).astype(jnp.int32)
    mask = (keys[3:4, :] - 1.0) * MASK_PENALTY
    pad_ref[...] = jnp.zeros_like(pad_ref)
    pad_ref[:, pl.ds(0, bins)] = tab_ref[...]
    out = []
    for h in range(heads):
        table = jnp.broadcast_to(pad_ref[h : h + 1, :], (tokens, LANES))
        rel = [
            jnp.take_along_axis(
                table, bucket[:, at : at + LANES], axis=1, mode="promise_in_bounds"
            )
            for at in range(0, wide, LANES)
        ]
        out.append((jnp.concatenate(rel, axis=1) if len(rel) > 1 else rel[0]) + mask)
    return pair_ref[...] + jnp.transpose(jnp.concatenate(out, axis=0))[:total]


def head_windows(width, hs):
    windows, h = [], 0
    while h * hs < width:
        start = min(h * hs // LANES * LANES, width - TILE)
        last = min((start + TILE) // hs, width // hs) - 1
        windows.append((h, last, start))
        h = last + 1
    return windows


def spread_queries(samples, heads, q_ref, out_ref):
    rows, width = q_ref.shape
    tokens = rows // samples
    hs = width // heads
    lines = heads * tokens
    token = lax.broadcasted_iota(jnp.int32, (tokens, lines), 0)
    lane = lax.broadcasted_iota(jnp.int32, (tokens, lines), 1)
    spread = (lane % tokens == token).astype(F32).astype(BF16)
    feature = lax.broadcasted_iota(jnp.int32, (width, lines), 0)
    lane = lax.broadcasted_iota(jnp.int32, (width, lines), 1)
    inside = feature // hs == lane // tokens
    for s in range(samples):
        wide = lax.dot_general(
            q_ref[pl.ds(s * tokens, tokens), :], spread, (((0,), (0,)), ((), ())),
            preferred_element_type=F32,
        )
        out_ref[pl.ds(s * width, width), :] = jnp.where(inside, wide, 0.0).astype(BF16)


def gather(kv_refs, rows, at, tokens, values):
    found = []
    for r in kv_refs:
        n = kv_count(r, rows)
        first = n if values else 0
        found += [r[pl.ds((first + u) * rows + at, tokens), :] for u in range(n)]
    return found


def weights_body(samples, scale, more, *refs):
    exp_ref, top_ref, mass_ref, pad_ref = refs[-4:]
    q_ref, pair_ref, tab_ref, own_ref = refs[-8:-4]
    kv_refs = refs[:-8]
    if more:
        kv_refs, before_ref, mass_before_ref = refs[:-10], refs[-10], refs[-9]
    count, lines = pair_ref.shape
    tokens = lines // tab_ref.shape[0]
    rows = tokens * samples
    width = kv_refs[0].shape[1]
    metas = kv_metas(kv_refs, rows)
    bias = full_bias(own_ref[...], metas, tokens, pair_ref, tab_ref, pad_ref)
    for s in range(samples):
        here = pl.ds(s, 1)
        keys = jnp.concatenate(gather(kv_refs, rows, s * tokens, tokens, False), axis=0)
        scores = matmul(keys, q_ref[pl.ds(s * width, width), :]) * scale + bias
        top = jnp.max(scores, axis=0, keepdims=True)
        if more:
            top = jnp.maximum(top, before_ref[here, :])
        weights = jnp.exp(scores - top)
        mass = jnp.sum(weights, axis=0, keepdims=True)
        if more:
            mass = mass + mass_before_ref[here, :] * jnp.exp(before_ref[here, :] - top)
        top_ref[here, :] = top
        mass_ref[here, :] = mass
        exp_ref[pl.ds(s * count, count), :] = weights


def last_body(first_ref, second_ref, wk_ref, wv_ref, out_ref):
    rows = out_ref.shape[0] // 2
    share = rows - second_ref.shape[0]
    data = jnp.concatenate([first_ref[pl.ds(0, share), :], second_ref[...]], axis=0)
    out_ref[pl.ds(0, rows), :] = matmul(data, wk_ref[...]).astype(BF16)
    out_ref[pl.ds(rows, rows), :] = matmul(data, wv_ref[...]).astype(BF16)


def finish_body(heads, scale, split, *refs):
    (
        q_ref, gate_ref, exp_ref, top_ref, mass_ref, wk_ref, wv_ref, pair_ref, tab_ref, own_ref,
        single_ref, wo_ref, out_ref, pad_ref, weight_ref,
    ) = refs[-15:]
    kv_refs, lasts, mine_ref = refs[:-19], refs[-19:-16], refs[-16]
    tokens, samples, width = single_ref.shape
    rows = tokens * samples
    hs = width // heads
    share = lasts[0].shape[0] - META_ROWS
    metas = kv_metas(kv_refs[split:], rows) + [r[pl.ds(share, META_ROWS), :] for r in lasts[:2]]
    data = jnp.concatenate([lasts[1][pl.ds(0, share), :], lasts[2][...]], axis=0)
    k_last = matmul(data, wk_ref[...]).astype(BF16)
    v_last = matmul(data, wv_ref[...]).astype(BF16)
    bias = full_bias(own_ref[...], metas, tokens, pair_ref, tab_ref, pad_ref)
    count = exp_ref.shape[0] // samples
    lane_head = lax.broadcasted_iota(jnp.int32, (tokens, width), 1) // hs
    lines = heads * tokens
    for s in range(samples):
        new = slice(s * tokens, (s + 1) * tokens)
        keys = gather(kv_refs[split:], rows, s * tokens, tokens, False)
        keys = jnp.concatenate(keys + [mine_ref[pl.ds(s * tokens, tokens), :], k_last[new]], axis=0)
        scores = matmul(keys, q_ref[pl.ds(s * width, width), :]) * scale + bias
        before = top_ref[pl.ds(s, 1), :]
        top = jnp.maximum(jnp.max(scores, axis=0, keepdims=True), before)
        shrink = jnp.exp(before - top)
        late = jnp.exp(scores - top)
        mass = jnp.sum(late, axis=0, keepdims=True) + mass_ref[pl.ds(s, 1), :] * shrink
        inv = 1.0 / mass
        old = exp_ref[pl.ds(s * count, count), :] * (shrink * inv)
        weights = jnp.concatenate([old, late * inv], axis=0)
        weight_ref[pl.ds(s * lines, lines), :] = jnp.transpose(weights).astype(BF16)
    gated = []
    for s in range(samples):
        new = slice(s * tokens, (s + 1) * tokens)
        values = gather(kv_refs, rows, s * tokens, tokens, True)
        values = jnp.concatenate(values + [mine_ref[pl.ds(rows + s * tokens, tokens), :], v_last[new]], axis=0)
        pieces = {}
        for h0, h1, start in head_windows(width, hs):
            here = pl.ds(s * lines + h0 * tokens, (h1 + 1 - h0) * tokens)
            ot = matmul(weight_ref[here, :], values[:, start : start + TILE])
            for first in range(start, start + TILE, LANES):
                for h in range(h0, h1 + 1):
                    if (h + 1) * hs <= first or h * hs >= first + LANES:
                        continue
                    lanes = slice(first - start, first - start + LANES)
                    part = ot[(h - h0) * tokens : (h + 1 - h0) * tokens, lanes]
                    if first in pieces:
                        mine = lane_head[:, first : first + LANES] == h
                        part = jnp.where(mine, part, pieces[first])
                    pieces[first] = part
        attended = jnp.concatenate([pieces[at] for at in sorted(pieces)], axis=1)
        gated.append((gate_ref[pl.ds(s * tokens, tokens), :] * attended).astype(BF16))
    gated = matmul(token_major(tokens, samples), jnp.concatenate(gated, axis=0)).astype(BF16)
    out = matmul(gated, wo_ref[...]).reshape(tokens, samples, width)
    out_ref[...] = (single_ref[...].astype(F32) + out).astype(BF16)


def call(body, out_shape, args, in_specs=None, flops=0, moved=0, limit=8 << 20, scratch=()):
    return pl.pallas_call(
        body,
        out_shape=out_shape,
        in_specs=in_specs or [VMEM] * len(args),
        out_specs=jax.tree.map(lambda _: VMEM, out_shape),
        scratch_shapes=scratch,
        compiler_params=pltpu.CompilerParams(vmem_limit_bytes=limit),
        cost_estimate=pl.CostEstimate(flops=flops, bytes_accessed=moved, transcendentals=0),
    )(*args)


def shards(
    single, pair, chain, residue, valid, w_query, w_key, w_value, w_gate, w_out, w_pair, rel_table
):
    tokens, samples, width = single.shape
    heads = w_pair.shape[1]
    total = pair.shape[1]
    rows = tokens * samples
    devices = lax.axis_size("tok")
    chips = devices // CORES
    half = chips // 2
    order = list(range(0, chips, 2)) + list(range(1, chips, 2))[::-1]
    me = lax.axis_index("tok").astype(jnp.int32).reshape(1)

    def ring(value, step):
        pairs = [
            (order[i] * CORES + c, order[(i + step) % chips] * CORES + c)
            for i in range(chips)
            for c in range(CORES)
        ]
        return lax.ppermute(value, "tok", pairs)

    def flip(value):
        return lax.ppermute(value, "tok", [(d, d ^ 1) for d in range(devices)])

    steps = [(0, 0), (0, 1)]
    for k in range(1, half):
        steps += [(-k, 0), (k, 0), (-k, 1), (k, 1)]
    steps += [(half, 0), (half, 1)]

    cw = ring(single, 1)
    ccw = ring(single, -1)
    blocks = jax.ShapeDtypeStruct((rows + META_ROWS, width), BF16)
    payload, meta, query = call(
        prep_body,
        (
            blocks,
            jax.ShapeDtypeStruct((META_ROWS, width), BF16),
            jax.ShapeDtypeStruct((rows, width), BF16),
        ),
        (single, *(v.reshape(1, tokens) for v in (chain, residue, valid)), w_query),
        in_specs=[ANY] * 5,
        scratch=[
            pltpu.VMEM(single.shape, BF16),
            pltpu.VMEM((3, 1, tokens), jnp.int32),
            pltpu.VMEM((width, width), BF16),
            pltpu.SemaphoreType.DMA((5,)),
        ],
        flops=2 * rows * width * width,
        moved=6 * rows * width + 2 * width * width,
        limit=FULL,
    )
    cw_meta = ring(meta, 1)
    ccw_meta = ring(meta, -1)
    lines = heads * tokens
    query = call(
        functools.partial(spread_body, samples, heads),
        jax.ShapeDtypeStruct((samples * width, lines), BF16),
        (me, query),
        in_specs=[SMEM, VMEM],
        flops=2 * rows * width * lines,
        moved=2 * samples * width * lines,
    )
    gate = call(
        gate_body,
        jax.ShapeDtypeStruct((rows, width), F32),
        (payload, w_gate),
        flops=2 * rows * width * width,
        moved=2 * width * width + 6 * rows * width,
    )

    def join(value, extra):
        return call(join_body, blocks, (value, extra), moved=4 * rows * width)

    cw = join(cw, cw_meta)
    ccw = join(ccw, ccw_meta)

    def kv(parts):
        n = len(parts)
        return call(
            kv_body,
            jax.ShapeDtypeStruct((n * (2 * rows + META_ROWS), width), BF16),
            (*parts, w_key, w_value),
            flops=4 * n * rows * width * width,
            moved=4 * width * width + 6 * n * rows * width,
        )

    def piece(value, at, size, meta):
        count = size + (META_ROWS if meta else 0)

        def body(in_ref, out_ref):
            out_ref[pl.ds(0, size), :] = in_ref[pl.ds(at, size), :]
            if meta:
                out_ref[pl.ds(size, META_ROWS), :] = in_ref[pl.ds(rows, META_ROWS), :]

        shape = jax.ShapeDtypeStruct((count, width), BF16)
        return call(body, shape, (value,), moved=2 * rows * width)

    sizes = [len(steps) - 3 * CORES, 3 * CORES]
    pair_bias = call(
        functools.partial(pair_body, steps, chips),
        tuple(jax.ShapeDtypeStruct((n * tokens, lines), F32) for n in sizes),
        (me, pair, w_pair.T),
        in_specs=[SMEM, VMEM, VMEM],
        flops=2 * pair.size * lines,
        moved=2 * pair.size + 4 * total * lines,
        limit=(6 << 20) + 4 * pair.size,
    )
    share = samples * 3 // 4 * tokens
    kvs = [kv([payload])]
    kvs.append(flip(kvs[-1]))
    for k in range(1, half):
        if k + 1 < half:
            cw_next = ring(cw, 1)
            ccw_next = ring(ccw, -1)
        else:
            cw_next = ring(piece(cw, 0, share, True), 1)
            ccw_next = ring(piece(ccw, share, rows - share, False), -1)
        kvs.append(kv([cw, ccw]))
        kvs.append(flip(kvs[-1]))
        cw, ccw = cw_next, ccw_next
    scale = 1.0 / math.sqrt(width // heads)
    state = jax.ShapeDtypeStruct((samples, lines), F32)
    table = rel_table.T
    pad = [pltpu.VMEM((heads, LANES), F32)]
    limit = (10 << 20) + 4 * samples * total * width

    split = 2 * (half - 1)
    keys = sizes[0] * tokens
    first = call(
        functools.partial(weights_body, samples, scale, False),
        (jax.ShapeDtypeStruct((samples * keys, lines), F32), state, state),
        (*kvs[:split], query, pair_bias[0], table, meta),
        flops=2 * samples * keys * width * lines,
        moved=6 * samples * keys * width,
        limit=limit,
        scratch=pad,
    )
    cw_other, ccw_other = flip(cw), flip(ccw)
    mine = call(
        last_body,
        jax.ShapeDtypeStruct((2 * rows, width), BF16),
        (cw, ccw, w_key, w_value),
        flops=4 * rows * width * width,
        moved=4 * width * width + 6 * rows * width,
    )
    return call(
        functools.partial(finish_body, heads, scale, split),
        jax.ShapeDtypeStruct(single.shape, BF16),
        (
            *kvs, cw, cw_other, ccw_other, mine, query, gate, *first, w_key, w_value,
            pair_bias[1], table, meta, single, w_out,
        ),
        flops=4 * rows * total * width,
        moved=2 * samples * total * width,
        limit=limit,
        scratch=[*pad, pltpu.VMEM((samples * lines, total), BF16)],
    )


def solution(mesh):
    placed = (
        P(("groups", "tok"), None, None),
        P(("groups", "tok"), None, None),
        P(("groups", "tok")),
        P(("groups", "tok")),
        P(("groups", "tok")),
        P(),
        P(),
        P(),
        P(),
        P(),
        P(),
        P(),
    )

    return jax.shard_map(
        shards,
        mesh=mesh,
        in_specs=placed,
        out_specs=P(("groups", "tok"), None, None),
        check_vma=False,
    )
```
